32 devices in a mesh: cuts: 4 (over z), tile: 8 (over y, x, core).
Axes of the slice: x: 2, y: 2, z: 4, core: 2. Of those that a mesh axis runs over, the one named last changes fastest.
Arguments:
- start_states: float32 [4, 3, 128, 2048], P('cuts', None, 'tile'), may hold values from -6 to 6
Outputs:
- next_states: float32 [4, 3, 128, 2048], P('cuts', None, 'tile')
The draws below stay inside these ranges and needn't reach their ends.
All inputs are finite; a program needn't handle non-finite values.
Results may differ from the reference program's by a relative error of at most 0.0001.
Values sent between devices are 32-bit elements; how exact they have to be, the bound alone decides.
A program may use at most 128 MiB of HBM per device.

```python
import jax
import jax.numpy as jnp
from jax import lax

NX = 2048
STEPS = 3
SLICES = 4
NY = 128
N_CUTS = 4


def level_of(stream_key, extent, shards, smallest, largest):
    gain = 1.0
    for axis_at, shards_of in shards:
        steps = jax.random.uniform(jax.random.fold_in(jax.random.fold_in(stream_key, 6), axis_at), (shards_of,), jnp.float32, smallest / len(shards), largest / len(shards))
        gain = gain * jnp.repeat(jnp.exp(steps), extent[axis_at] // shards_of).reshape((-1,) + (1,) * (len(extent) - 1 - axis_at))
    return gain


def centred(stream_key, extent, spread, limit, shards=(), dtype=jnp.bfloat16):
    result = jax.random.normal(stream_key, extent, jnp.float32) * spread
    if len(shards) > 0:
        result = level_of(stream_key, extent, shards, -0.22, 0.18) * result
    return jnp.clip(result, min=-limit, max=limit).astype(dtype)


def setup_inputs(seed: int = 0) -> dict:
    key_of = jax.random.split(jax.random.key(seed), 2)
    start_states = centred(key_of[0], (SLICES, 3, NY, NX), 1.0, 6.0, ((0, 4), (2, 8)), jnp.float32)
    return dict(start_states=start_states)


FINE_SPACING = 0.05
COARSE_SPACING = 0.1
FINE_STEP = 0.015
COARSE_STEP = 0.045

def depth_profile(columns, stride, length):
    centers = (jnp.arange(columns).astype(jnp.float32) + 0.5) * stride
    return 0.9 + 0.3 * jnp.sin(6.0 * jnp.pi * centers / length)

def along_x(values, spacing):
    padded = jnp.pad(values, [(0, 0)] * (values.ndim - 1) + [(1, 1)])
    return (padded[..., 2:] - padded[..., :-2]) / (2.0 * spacing)

def along_y(values, spacing):
    padded = jnp.pad(values, [(0, 0)] * (values.ndim - 2) + [(1, 1), (0, 0)])
    return (padded[..., 2:, :] - padded[..., :-2, :]) / (2.0 * spacing)

def second_y(values):
    padded = jnp.pad(values, [(0, 0)] * (values.ndim - 2) + [(1, 1), (0, 0)])
    return padded[..., 2:, :] - 2.0 * values + padded[..., :-2, :]

def solve_lines(forcing, seabed, spacing):
    columns = forcing.shape[-1]
    coupling = seabed * seabed / (3.0 * spacing * spacing)
    below_diag = (-coupling).at[0].set(0.0)
    above_diag = (-coupling).at[columns - 1].set(0.0)
    middle = 1.0 + 2.0 * coupling
    stacked_lines = forcing.reshape(-1, columns).T
    solved = lax.linalg.tridiagonal_solve(below_diag, middle, above_diag, stacked_lines)
    return solved.T.reshape(forcing.shape)

def wave_step(fields, seabed, spacing, time_step, inside):
    height = fields[..., 0, :, :]
    flux_x = fields[..., 1, :, :]
    flux_y = fields[..., 2, :, :]
    height_new = (height - time_step * (along_x(flux_x, spacing) + along_y(flux_y, spacing))) * inside
    forcing = jnp.stack([flux_x - time_step * seabed * along_x(height_new, spacing), flux_y - time_step * seabed * along_y(height_new, spacing)], axis=-3)
    trial_flux = solve_lines(forcing, seabed, spacing) * inside
    dispersion = seabed * seabed / 3.0
    weight = dispersion / (spacing * spacing + 4.0 * dispersion)
    fluxes = fields[..., 1:, :, :]
    fluxes_new = (trial_flux + weight * second_y(trial_flux - fluxes)) * inside
    return jnp.concatenate([height_new[..., None, :, :], fluxes_new], axis=-3)

def restrict(fields):
    shape_list = list(fields.shape)
    row_count = shape_list[-2]
    columns = shape_list[-1]
    blocks = fields.reshape(shape_list[:-2] + [row_count // 2, 2, columns // 2, 2])
    return 0.25 * jnp.sum(blocks, axis=(-3, -1))

def prolong(coarse):
    return jnp.repeat(jnp.repeat(coarse, 2, axis=-2), 2, axis=-1)

def reference(start_states):
    columns = start_states.shape[-1]
    fine_depth = depth_profile(columns, 1.0, columns)
    coarse_depth = depth_profile(columns // 2, 2.0, columns)
    fields = start_states
    for substep in range(STEPS):
        fields = wave_step(fields, fine_depth, FINE_SPACING, FINE_STEP, 1.0)
    fine_end = fields
    restricted_start = restrict(start_states)
    restricted_end = restrict(fine_end)
    previous = wave_step(restricted_start, coarse_depth, COARSE_SPACING, COARSE_STEP, 1.0)
    current = restricted_start[0]
    outputs = []
    for slice_index in range(N_CUTS):
        coarse_new = wave_step(current, coarse_depth, COARSE_SPACING, COARSE_STEP, 1.0) - previous[slice_index]
        outputs.append(prolong(coarse_new) + fine_end[slice_index])
        current = coarse_new + restricted_end[slice_index]
    return jnp.stack(outputs)
```

```python
import functools

import ml_dtypes
import numpy as np
import jax
import jax.numpy as jnp
from jax import lax
from jax.experimental import pallas as pl
from jax.experimental.pallas import tpu as pltpu
from jax.sharding import PartitionSpec as P

STEPS = 3
FINE_SPACING = 0.05
COARSE_SPACING = 0.1
FINE_STEP = 0.015
COARSE_STEP = 0.045
LANES = 128
SUB = 8
HALO = (2, 2, 3)
OWN = 2 * SUB
MESH = pl.DeviceIdType.MESH


def line_tables(tiles, fine_tiles, stride, length, spacing, step):
    groups = LANES // fine_tiles
    lane = np.arange(LANES)
    chunk = (lane % fine_tiles) * groups + lane // fine_tiles
    columns = tiles * LANES
    centers = (np.arange(columns) + 0.5) * stride
    depth = (0.9 + 0.3 * np.sin(6.0 * np.pi * centers / length)).reshape(LANES, tiles).T
    beta = depth * depth / 3.0
    b = beta / spacing**2
    mid = 1.0 + 2.0 * b
    last = tiles - 1
    inv = np.zeros_like(b)
    cp = np.zeros_like(b)
    for j in range(last):
        inv[j] = 1.0 / (mid[j] - (b[j] * cp[j - 1] if j else 0.0))
        cp[j] = b[j] * inv[j]
    run = np.ones_like(b)
    for j in range(1, tiles):
        run[j] = run[j - 1] * cp[j - 1]
    p = np.zeros_like(b)
    q = np.zeros_like(b)
    q[last] = 1.0
    for j in range(last - 1, -1, -1):
        p[j] = run[j + 1] + cp[j] * p[j + 1]
        q[j] = cp[j] * q[j + 1]
    system = np.zeros((LANES, LANES))
    for k in range(LANES):
        system[k, k] = mid[last, k] - b[last, k] * q[last - 1, k]
        if k:
            system[k, k - 1] = -b[last, k] * p[last - 1, k]
        if k + 1 < LANES:
            system[k, k] -= b[last, k] * p[0, k + 1]
            system[k, k + 1] = -b[last, k] * q[0, k + 1]
    solve = np.linalg.inv(system).T[chunk][:, chunk]
    high = solve.astype(ml_dtypes.bfloat16)
    low = (solve - high.astype(np.float64)).astype(ml_dtypes.bfloat16)
    half = np.concatenate([high, low], axis=1)
    weights = np.concatenate([half, half], axis=0)
    slope = step * depth / (2.0 * spacing)
    weight = beta / (spacing**2 + 4.0 * beta)
    inv[last] = b[last]
    rows = np.stack([inv, cp, run, slope, weight])[:, :, chunk]
    return rows.astype(np.float32), weights


def relaid(tiles):
    tiles = list(tiles)
    lane = lax.broadcasted_iota(jnp.int32, tiles[0].shape, 1)
    bit = 1
    while bit < len(tiles):
        keep = (lane & bit) == 0
        for t in range(len(tiles)):
            if t & bit == 0:
                a, b = tiles[t], tiles[t | bit]
                tiles[t] = jnp.where(keep, a, pltpu.roll(b, bit, 1))
                tiles[t | bit] = jnp.where(keep, pltpu.roll(a, LANES - bit, 1), b)
        bit *= 2
    return tiles


def wave(state, held, change, rows, weights, inside, tiles, fine_tiles, wide, core):
    factor_in, slope_in, weight_in = inside
    h0, hn = wide
    t0, tn = core
    at = pl.ds(t0, tn)

    def lane(x):
        return lax.broadcasted_iota(jnp.int32, x.shape, 1)

    def chunk_before(x):
        wrapped = jnp.where(lane(x) == 0, 0.0, pltpu.roll(x, fine_tiles + 1, 1))
        return jnp.where(lane(x) >= fine_tiles, pltpu.roll(x, fine_tiles, 1), wrapped)

    def chunk_after(x):
        wrapped = jnp.where(lane(x) == LANES - 1, 0.0, pltpu.roll(x, LANES - fine_tiles - 1, 1))
        return jnp.where(
            lane(x) < LANES - fine_tiles, pltpu.roll(x, LANES - fine_tiles, 1), wrapped
        )

    def across(load, j):
        right = load(j + 1) if j + 1 < tiles else chunk_after(load(0))
        left = load(j - 1) if j else chunk_before(load(tiles - 1))
        return right - left

    def table(kind, j):
        return rows[kind, pl.ds(j, 1), :]

    last = tiles - 1
    near = pl.ds(h0, hn)
    factor = factor_in[near, :]
    for j in range(tiles):
        along = across(lambda i: state[1, i, near, :], j)
        down = state[2, j, pl.ds(h0 + 1, hn), :] - state[2, j, pl.ds(h0 - 1, hn), :]
        state[0, j, near, :] = state[0, j, near, :] - factor * (along + down)
    total = None
    inner = None
    for j in range(tiles):
        along = across(lambda i: state[0, i, at, :], j)
        down = state[0, j, pl.ds(t0 + 1, tn), :] - state[0, j, pl.ds(t0 - 1, tn), :]
        force_x = state[1, j, at, :] - table(3, j) * along
        force_y = state[2, j, at, :] - slope_in[j, at, :] * down
        force = jnp.concatenate([force_x, force_y], axis=0)
        if j == last:
            edge = force + table(0, j) * inner
        elif j == 0:
            inner = force * table(0, j)
            total = inner
            held[j, pl.ds(0, 2 * tn), :] = inner
        else:
            inner = force * table(0, j) + table(1, j) * inner
            total = total + table(2, j) * inner
            held[j, pl.ds(0, 2 * tn), :] = inner
    met = edge + table(0, last) * chunk_after(total)
    high = met.astype(jnp.bfloat16)
    low = (met - high.astype(jnp.float32)).astype(jnp.bfloat16)
    met = jnp.dot(
        jnp.concatenate([high, low], axis=1),
        weights[...],
        preferred_element_type=jnp.float32,
    )
    value = met[:, :LANES] + met[:, LANES:]
    before = chunk_before(value)
    for j in range(last, -1, -1):
        if j < last:
            value = (
                held[j, pl.ds(0, 2 * tn), :] + table(2, j + 1) * before + table(1, j) * value
            )
        for part in range(2):
            trial = value[part * tn : (part + 1) * tn]
            moved = trial - state[1 + part, j, at, :]
            change[j, part, at, :] = moved
            around = change[j, part, pl.ds(t0 + 1, tn), :] + change[j, part, pl.ds(t0 - 1, tn), :]
            state[1 + part, j, at, :] = trial + weight_in[j, at, :] * (around - 2.0 * moved)


def kernel(
    tile_count, slices, x_hbm, fine_rows_hbm, fine_weights_hbm, coarse_rows_hbm,
    coarse_weights_hbm, out_ref,
    x_ref, fine_rows, fine_weights, coarse_rows, coarse_weights,
    down_edge, up_edge, from_up, from_down, state, held, change,
    c_state, c_held, c_change, factor_in, slope_in, weight_in, c_factor_in, c_slope_in,
    c_weight_in, spread,
    start, end, arrived, leaving, low, above_in, below_in,
    local, send, recv, ready,
):
    cut = lax.axis_index("cuts")
    tile = lax.axis_index("tile")
    has_up = tile > 0
    has_down = tile < tile_count - 1
    has_before = cut > 0
    has_after = cut < slices - 1
    planes, row_count, columns = x_ref.shape
    tiles = columns // LANES
    half = tiles // 2
    total_rows = row_count * tile_count
    coarse_count = row_count // 2
    last = planes - 1
    tail = OWN + row_count
    lead = SUB + SUB // 2

    pairs = [
        (x_hbm, x_ref), (fine_rows_hbm, fine_rows), (fine_weights_hbm, fine_weights),
        (coarse_rows_hbm, coarse_rows), (coarse_weights_hbm, coarse_weights),
    ]
    loads = [pltpu.make_async_copy(a, b, local.at[i]) for i, (a, b) in enumerate(pairs)]
    for load in loads:
        load.start()

    barrier = pltpu.get_barrier_semaphore()
    beside = [(has_up, cut, tile - 1), (has_down, cut, tile + 1)]

    def in_cut(there, other):
        return [
            (there, other, tile),
            (there & has_up, other, tile - 1),
            (there & has_down, other, tile + 1),
        ]

    before = in_cut(has_before, cut - 1)
    after = in_cut(has_after, cut + 1)

    def signal(semaphore, devices):
        for exists, to_cut, to_tile in devices:
            @pl.when(exists)
            def _():
                pl.semaphore_signal(
                    semaphore, inc=1, device_id=(to_cut, to_tile), device_id_type=MESH
                )

    def count(devices):
        return sum(exists.astype(jnp.int32) for exists, _, _ in devices)

    signal(barrier, beside + after)

    def remote(source, target, which, to_cut, to_tile):
        return pltpu.make_async_remote_copy(
            src_ref=source, dst_ref=target, send_sem=send.at[which], recv_sem=recv.at[which],
            device_id=(to_cut, to_tile), device_id_type=MESH,
        )

    def rows_at(row):
        return state.at[:, :, pl.ds(row, SUB), :]

    main_down = remote(rows_at(tail - SUB), rows_at(SUB), 0, cut, tile + 1)
    edge_down = remote(down_edge, from_up, 1, cut, tile + 1)
    main_up = remote(rows_at(OWN), rows_at(tail), 2, cut, tile - 1)
    edge_up = remote(up_edge, from_down, 3, cut, tile - 1)

    zero = jnp.zeros((SUB, LANES), jnp.float32)
    for j in range(tiles):
        for plane in range(planes):
            state[plane, j, pl.ds(0, SUB), :] = zero
            state[plane, j, pl.ds(tail + SUB, SUB), :] = zero
        for part in range(2):
            change[j, part, pl.ds(0, SUB), :] = zero
            change[j, part, pl.ds(tail + SUB, SUB), :] = zero
    for j in range(half):
        for row in range(0, 4 * SUB, SUB):
            for plane in range(planes):
                c_state[plane, j, pl.ds(row, SUB), :] = zero
            for part in range(2):
                c_change[j, part, pl.ds(row, SUB), :] = zero

    @pl.when(jnp.logical_not(has_up))
    def _():
        for plane in range(planes):
            for j in range(tiles):
                state[plane, j, pl.ds(SUB, SUB), :] = zero

    @pl.when(jnp.logical_not(has_down))
    def _():
        for plane in range(planes):
            for j in range(tiles):
                state[plane, j, pl.ds(tail, SUB), :] = zero

    loads[0].wait()
    for row in range(0, row_count, SUB):
        for plane in range(planes):
            values = x_ref[plane, pl.ds(row, SUB), :]
            parts = relaid([values[:, t * LANES : (t + 1) * LANES] for t in range(tiles)])
            for j in range(tiles):
                state[plane, j, pl.ds(OWN + row, SUB), :] = parts[j]
                if plane == last and row == 0:
                    down_edge[pl.ds(j, 1), :] = parts[j][SUB - 1 :]
                if plane == last and row == row_count - SUB:
                    up_edge[pl.ds(j, 1), :] = parts[j][:1]

    pl.semaphore_wait(barrier, count(beside + before))

    @pl.when(has_down)
    def _():
        main_down.start()
        edge_down.start()

    @pl.when(has_up)
    def _():
        main_up.start()
        edge_up.start()

    signal(ready, before)

    def mask(total, origin, shape):
        at = lax.broadcasted_iota(jnp.int32, shape, 0) + origin
        return ((at >= 0) & (at < total)).astype(jnp.float32)

    for load in loads[1:]:
        load.wait()
    inside = mask(total_rows, tile * row_count - SUB, (row_count + 2 * SUB, LANES))
    window = pl.ds(SUB, row_count + 2 * SUB)
    factor_in[window, :] = inside * (FINE_STEP / (2.0 * FINE_SPACING))
    for j in range(tiles):
        slope_in[j, window, :] = inside * fine_rows[3, pl.ds(j, 1), :]
        weight_in[j, window, :] = inside * fine_rows[4, pl.ds(j, 1), :]
    c_window = pl.ds(SUB, 2 * SUB)

    def restricted(plane, j, row, count):
        parts = [
            state[plane, 2 * j + k, pl.ds(row + r, count, stride=2), :]
            for r in range(2)
            for k in range(2)
        ]
        return 0.25 * ((parts[0] + parts[1]) + (parts[2] + parts[3]))

    def each_slab():
        return [(plane, j) for plane in range(planes) for j in range(half)]

    @pl.when(has_before)
    def _():
        c_inside = mask(total_rows // 2, tile * coarse_count - SUB // 2, (2 * SUB, LANES))
        c_factor_in[c_window, :] = c_inside * (COARSE_STEP / (2.0 * COARSE_SPACING))
        for j in range(half):
            c_slope_in[j, c_window, :] = c_inside * coarse_rows[3, pl.ds(j, 1), :]
            c_weight_in[j, c_window, :] = c_inside * coarse_rows[4, pl.ds(j, 1), :]

    @pl.when(has_up)
    def _():
        main_down.wait_recv()
        edge_down.wait_recv()
        for j in range(tiles):
            state[last, j, pl.ds(SUB - 1, 1), :] = from_up[pl.ds(j, 1), :]

    @pl.when(has_down)
    def _():
        main_up.wait_recv()
        edge_up.wait_recv()
        for j in range(tiles):
            state[last, j, pl.ds(tail + SUB, 1), :] = from_down[pl.ds(j, 1), :]

    @pl.when(has_before)
    def _():
        for plane, j in each_slab():
            start[plane, j] = restricted(plane, j, SUB, 2 * SUB)

    @pl.when(has_down)
    def _():
        main_down.wait_send()
        edge_down.wait_send()

    @pl.when(has_up)
    def _():
        main_up.wait_send()
        edge_up.wait_send()

    full = (SUB, row_count + 2 * SUB)
    mid = (lead, row_count + SUB)
    for wide, core in ((full, full), (full, mid), (mid, mid)):
        wave(
            state, held, change, fine_rows, fine_weights, (factor_in, slope_in, weight_in),
            tiles, tiles, wide, core,
        )

    first_part = (pl.ds(0, last), slice(None), pl.ds(0, HALO[0]))
    last_part = (last, slice(None), pl.ds(0, HALO[last]))
    to_own = remote(leaving, arrived, 4, cut + 1, tile)
    to_above = [
        remote(leaving.at[part], below_in.at[part], 5 + i, cut + 1, tile - 1)
        for i, part in enumerate((first_part, last_part))
    ]
    to_below = [
        remote(low.at[part], above_in.at[part], 7 + i, cut + 1, tile + 1)
        for i, part in enumerate((first_part, last_part))
    ]

    def leave(plane, j, value):
        leaving[plane, j] = value
        low[plane, j] = pltpu.roll(value, HALO[plane], 0)

    def launch():
        pl.semaphore_wait(ready, count(after))

        @pl.when(has_after & has_up)
        def _():
            for copy in to_above:
                copy.start()

        @pl.when(has_after & has_down)
        def _():
            for copy in to_below:
                copy.start()

        @pl.when(has_after)
        def _():
            to_own.start()

    @pl.when(cut == 0)
    def _():
        for plane, j in each_slab():
            leave(plane, j, restricted(plane, j, OWN, coarse_count))
        launch()

    for plane in range(planes):
        for row in range(0, row_count, SUB):
            parts = relaid([state[plane, j, pl.ds(OWN + row, SUB), :] for j in range(tiles)])
            for t in range(tiles):
                out_ref[plane, pl.ds(row, SUB), pl.ds(t * LANES, LANES)] = parts[t]

    @pl.when(has_before)
    def _():
        for plane, j in each_slab():
            end[plane, j] = restricted(plane, j, OWN, coarse_count)

        @pl.when(has_up)
        def _():
            for copy in to_below:
                copy.wait_recv()
            for plane, j in each_slab():
                size = HALO[plane]
                c_state[plane, j, pl.ds(lead - size, size), :] = (
                    above_in[plane, j, pl.ds(0, size), :]
                    - start[plane, j, pl.ds(SUB // 2 - size, size), :]
                )

        @pl.when(has_down)
        def _():
            for copy in to_above:
                copy.wait_recv()
            for plane, j in each_slab():
                size = HALO[plane]
                c_state[plane, j, pl.ds(lead + coarse_count, size), :] = (
                    below_in[plane, j, pl.ds(0, size), :]
                    - start[plane, j, pl.ds(SUB // 2 + coarse_count, size), :]
                )

        to_own.wait_recv()
        own = pl.ds(lead, coarse_count)
        for plane, j in each_slab():
            c_state[plane, j, own, :] = (
                arrived[plane, j] - start[plane, j, pl.ds(SUB // 2, coarse_count), :]
            )
        wave(
            c_state, c_held, c_change, coarse_rows, coarse_weights,
            (c_factor_in, c_slope_in, c_weight_in), half, tiles, (SUB, 2 * SUB), (SUB, 2 * SUB),
        )

        @pl.when(has_after)
        def _():
            for plane, j in each_slab():
                leave(plane, j, c_state[plane, j, own, :] + end[plane, j])
            launch()

        for plane in range(planes):
            parts = relaid([c_state[plane, j // 2, own, :] for j in range(tiles)])
            for t in range(tiles):
                for r in range(2):
                    spread[plane, t, pl.ds(r, coarse_count, stride=2), :] = parts[t]
            for t in range(tiles):
                at = (plane, slice(None), pl.ds(t * LANES, LANES))
                out_ref[at] = out_ref[at] + spread[plane, t]

    @pl.when(has_after & has_up)
    def _():
        for copy in to_above:
            copy.wait_send()

    @pl.when(has_after & has_down)
    def _():
        for copy in to_below:
            copy.wait_send()

    @pl.when(has_after)
    def _():
        to_own.wait_send()


def per_device(tile_count, slices, start_states):
    fields = start_states[0]
    planes, row_count, columns = fields.shape
    tiles = columns // LANES
    half = tiles // 2
    fine = line_tables(tiles, tiles, 1.0, columns, FINE_SPACING, FINE_STEP)
    coarse = line_tables(half, tiles, 2.0, columns, COARSE_SPACING, COARSE_STEP)
    fine_count = row_count + 4 * SUB
    coarse_count = row_count // 2
    c_count = coarse_count + 3 * SUB
    f32 = jnp.float32

    def vmem(*shape):
        return pltpu.VMEM(shape, f32)

    slab = vmem(planes, half, coarse_count, LANES)
    out = pl.pallas_call(
        functools.partial(kernel, tile_count, slices),
        out_shape=jax.ShapeDtypeStruct(fields.shape, f32),
        in_specs=[pl.BlockSpec(memory_space=pltpu.HBM)] * 5,
        out_specs=pl.BlockSpec(memory_space=pltpu.VMEM),
        scratch_shapes=[vmem(*fields.shape)]
        + [pltpu.VMEM(a.shape, a.dtype) for a in fine + coarse]
        + [vmem(tiles, LANES)] * 4
        + [
            vmem(planes, tiles, fine_count, LANES),
            vmem(tiles, 2 * (row_count + 2 * SUB), LANES),
            vmem(tiles, 2, fine_count, LANES),
            vmem(planes, half, c_count, LANES),
            vmem(half, 4 * SUB, LANES),
            vmem(half, 2, c_count, LANES),
            vmem(fine_count, LANES),
            vmem(tiles, fine_count, LANES),
            vmem(tiles, fine_count, LANES),
            vmem(c_count, LANES),
            vmem(half, c_count, LANES),
            vmem(half, c_count, LANES),
            vmem(planes, tiles, row_count, LANES),
            vmem(planes, half, 2 * SUB, LANES),
        ]
        + [slab] * 6
        + [
            pltpu.SemaphoreType.DMA((5,)),
            pltpu.SemaphoreType.DMA((9,)),
            pltpu.SemaphoreType.DMA((9,)),
            pltpu.SemaphoreType.REGULAR,
        ],
        compiler_params=pltpu.CompilerParams(
            collective_id=0, has_side_effects=True, vmem_limit_bytes=24 * 1024 * 1024
        ),
    )(*[pltpu.with_memory_space_constraint(jnp.asarray(a), pltpu.HBM) for a in (fields,) + fine + coarse])
    return out[None]


def solution(mesh):
    spec = P("cuts", None, "tile", None)
    body = functools.partial(per_device, mesh.shape["tile"], mesh.shape["cuts"])
    return jax.shard_map(body, mesh=mesh, in_specs=(spec,), out_specs=spec, check_vma=False)
```

```python
import functools

import ml_dtypes
import numpy as np
import jax
import jax.numpy as jnp
from jax import lax
from jax.experimental import pallas as pl
from jax.experimental.pallas import tpu as pltpu
from jax.sharding import PartitionSpec as P

STEPS = 3
FINE_SPACING = 0.05
COARSE_SPACING = 0.1
FINE_STEP = 0.015
COARSE_STEP = 0.045
LANES = 128
SUB = 8
HALO = (2, 2, 3)
OWN = 2 * SUB
SPILL = 5
MESH = pl.DeviceIdType.MESH


def line_tables(tiles, fine_tiles, stride, length, spacing, step):
    groups = LANES // fine_tiles
    lane = np.arange(LANES)
    chunk = (lane % fine_tiles) * groups + lane // fine_tiles
    columns = tiles * LANES
    centers = (np.arange(columns) + 0.5) * stride
    depth = (0.9 + 0.3 * np.sin(6.0 * np.pi * centers / length)).reshape(LANES, tiles).T
    beta = depth * depth / 3.0
    b = beta / spacing**2
    mid = 1.0 + 2.0 * b
    last = tiles - 1
    inv = np.zeros_like(b)
    cp = np.zeros_like(b)
    for j in range(last):
        inv[j] = 1.0 / (mid[j] - (b[j] * cp[j - 1] if j else 0.0))
        cp[j] = b[j] * inv[j]
    run = np.ones_like(b)
    for j in range(1, tiles):
        run[j] = run[j - 1] * cp[j - 1]
    p = np.zeros_like(b)
    q = np.zeros_like(b)
    q[last] = 1.0
    for j in range(last - 1, -1, -1):
        p[j] = run[j + 1] + cp[j] * p[j + 1]
        q[j] = cp[j] * q[j + 1]
    system = np.zeros((LANES, LANES))
    for k in range(LANES):
        system[k, k] = mid[last, k] - b[last, k] * q[last - 1, k]
        if k:
            system[k, k - 1] = -b[last, k] * p[last - 1, k]
        if k + 1 < LANES:
            system[k, k] -= b[last, k] * p[0, k + 1]
            system[k, k + 1] = -b[last, k] * q[0, k + 1]
    solve = np.linalg.inv(system).T[chunk][:, chunk]
    high = solve.astype(ml_dtypes.bfloat16)
    low = (solve - high.astype(np.float64)).astype(ml_dtypes.bfloat16)
    half = np.concatenate([high, low], axis=1)
    weights = np.concatenate([half, half], axis=0)
    slope = step * depth / (2.0 * spacing)
    weight = beta / (spacing**2 + 4.0 * beta)
    inv[last] = b[last]
    rows = np.stack([inv, cp, run, slope, weight])[:, :, chunk]
    return rows.astype(np.float32), weights


def relaid(tiles):
    tiles = list(tiles)
    lane = lax.broadcasted_iota(jnp.int32, tiles[0].shape, 1)
    bit = 1
    while bit < len(tiles):
        keep = (lane & bit) == 0
        for t in range(len(tiles)):
            if t & bit == 0:
                a, b = tiles[t], tiles[t | bit]
                tiles[t] = jnp.where(keep, a, pltpu.roll(b, bit, 1))
                tiles[t | bit] = jnp.where(keep, pltpu.roll(a, LANES - bit, 1), b)
        bit *= 2
    return tiles


def wave(state, held, change, rows, weights, inside, tiles, fine_tiles, wide, core):
    factor_in, slope_in, weight_in = inside
    h0, hn = wide
    t0, tn = core
    at = pl.ds(t0, tn)

    def lane(x):
        return lax.broadcasted_iota(jnp.int32, x.shape, 1)

    def chunk_before(x):
        wrapped = jnp.where(lane(x) == 0, 0.0, pltpu.roll(x, fine_tiles + 1, 1))
        return jnp.where(lane(x) >= fine_tiles, pltpu.roll(x, fine_tiles, 1), wrapped)

    def chunk_after(x):
        wrapped = jnp.where(lane(x) == LANES - 1, 0.0, pltpu.roll(x, LANES - fine_tiles - 1, 1))
        return jnp.where(
            lane(x) < LANES - fine_tiles, pltpu.roll(x, LANES - fine_tiles, 1), wrapped
        )

    def across(load, j):
        right = load(j + 1) if j + 1 < tiles else chunk_after(load(0))
        left = load(j - 1) if j else chunk_before(load(tiles - 1))
        return right - left

    def table(kind, j):
        return rows[kind, pl.ds(j, 1), :]

    last = tiles - 1
    near = pl.ds(h0, hn)
    factor = factor_in[near, :]
    for j in range(tiles):
        along = across(lambda i: state[1, i, near, :], j)
        down = state[2, j, pl.ds(h0 + 1, hn), :] - state[2, j, pl.ds(h0 - 1, hn), :]
        state[0, j, near, :] = state[0, j, near, :] - factor * (along + down)
    total = None
    inner = None
    for j in range(tiles):
        along = across(lambda i: state[0, i, at, :], j)
        down = state[0, j, pl.ds(t0 + 1, tn), :] - state[0, j, pl.ds(t0 - 1, tn), :]
        force_x = state[1, j, at, :] - table(3, j) * along
        force_y = state[2, j, at, :] - slope_in[j, at, :] * down
        force = jnp.concatenate([force_x, force_y], axis=0)
        if j == last:
            edge = force + table(0, j) * inner
        elif j == 0:
            inner = force * table(0, j)
            total = inner
            held[j, pl.ds(0, 2 * tn), :] = inner
        else:
            inner = force * table(0, j) + table(1, j) * inner
            total = total + table(2, j) * inner
            held[j, pl.ds(0, 2 * tn), :] = inner
    met = edge + table(0, last) * chunk_after(total)
    high = met.astype(jnp.bfloat16)
    low = (met - high.astype(jnp.float32)).astype(jnp.bfloat16)
    met = jnp.dot(
        jnp.concatenate([high, low], axis=1),
        weights[...],
        preferred_element_type=jnp.float32,
    )
    value = met[:, :LANES] + met[:, LANES:]
    before = chunk_before(value)
    for j in range(last, -1, -1):
        if j < last:
            value = (
                held[j, pl.ds(0, 2 * tn), :] + table(2, j + 1) * before + table(1, j) * value
            )
        for part in range(2):
            trial = value[part * tn : (part + 1) * tn]
            moved = trial - state[1 + part, j, at, :]
            change[j, part, at, :] = moved
            around = change[j, part, pl.ds(t0 + 1, tn), :] + change[j, part, pl.ds(t0 - 1, tn), :]
            state[1 + part, j, at, :] = trial + weight_in[j, at, :] * (around - 2.0 * moved)


def kernel(
    tile_count, slices, x_hbm, fine_rows_hbm, fine_weights_hbm, coarse_rows_hbm,
    coarse_weights_hbm, out_ref,
    x_ref, fine_rows, fine_weights, coarse_rows, coarse_weights,
    up_edge, down_edge, from_up_edge, from_down_edge, state, held, change,
    from_up, from_down, up_spill, down_spill, from_up_spill, from_down_spill,
    c_state, c_held, c_change, factor_in, slope_in, weight_in, c_factor_in, c_slope_in,
    c_weight_in, spread, start, low_start, start_above, start_below,
    end, arrived, leaving, low, above_in, below_in,
    local, send, recv, ready,
):
    cut = lax.axis_index("cuts")
    tile = lax.axis_index("tile")
    has_up = tile > 0
    has_down = tile < tile_count - 1
    has_before = cut > 0
    has_after = cut < slices - 1
    planes, row_count, columns = x_ref.shape
    tiles = columns // LANES
    half = tiles // 2
    total_rows = row_count * tile_count
    coarse_count = row_count // 2
    last = planes - 1
    tail = OWN + row_count
    lead = SUB + SUB // 2
    deep = HALO[last]

    pairs = [(fine_rows_hbm, fine_rows)]
    pairs += [(x_hbm.at[plane], x_ref.at[plane]) for plane in range(planes)]
    pairs += [
        (fine_weights_hbm, fine_weights), (coarse_rows_hbm, coarse_rows),
        (coarse_weights_hbm, coarse_weights),
    ]
    loads = [pltpu.make_async_copy(a, b, local.at[i]) for i, (a, b) in enumerate(pairs)]
    for load in loads:
        load.start()

    zero = jnp.zeros((SUB, LANES), jnp.float32)

    def each_slab():
        return [(plane, j) for plane in range(planes) for j in range(half)]

    for plane, j in each_slab():
        from_up_spill[plane, j] = zero
        from_down_spill[plane, j, pl.ds(0, SUB), :] = zero
        from_down_spill[plane, j, pl.ds(SUB, SUB), :] = zero

    barrier = pltpu.get_barrier_semaphore()
    beside = [(has_up, cut, tile - 1), (has_down, cut, tile + 1)]

    def in_cut(there, other):
        return [
            (there, other, tile),
            (there & has_up, other, tile - 1),
            (there & has_down, other, tile + 1),
        ]

    before = in_cut(has_before, cut - 1)
    after = in_cut(has_after, cut + 1)

    def signal(semaphore, devices):
        for exists, to_cut, to_tile in devices:
            @pl.when(exists)
            def _():
                pl.semaphore_signal(
                    semaphore, inc=1, device_id=(to_cut, to_tile), device_id_type=MESH
                )

    def count(devices):
        return sum(exists.astype(jnp.int32) for exists, _, _ in devices)

    signal(barrier, beside + after)

    def remote(source, target, which, to_cut, to_tile):
        return pltpu.make_async_remote_copy(
            src_ref=source, dst_ref=target, send_sem=send.at[which], recv_sem=recv.at[which],
            device_id=(to_cut, to_tile), device_id_type=MESH,
        )

    def rows_at(ref, row, count):
        return ref.at[:, :, pl.ds(row, count), :]

    spill_up = remote(
        rows_at(up_spill, 0, SPILL), rows_at(from_down_spill, SUB, SPILL), 0, cut, tile - 1
    )
    spill_down = remote(
        rows_at(down_spill, 0, SPILL), rows_at(from_up_spill, 0, SPILL), 1, cut, tile + 1
    )
    rest_up = [
        remote(rows_at(state, SUB, SUB), from_down, 2, cut, tile - 1),
        remote(up_edge, from_down_edge, 3, cut, tile - 1),
    ]
    rest_down = [
        remote(rows_at(state, tail, SUB), from_up, 4, cut, tile + 1),
        remote(down_edge, from_up_edge, 5, cut, tile + 1),
    ]
    start_up = remote(rows_at(start, 0, deep), start_below, 6, cut, tile - 1)
    start_down = remote(rows_at(low_start, 0, deep), start_above, 7, cut, tile + 1)

    for j in range(tiles):
        for row in (0, SUB, tail, tail + SUB):
            for plane in range(planes):
                state[plane, j, pl.ds(row, SUB), :] = zero
            for part in range(2):
                change[j, part, pl.ds(row, SUB), :] = zero

    def mask(total, origin, shape):
        at = lax.broadcasted_iota(jnp.int32, shape, 0) + origin
        return ((at >= 0) & (at < total)).astype(jnp.float32)

    loads[0].wait()
    inside = mask(total_rows, tile * row_count - SUB, (row_count + 2 * SUB, LANES))
    window = pl.ds(SUB, row_count + 2 * SUB)
    factor_in[window, :] = inside * (FINE_STEP / (2.0 * FINE_SPACING))
    for j in range(tiles):
        slope_in[j, window, :] = inside * fine_rows[3, pl.ds(j, 1), :]
        weight_in[j, window, :] = inside * fine_rows[4, pl.ds(j, 1), :]

    for plane in range(planes):
        loads[1 + plane].wait()
        for row in range(0, row_count, SUB):
            values = x_ref[plane, pl.ds(row, SUB), :]
            parts = relaid([values[:, t * LANES : (t + 1) * LANES] for t in range(tiles)])
            for j in range(tiles):
                state[plane, j, pl.ds(OWN + row, SUB), :] = parts[j]

    def restricted(plane, j, row, count):
        parts = [
            state[plane, 2 * j + k, pl.ds(row + r, count, stride=2), :]
            for r in range(2)
            for k in range(2)
        ]
        return 0.25 * ((parts[0] + parts[1]) + (parts[2] + parts[3]))

    @pl.when(has_before)
    def _():
        for plane, j in each_slab():
            value = restricted(plane, j, OWN, coarse_count)
            start[plane, j] = value
            low_start[plane, j] = pltpu.roll(value, deep, 0)

    loads[1 + planes].wait()
    inner = (lead, row_count + SUB)
    outer = (SUB, row_count + 2 * SUB)
    for wide, core in ((inner, inner), (inner, outer), (outer, outer)):
        wave(
            state, held, change, fine_rows, fine_weights, (factor_in, slope_in, weight_in),
            tiles, tiles, wide, core,
        )
    for j in range(tiles):
        for row, near, edge in ((SUB - 1, SUB, up_edge), (tail + SUB, tail + SUB - 1, down_edge)):
            value = fine_rows[4, pl.ds(j, 1), :] * change[j, 1, pl.ds(near, 1), :]
            state[last, j, pl.ds(row, 1), :] = value
            edge[pl.ds(j, 1), :] = value

    pl.semaphore_wait(barrier, count(beside + before))

    @pl.when(has_after)
    def _():
        @pl.when(has_up)
        def _():
            for plane, j in each_slab():
                up_spill[plane, j, pl.ds(0, SPILL), :] = restricted(
                    plane, j, OWN - 2 * SPILL, SPILL
                )
            spill_up.start()

        @pl.when(has_down)
        def _():
            for plane, j in each_slab():
                down_spill[plane, j, pl.ds(0, SPILL), :] = restricted(plane, j, tail, SPILL)
            spill_down.start()

    @pl.when(has_before)
    def _():
        @pl.when(has_up)
        def _():
            start_up.start()

        @pl.when(has_down)
        def _():
            start_down.start()

    def pass_rest():
        @pl.when(has_up)
        def _():
            for copy in rest_up:
                copy.start()

        @pl.when(has_down)
        def _():
            for copy in rest_down:
                copy.start()

    pl.when(has_before)(pass_rest)
    signal(ready, before)
    for load in loads[2 + planes :]:
        load.wait()

    first_part = (pl.ds(0, last), slice(None), pl.ds(0, HALO[0]))
    last_part = (last, slice(None), pl.ds(0, HALO[last]))
    to_own = remote(leaving, arrived, 8, cut + 1, tile)
    to_above = [
        remote(leaving.at[part], below_in.at[part], 9 + i, cut + 1, tile - 1)
        for i, part in enumerate((first_part, last_part))
    ]
    to_below = [
        remote(low.at[part], above_in.at[part], 11 + i, cut + 1, tile + 1)
        for i, part in enumerate((first_part, last_part))
    ]

    def leave(plane, j, value):
        leaving[plane, j] = value
        low[plane, j] = pltpu.roll(value, HALO[plane], 0)

    def launch():
        pl.semaphore_wait(ready, count(after))

        @pl.when(has_after & has_up)
        def _():
            for copy in to_above:
                copy.start()

        @pl.when(has_after & has_down)
        def _():
            for copy in to_below:
                copy.start()

        @pl.when(has_after)
        def _():
            to_own.start()

    def landed():
        for there, copies in (
            (has_after & has_up, to_above), (has_after & has_down, to_below),
            (has_after, [to_own]),
        ):
            @pl.when(there)
            def _():
                for copy in copies:
                    copy.wait_send()

    def natural():
        for has, copies, into, edges, row, at in (
            (has_up, rest_down, from_up, from_up_edge, OWN, OWN + SUB),
            (has_down, rest_up, from_down, from_down_edge, tail - SUB, tail - SUB - 1),
        ):
            @pl.when(has)
            def _():
                for copy in copies:
                    copy.wait_recv()
                for j in range(tiles):
                    for plane in range(planes):
                        rows = pl.ds(row, SUB)
                        state[plane, j, rows, :] = state[plane, j, rows, :] + into[plane, j]
                for j in range(tiles):
                    one = pl.ds(at, 1)
                    state[last, j, one, :] = state[last, j, one, :] + edges[pl.ds(j, 1), :]

        for plane in range(planes):
            for row in range(0, row_count, SUB):
                parts = relaid([state[plane, j, pl.ds(OWN + row, SUB), :] for j in range(tiles)])
                for t in range(tiles):
                    out_ref[plane, pl.ds(row, SUB), pl.ds(t * LANES, LANES)] = parts[t]

    @pl.when(has_after)
    def _():
        for plane, j in each_slab():
            end[plane, j] = restricted(plane, j, OWN, coarse_count)

        @pl.when(has_up)
        def _():
            spill_down.wait_recv()

        @pl.when(has_down)
        def _():
            spill_up.wait_recv()

        for plane, j in each_slab():
            value = (
                end[plane, j]
                + from_up_spill[plane, j]
                + from_down_spill[plane, j, pl.ds(SPILL, SUB), :]
            )
            end[plane, j] = value

    @pl.when(cut == 0)
    def _():
        for plane, j in each_slab():
            leave(plane, j, end[plane, j])
        launch()
        landed()
        pass_rest()

    @pl.when(jnp.logical_not(has_after))
    def _():
        natural()

    own = pl.ds(lead, coarse_count)

    @pl.when(has_before)
    def _():
        c_window = pl.ds(SUB, 2 * SUB)
        c_inside = mask(total_rows // 2, tile * coarse_count - SUB // 2, (2 * SUB, LANES))
        c_factor_in[c_window, :] = c_inside * (COARSE_STEP / (2.0 * COARSE_SPACING))
        for j in range(half):
            c_slope_in[j, c_window, :] = c_inside * coarse_rows[3, pl.ds(j, 1), :]
            c_weight_in[j, c_window, :] = c_inside * coarse_rows[4, pl.ds(j, 1), :]
            for row in range(0, 4 * SUB, SUB):
                for plane in range(planes):
                    c_state[plane, j, pl.ds(row, SUB), :] = zero
                for part in range(2):
                    c_change[j, part, pl.ds(row, SUB), :] = zero

        @pl.when(has_up)
        def _():
            start_down.wait_recv()
            for copy in to_below:
                copy.wait_recv()
            for plane, j in each_slab():
                size = HALO[plane]
                c_state[plane, j, pl.ds(lead - size, size), :] = (
                    above_in[plane, j, pl.ds(0, size), :]
                    - start_above[plane, j, pl.ds(deep - size, size), :]
                )

        @pl.when(has_down)
        def _():
            start_up.wait_recv()
            for copy in to_above:
                copy.wait_recv()
            for plane, j in each_slab():
                size = HALO[plane]
                c_state[plane, j, pl.ds(lead + coarse_count, size), :] = (
                    below_in[plane, j, pl.ds(0, size), :]
                    - start_below[plane, j, pl.ds(0, size), :]
                )

        to_own.wait_recv()
        for plane, j in each_slab():
            c_state[plane, j, own, :] = arrived[plane, j] - start[plane, j]
        wave(
            c_state, c_held, c_change, coarse_rows, coarse_weights,
            (c_factor_in, c_slope_in, c_weight_in), half, tiles, (SUB, 2 * SUB), (SUB, 2 * SUB),
        )

        @pl.when(has_after)
        def _():
            for plane, j in each_slab():
                leave(plane, j, c_state[plane, j, own, :] + end[plane, j])
            launch()

    @pl.when(has_after)
    def _():
        natural()

    @pl.when(has_before)
    def _():
        for plane in range(planes):
            parts = relaid([c_state[plane, j // 2, own, :] for j in range(tiles)])
            for t in range(tiles):
                for r in range(2):
                    spread[plane, t, pl.ds(r, coarse_count, stride=2), :] = parts[t]
            for t in range(tiles):
                at = (plane, slice(None), pl.ds(t * LANES, LANES))
                out_ref[at] = out_ref[at] + spread[plane, t]

    pl.when(has_before)(landed)
    for there, copies in (
        (has_up, rest_up), (has_down, rest_down),
        (has_after & has_up, [spill_up]), (has_after & has_down, [spill_down]),
        (has_before & has_up, [start_up]), (has_before & has_down, [start_down]),
    ):
        @pl.when(there)
        def _():
            for copy in copies:
                copy.wait_send()


def per_device(tile_count, slices, start_states):
    fields = start_states[0]
    planes, row_count, columns = fields.shape
    tiles = columns // LANES
    half = tiles // 2
    fine = line_tables(tiles, tiles, 1.0, columns, FINE_SPACING, FINE_STEP)
    coarse = line_tables(half, tiles, 2.0, columns, COARSE_SPACING, COARSE_STEP)
    fine_count = row_count + 4 * SUB
    coarse_count = row_count // 2
    c_count = coarse_count + 3 * SUB
    f32 = jnp.float32

    def vmem(*shape):
        return pltpu.VMEM(shape, f32)

    slab = vmem(planes, half, coarse_count, LANES)
    out = pl.pallas_call(
        functools.partial(kernel, tile_count, slices),
        out_shape=jax.ShapeDtypeStruct(fields.shape, f32),
        in_specs=[pl.BlockSpec(memory_space=pltpu.HBM)] * 5,
        out_specs=pl.BlockSpec(memory_space=pltpu.VMEM),
        scratch_shapes=[vmem(*fields.shape)]
        + [pltpu.VMEM(a.shape, a.dtype) for a in fine + coarse]
        + [vmem(tiles, LANES)] * 4
        + [
            vmem(planes, tiles, fine_count, LANES),
            vmem(tiles, 2 * (row_count + 2 * SUB), LANES),
            vmem(tiles, 2, fine_count, LANES),
        ]
        + [vmem(planes, tiles, SUB, LANES)] * 2
        + [slab] * 3
        + [
            vmem(planes, half, 2 * SUB, LANES),
            vmem(planes, half, c_count, LANES),
            vmem(half, 4 * SUB, LANES),
            vmem(half, 2, c_count, LANES),
            vmem(fine_count, LANES),
            vmem(tiles, fine_count, LANES),
            vmem(tiles, fine_count, LANES),
            vmem(c_count, LANES),
            vmem(half, c_count, LANES),
            vmem(half, c_count, LANES),
            vmem(planes, tiles, row_count, LANES),
        ]
        + [slab] * 2
        + [vmem(planes, half, HALO[-1], LANES)] * 2
        + [slab] * 6
        + [
            pltpu.SemaphoreType.DMA((len(fine + coarse) + planes,)),
            pltpu.SemaphoreType.DMA((13,)),
            pltpu.SemaphoreType.DMA((13,)),
            pltpu.SemaphoreType.REGULAR,
        ],
        compiler_params=pltpu.CompilerParams(
            collective_id=0, has_side_effects=True, vmem_limit_bytes=24 * 1024 * 1024
        ),
    )(*[pltpu.with_memory_space_constraint(jnp.asarray(a), pltpu.HBM) for a in (fields,) + fine + coarse])
    return out[None]


def solution(mesh):
    spec = P("cuts", None, "tile", None)
    body = functools.partial(per_device, mesh.shape["tile"], mesh.shape["cuts"])
    return jax.shard_map(body, mesh=mesh, in_specs=(spec,), out_specs=spec, check_vma=False)
```

```python
import functools

import ml_dtypes
import numpy as np
import jax
import jax.numpy as jnp
from jax import lax
from jax.experimental import pallas as pl
from jax.experimental.pallas import tpu as pltpu
from jax.sharding import PartitionSpec as P

STEPS = 3
FINE_SPACING = 0.05
COARSE_SPACING = 0.1
FINE_STEP = 0.015
COARSE_STEP = 0.045
LANES = 128
SUB = 8
HALO = (2, 2, 3)
OWN = 2 * SUB
SPILL = 5
FAR = 2 * HALO[-1]
MESH = pl.DeviceIdType.MESH


def line_tables(tiles, fine_tiles, stride, length, spacing, step):
    groups = LANES // fine_tiles
    lane = np.arange(LANES)
    chunk = (lane % fine_tiles) * groups + lane // fine_tiles
    columns = tiles * LANES
    centers = (np.arange(columns) + 0.5) * stride
    depth = (0.9 + 0.3 * np.sin(6.0 * np.pi * centers / length)).reshape(LANES, tiles).T
    beta = depth * depth / 3.0
    b = beta / spacing**2
    mid = 1.0 + 2.0 * b
    last = tiles - 1
    inv = np.zeros_like(b)
    cp = np.zeros_like(b)
    for j in range(last):
        inv[j] = 1.0 / (mid[j] - (b[j] * cp[j - 1] if j else 0.0))
        cp[j] = b[j] * inv[j]
    run = np.ones_like(b)
    for j in range(1, tiles):
        run[j] = run[j - 1] * cp[j - 1]
    p = np.zeros_like(b)
    q = np.zeros_like(b)
    q[last] = 1.0
    for j in range(last - 1, -1, -1):
        p[j] = run[j + 1] + cp[j] * p[j + 1]
        q[j] = cp[j] * q[j + 1]
    system = np.zeros((LANES, LANES))
    for k in range(LANES):
        system[k, k] = mid[last, k] - b[last, k] * q[last - 1, k]
        if k:
            system[k, k - 1] = -b[last, k] * p[last - 1, k]
        if k + 1 < LANES:
            system[k, k] -= b[last, k] * p[0, k + 1]
            system[k, k + 1] = -b[last, k] * q[0, k + 1]
    solve = np.linalg.inv(system).T[chunk][:, chunk]
    high = solve.astype(ml_dtypes.bfloat16)
    low = (solve - high.astype(np.float64)).astype(ml_dtypes.bfloat16)
    half = np.concatenate([high, low], axis=1)
    weights = np.concatenate([half, half], axis=0)
    slope = step * depth / (2.0 * spacing)
    weight = beta / (spacing**2 + 4.0 * beta)
    inv[last] = b[last]
    rows = np.stack([inv, cp, run, slope, weight])[:, :, chunk]
    return rows.astype(np.float32), weights


def relaid(tiles):
    tiles = list(tiles)
    lane = lax.broadcasted_iota(jnp.int32, tiles[0].shape, 1)
    bit = 1
    while bit < len(tiles):
        keep = (lane & bit) == 0
        for t in range(len(tiles)):
            if t & bit == 0:
                a, b = tiles[t], tiles[t | bit]
                tiles[t] = jnp.where(keep, a, pltpu.roll(b, bit, 1))
                tiles[t | bit] = jnp.where(keep, pltpu.roll(a, LANES - bit, 1), b)
        bit *= 2
    return tiles


def wave(state, held, change, rows, weights, inside, tiles, fine_tiles, wide, core):
    factor_in, slope_in, weight_in = inside
    h0, hn = wide
    t0, tn = core
    at = pl.ds(t0, tn)

    def lane(x):
        return lax.broadcasted_iota(jnp.int32, x.shape, 1)

    def chunk_before(x):
        wrapped = jnp.where(lane(x) == 0, 0.0, pltpu.roll(x, fine_tiles + 1, 1))
        return jnp.where(lane(x) >= fine_tiles, pltpu.roll(x, fine_tiles, 1), wrapped)

    def chunk_after(x):
        wrapped = jnp.where(lane(x) == LANES - 1, 0.0, pltpu.roll(x, LANES - fine_tiles - 1, 1))
        return jnp.where(
            lane(x) < LANES - fine_tiles, pltpu.roll(x, LANES - fine_tiles, 1), wrapped
        )

    def across(load, j):
        right = load(j + 1) if j + 1 < tiles else chunk_after(load(0))
        left = load(j - 1) if j else chunk_before(load(tiles - 1))
        return right - left

    def table(kind, j):
        return rows[kind, pl.ds(j, 1), :]

    last = tiles - 1
    near = pl.ds(h0, hn)
    factor = factor_in[near, :]
    for j in range(tiles):
        along = across(lambda i: state[1, i, near, :], j)
        down = state[2, j, pl.ds(h0 + 1, hn), :] - state[2, j, pl.ds(h0 - 1, hn), :]
        state[0, j, near, :] = state[0, j, near, :] - factor * (along + down)
    def forcing(part, j):
        if part == 0:
            along = across(lambda i: state[0, i, at, :], j)
            return state[1, j, at, :] - table(3, j) * along
        down = state[0, j, pl.ds(t0 + 1, tn), :] - state[0, j, pl.ds(t0 - 1, tn), :]
        return state[2, j, at, :] - slope_in[j, at, :] * down

    solved = []
    for part in range(2):
        spot = pl.ds(part * tn, tn)
        total = None
        inner = None
        for j in range(last):
            force = forcing(part, j)
            if j == 0:
                inner = force * table(0, j)
                total = inner
            else:
                inner = force * table(0, j) + table(1, j) * inner
                total = total + table(2, j) * inner
            held[j, spot, :] = inner
        edge = forcing(part, last) + table(0, last) * (inner + chunk_after(total))
        high = edge.astype(jnp.bfloat16)
        low = (edge - high.astype(jnp.float32)).astype(jnp.bfloat16)
        solved.append(
            jnp.dot(
                jnp.concatenate([high, low], axis=1),
                weights[...],
                preferred_element_type=jnp.float32,
            )
        )
    for part in range(2):
        spot = pl.ds(part * tn, tn)
        value = solved[part][:, :LANES] + solved[part][:, LANES:]
        before = chunk_before(value)
        for j in range(last, -1, -1):
            if j < last:
                value = held[j, spot, :] + table(2, j + 1) * before + table(1, j) * value
            moved = value - state[1 + part, j, at, :]
            change[j, part, at, :] = moved
            around = change[j, part, pl.ds(t0 + 1, tn), :] + change[j, part, pl.ds(t0 - 1, tn), :]
            state[1 + part, j, at, :] = value + weight_in[j, at, :] * (around - 2.0 * moved)


def kernel(
    tile_count, slices, x_hbm, fine_rows_hbm, fine_weights_hbm, coarse_rows_hbm,
    coarse_weights_hbm, out_ref,
    x_ref, fine_rows, fine_weights, coarse_rows, coarse_weights,
    up_edge, down_edge, from_up_edge, from_down_edge, state, held, change,
    from_up, from_down, up_spill, down_spill, from_up_spill, from_down_spill,
    c_state, c_held, c_change, factor_in, slope_in, weight_in, c_factor_in, c_slope_in,
    c_weight_in, offset, spread, start, low_start, start_above, start_below,
    end, arrived, leaving, low, above_in, below_in, far_in, far_leaving, far_low, gain,
    far_above, far_below, side_above, side_below, local, send, recv, ready, far_ready,
):
    cut = lax.axis_index("cuts")
    tile = lax.axis_index("tile")
    has_up = tile > 0
    has_down = tile < tile_count - 1
    has_before = cut > 0
    has_after = cut < slices - 1
    odd = cut % 2 == 1
    even = jnp.logical_not(odd)
    has_far_before = odd & (cut > 1)
    has_far_after = odd & (cut < slices - 2)
    planes, row_count, columns = x_ref.shape
    tiles = columns // LANES
    half = tiles // 2
    total_rows = row_count * tile_count
    coarse_count = row_count // 2
    last = planes - 1
    tail = OWN + row_count
    lead = SUB + SUB // 2
    deep = HALO[last]

    pairs = [(fine_rows_hbm, fine_rows)]
    pairs += [(x_hbm.at[plane], x_ref.at[plane]) for plane in range(planes)]
    pairs += [
        (fine_weights_hbm, fine_weights), (coarse_rows_hbm, coarse_rows),
        (coarse_weights_hbm, coarse_weights),
    ]
    loads = [pltpu.make_async_copy(a, b, local.at[i]) for i, (a, b) in enumerate(pairs)]
    for load in loads:
        load.start()

    zero = jnp.zeros((SUB, LANES), jnp.float32)

    def each_slab():
        return [(plane, j) for plane in range(planes) for j in range(half)]

    for plane, j in each_slab():
        from_up_spill[plane, j] = zero
        from_down_spill[plane, j, pl.ds(0, SUB), :] = zero
        from_down_spill[plane, j, pl.ds(SUB, SUB), :] = zero

    barrier = pltpu.get_barrier_semaphore()
    beside = [(has_up, cut, tile - 1), (has_down, cut, tile + 1)]

    def in_cut(there, other):
        return [
            (there, other, tile),
            (there & has_up, other, tile - 1),
            (there & has_down, other, tile + 1),
        ]

    before = in_cut(has_before, cut - 1)
    after = in_cut(has_after, cut + 1)
    far_before = in_cut(has_far_before, cut - 2)
    far_after = in_cut(has_far_after, cut + 2)

    def signal(semaphore, devices):
        for exists, to_cut, to_tile in devices:
            @pl.when(exists)
            def _():
                pl.semaphore_signal(
                    semaphore, inc=1, device_id=(to_cut, to_tile), device_id_type=MESH
                )

    def count(devices):
        return sum(exists.astype(jnp.int32) for exists, _, _ in devices)

    signal(barrier, beside + after + far_after)

    def remote(source, target, which, to_cut, to_tile):
        return pltpu.make_async_remote_copy(
            src_ref=source, dst_ref=target, send_sem=send.at[which], recv_sem=recv.at[which],
            device_id=(to_cut, to_tile), device_id_type=MESH,
        )

    def rows_at(ref, row, count):
        return ref.at[:, :, pl.ds(row, count), :]

    spill_up = remote(
        rows_at(up_spill, 0, SPILL), rows_at(from_down_spill, SUB, SPILL), 0, cut, tile - 1
    )
    spill_down = remote(
        rows_at(down_spill, 0, SPILL), rows_at(from_up_spill, 0, SPILL), 1, cut, tile + 1
    )
    rest_up = [
        remote(rows_at(state, SUB, SUB), from_down, 2, cut, tile - 1),
        remote(up_edge, from_down_edge, 3, cut, tile - 1),
    ]
    rest_down = [
        remote(rows_at(state, tail, SUB), from_up, 4, cut, tile + 1),
        remote(down_edge, from_up_edge, 5, cut, tile + 1),
    ]
    start_up = remote(rows_at(start, 0, deep), start_below, 6, cut, tile - 1)
    start_down = remote(rows_at(low_start, 0, deep), start_above, 7, cut, tile + 1)

    for j in range(tiles):
        for row in (0, SUB, tail, tail + SUB):
            for plane in range(planes):
                state[plane, j, pl.ds(row, SUB), :] = zero
            for part in range(2):
                change[j, part, pl.ds(row, SUB), :] = zero

    def mask(total, origin, shape):
        at = lax.broadcasted_iota(jnp.int32, shape, 0) + origin
        return ((at >= 0) & (at < total)).astype(jnp.float32)

    loads[0].wait()
    inside = mask(total_rows, tile * row_count - SUB, (row_count + 2 * SUB, LANES))
    window = pl.ds(SUB, row_count + 2 * SUB)
    factor_in[window, :] = inside * (FINE_STEP / (2.0 * FINE_SPACING))
    for j in range(tiles):
        slope_in[j, window, :] = inside * fine_rows[3, pl.ds(j, 1), :]
        weight_in[j, window, :] = inside * fine_rows[4, pl.ds(j, 1), :]

    for plane in range(planes):
        loads[1 + plane].wait()
        for row in range(0, row_count, SUB):
            values = x_ref[plane, pl.ds(row, SUB), :]
            parts = relaid([values[:, t * LANES : (t + 1) * LANES] for t in range(tiles)])
            for j in range(tiles):
                state[plane, j, pl.ds(OWN + row, SUB), :] = parts[j]

    def restricted(plane, j, row, count):
        parts = [
            state[plane, 2 * j + k, pl.ds(row + r, count, stride=2), :]
            for r in range(2)
            for k in range(2)
        ]
        return 0.25 * ((parts[0] + parts[1]) + (parts[2] + parts[3]))

    @pl.when(has_before)
    def _():
        for plane, j in each_slab():
            value = restricted(plane, j, OWN, coarse_count)
            start[plane, j] = value
            low_start[plane, j] = pltpu.roll(value, deep, 0)

    loads[1 + planes].wait()
    inner = (lead, row_count + SUB)
    outer = (SUB, row_count + 2 * SUB)
    for wide, core in ((inner, inner), (inner, outer), (outer, outer)):
        wave(
            state, held, change, fine_rows, fine_weights, (factor_in, slope_in, weight_in),
            tiles, tiles, wide, core,
        )
    for j in range(tiles):
        for row, near, edge in ((SUB - 1, SUB, up_edge), (tail + SUB, tail + SUB - 1, down_edge)):
            value = fine_rows[4, pl.ds(j, 1), :] * change[j, 1, pl.ds(near, 1), :]
            state[last, j, pl.ds(row, 1), :] = value
            edge[pl.ds(j, 1), :] = value

    pl.semaphore_wait(barrier, count(beside + before + far_before))

    @pl.when(has_after)
    def _():
        @pl.when(has_up)
        def _():
            for plane, j in each_slab():
                up_spill[plane, j, pl.ds(0, SPILL), :] = restricted(
                    plane, j, OWN - 2 * SPILL, SPILL
                )
            spill_up.start()

        @pl.when(has_down)
        def _():
            for plane, j in each_slab():
                down_spill[plane, j, pl.ds(0, SPILL), :] = restricted(plane, j, tail, SPILL)
            spill_down.start()

    @pl.when(has_before)
    def _():
        @pl.when(has_up)
        def _():
            start_up.start()

        @pl.when(has_down)
        def _():
            start_down.start()

    def pass_rest():
        @pl.when(has_up)
        def _():
            for copy in rest_up:
                copy.start()

        @pl.when(has_down)
        def _():
            for copy in rest_down:
                copy.start()

    pl.when(has_before)(pass_rest)
    signal(ready, before)
    signal(far_ready, far_before)
    for load in loads[2 + planes :]:
        load.wait()

    first_part = (pl.ds(0, last), slice(None), pl.ds(0, HALO[0]))
    last_part = (last, slice(None), pl.ds(0, HALO[last]))
    to_own = remote(leaving, arrived, 8, cut + 1, tile)
    to_above = [
        remote(leaving.at[part], below_in.at[part], 9 + i, cut + 1, tile - 1)
        for i, part in enumerate((first_part, last_part))
    ]
    to_below = [
        remote(low.at[part], above_in.at[part], 11 + i, cut + 1, tile + 1)
        for i, part in enumerate((first_part, last_part))
    ]

    far_own = remote(far_leaving, far_in, 13, cut + 2, tile)
    far_up = remote(rows_at(far_leaving, 0, FAR), far_below, 14, cut + 2, tile - 1)
    far_down = remote(rows_at(far_low, 0, FAR), far_above, 15, cut + 2, tile + 1)

    side_up = remote(rows_at(far_leaving, 0, deep), side_below, 16, cut, tile - 1)
    side_down = remote(rows_at(low, 0, deep), side_above, 17, cut, tile + 1)

    def far_launch():
        pl.semaphore_wait(far_ready, count(far_after))

        @pl.when(has_far_after & has_up)
        def _():
            far_up.start()

        @pl.when(has_far_after & has_down)
        def _():
            far_down.start()

        @pl.when(has_far_after)
        def _():
            far_own.start()

    def leave(plane, j, value):
        leaving[plane, j] = value
        low[plane, j] = pltpu.roll(value, HALO[plane], 0)

    def launch():
        pl.semaphore_wait(ready, count(after))

        @pl.when(has_after & even & has_up)
        def _():
            for copy in to_above:
                copy.start()

        @pl.when(has_after & even & has_down)
        def _():
            for copy in to_below:
                copy.start()

        @pl.when(has_after)
        def _():
            to_own.start()

    def landed():
        for there, copies in (
            (has_after & even & has_up, to_above), (has_after & even & has_down, to_below),
            (has_after, [to_own]),
            (has_far_after & has_up, [far_up]), (has_far_after & has_down, [far_down]),
            (has_far_after, [far_own]),
            (odd & has_after & has_up, [side_up]), (odd & has_after & has_down, [side_down]),
        ):
            @pl.when(there)
            def _():
                for copy in copies:
                    copy.wait_send()

    def natural():
        for has, copies, into, edges, row, at in (
            (has_up, rest_down, from_up, from_up_edge, OWN, OWN + SUB),
            (has_down, rest_up, from_down, from_down_edge, tail - SUB, tail - SUB - 1),
        ):
            @pl.when(has)
            def _():
                for copy in copies:
                    copy.wait_recv()
                for j in range(tiles):
                    for plane in range(planes):
                        rows = pl.ds(row, SUB)
                        state[plane, j, rows, :] = state[plane, j, rows, :] + into[plane, j]
                for j in range(tiles):
                    one = pl.ds(at, 1)
                    state[last, j, one, :] = state[last, j, one, :] + edges[pl.ds(j, 1), :]

        for plane in range(planes):
            for row in range(0, row_count, SUB):
                parts = relaid([state[plane, j, pl.ds(OWN + row, SUB), :] for j in range(tiles)])
                for t in range(tiles):
                    out_ref[plane, pl.ds(row, SUB), pl.ds(t * LANES, LANES)] = parts[t]

    @pl.when(has_after)
    def _():
        for plane, j in each_slab():
            end[plane, j] = restricted(plane, j, OWN, coarse_count)

        @pl.when(has_up)
        def _():
            spill_down.wait_recv()

        @pl.when(has_down)
        def _():
            spill_up.wait_recv()

        for plane, j in each_slab():
            value = (
                end[plane, j]
                + from_up_spill[plane, j]
                + from_down_spill[plane, j, pl.ds(SPILL, SUB), :]
            )
            end[plane, j] = value

    @pl.when(cut == 0)
    def _():
        for plane, j in each_slab():
            leave(plane, j, end[plane, j])
        launch()
        landed()
        pass_rest()

    own = pl.ds(lead, coarse_count)
    c_core = (SUB, 2 * SUB)

    def above(size):
        return pl.ds(lead - size, size)

    def below(size):
        return pl.ds(lead + coarse_count, size)

    def coarse_wave(wide):
        wave(
            c_state, c_held, c_change, coarse_rows, coarse_weights,
            (c_factor_in, c_slope_in, c_weight_in), half, tiles, wide, c_core,
        )

    @pl.when(has_before)
    def _():
        c_wide = pl.ds(SUB // 2, 3 * SUB)
        c_window = pl.ds(SUB, 2 * SUB)
        origin = tile * coarse_count - lead
        c_inside = mask(total_rows // 2, origin + SUB // 2, (3 * SUB, LANES))
        c_factor_in[c_wide, :] = c_inside * (COARSE_STEP / (2.0 * COARSE_SPACING))
        c_inside = mask(total_rows // 2, origin + SUB, (2 * SUB, LANES))
        for j in range(half):
            c_slope_in[j, c_window, :] = c_inside * coarse_rows[3, pl.ds(j, 1), :]
            c_weight_in[j, c_window, :] = c_inside * coarse_rows[4, pl.ds(j, 1), :]
            for row in range(0, 4 * SUB, SUB):
                for plane in range(planes):
                    c_state[plane, j, pl.ds(row, SUB), :] = zero
                for part in range(2):
                    c_change[j, part, pl.ds(row, SUB), :] = zero

        @pl.when(has_up)
        def _():
            start_down.wait_recv()

        @pl.when(has_down)
        def _():
            start_up.wait_recv()

    @pl.when(has_before & even)
    def _():
        @pl.when(has_up)
        def _():
            for plane, j in each_slab():
                c_state[plane, j, above(deep), :] = start_above[plane, j]

        @pl.when(has_down)
        def _():
            for plane, j in each_slab():
                c_state[plane, j, below(deep), :] = start_below[plane, j]

        for plane, j in each_slab():
            c_state[plane, j, own, :] = start[plane, j]
        coarse_wave(c_core)
        for plane, j in each_slab():
            gain[plane, j] = c_state[plane, j, own, :]

        @pl.when(has_after)
        def _():
            for plane, j in each_slab():
                leave(plane, j, end[plane, j] - gain[plane, j])
            launch()

    @pl.when((has_before & even) | jnp.logical_not(has_after))
    def _():
        natural()

    def joined(place):
        @pl.when(has_up)
        def _():
            for copy in to_below:
                copy.wait_recv()
            for plane, j in each_slab():
                size = HALO[plane]
                place(
                    plane, j, above(size),
                    above_in[plane, j, pl.ds(0, size), :]
                    - start_above[plane, j, pl.ds(deep - size, size), :],
                )

        @pl.when(has_down)
        def _():
            for copy in to_above:
                copy.wait_recv()
            for plane, j in each_slab():
                size = HALO[plane]
                place(
                    plane, j, below(size),
                    below_in[plane, j, pl.ds(0, size), :]
                    - start_below[plane, j, pl.ds(0, size), :],
                )

        to_own.wait_recv()
        for plane, j in each_slab():
            place(plane, j, own, arrived[plane, j] - start[plane, j])

    @pl.when(cut == 1)
    def _():
        def place(plane, j, rows, value):
            c_state[plane, j, rows, :] = value

        joined(place)

    @pl.when(has_far_before)
    def _():
        def hold(plane, j, rows, value):
            offset[plane, j, rows, :] = value

        def add(plane, j, rows):
            c_state[plane, j, rows, :] = c_state[plane, j, rows, :] + offset[plane, j, rows, :]

        joined(hold)

        @pl.when(has_up)
        def _():
            far_down.wait_recv()
            for plane, j in each_slab():
                c_state[plane, j, above(FAR), :] = far_above[plane, j]

        @pl.when(has_down)
        def _():
            far_up.wait_recv()
            for plane, j in each_slab():
                c_state[plane, j, below(FAR), :] = far_below[plane, j]

        far_own.wait_recv()
        for plane, j in each_slab():
            c_state[plane, j, own, :] = far_in[plane, j]
        coarse_wave((SUB // 2, 3 * SUB))

        @pl.when(has_up)
        def _():
            for plane, j in each_slab():
                add(plane, j, above(HALO[plane]))

        @pl.when(has_down)
        def _():
            for plane, j in each_slab():
                add(plane, j, below(HALO[plane]))

        for plane, j in each_slab():
            add(plane, j, own)

    @pl.when(odd)
    def _():
        coarse_wave(c_core)
        for plane, j in each_slab():
            gain[plane, j] = c_state[plane, j, own, :]

        @pl.when(has_after)
        def _():
            for plane, j in each_slab():
                value = gain[plane, j] + end[plane, j]
                far_leaving[plane, j] = value
                far_low[plane, j] = pltpu.roll(value, FAR, 0)
                low[plane, j] = pltpu.roll(value, deep, 0)
                c_state[plane, j, own, :] = value
            far_launch()

            @pl.when(has_up)
            def _():
                side_up.start()

            @pl.when(has_down)
            def _():
                side_down.start()

            @pl.when(has_up)
            def _():
                side_down.wait_recv()
                for plane, j in each_slab():
                    c_state[plane, j, above(deep), :] = side_above[plane, j]

            @pl.when(has_down)
            def _():
                side_up.wait_recv()
                for plane, j in each_slab():
                    c_state[plane, j, below(deep), :] = side_below[plane, j]

            coarse_wave(c_core)
            for plane, j in each_slab():
                leaving[plane, j] = c_state[plane, j, own, :]
            launch()

    @pl.when(has_after & ((cut == 0) | odd))
    def _():
        natural()

    @pl.when(has_before & even)
    def _():
        to_own.wait_recv()
        for plane, j in each_slab():
            gain[plane, j] = arrived[plane, j] - gain[plane, j]

    @pl.when(has_before)
    def _():
        for plane in range(planes):
            parts = relaid([gain[plane, j // 2] for j in range(tiles)])
            for t in range(tiles):
                for r in range(2):
                    spread[plane, t, pl.ds(r, coarse_count, stride=2), :] = parts[t]
            for t in range(tiles):
                at = (plane, slice(None), pl.ds(t * LANES, LANES))
                out_ref[at] = out_ref[at] + spread[plane, t]

    pl.when(has_before)(landed)
    for there, copies in (
        (has_up, rest_up), (has_down, rest_down),
        (has_after & has_up, [spill_up]), (has_after & has_down, [spill_down]),
        (has_before & has_up, [start_up]), (has_before & has_down, [start_down]),
    ):
        @pl.when(there)
        def _():
            for copy in copies:
                copy.wait_send()


def per_device(tile_count, slices, start_states):
    fields = start_states[0]
    planes, row_count, columns = fields.shape
    tiles = columns // LANES
    half = tiles // 2
    fine = line_tables(tiles, tiles, 1.0, columns, FINE_SPACING, FINE_STEP)
    coarse = line_tables(half, tiles, 2.0, columns, COARSE_SPACING, COARSE_STEP)
    fine_count = row_count + 4 * SUB
    coarse_count = row_count // 2
    c_count = coarse_count + 3 * SUB
    f32 = jnp.float32

    def vmem(*shape):
        return pltpu.VMEM(shape, f32)

    slab = vmem(planes, half, coarse_count, LANES)
    out = pl.pallas_call(
        functools.partial(kernel, tile_count, slices),
        out_shape=jax.ShapeDtypeStruct(fields.shape, f32),
        in_specs=[pl.BlockSpec(memory_space=pltpu.HBM)] * 5,
        out_specs=pl.BlockSpec(memory_space=pltpu.VMEM),
        scratch_shapes=[vmem(*fields.shape)]
        + [pltpu.VMEM(a.shape, a.dtype) for a in fine + coarse]
        + [vmem(tiles, LANES)] * 4
        + [
            vmem(planes, tiles, fine_count, LANES),
            vmem(tiles, 2 * (row_count + 2 * SUB), LANES),
            vmem(tiles, 2, fine_count, LANES),
        ]
        + [vmem(planes, tiles, SUB, LANES)] * 2
        + [slab] * 3
        + [
            vmem(planes, half, 2 * SUB, LANES),
            vmem(planes, half, c_count, LANES),
            vmem(half, 4 * SUB, LANES),
            vmem(half, 2, c_count, LANES),
            vmem(fine_count, LANES),
            vmem(tiles, fine_count, LANES),
            vmem(tiles, fine_count, LANES),
            vmem(c_count, LANES),
            vmem(half, c_count, LANES),
            vmem(half, c_count, LANES),
            vmem(planes, half, c_count, LANES),
            vmem(planes, tiles, row_count, LANES),
        ]
        + [slab] * 2
        + [vmem(planes, half, HALO[-1], LANES)] * 2
        + [slab] * 10
        + [vmem(planes, half, FAR, LANES)] * 2
        + [vmem(planes, half, HALO[-1], LANES)] * 2
        + [
            pltpu.SemaphoreType.DMA((len(fine + coarse) + planes,)),
            pltpu.SemaphoreType.DMA((18,)),
            pltpu.SemaphoreType.DMA((18,)),
            pltpu.SemaphoreType.REGULAR,
            pltpu.SemaphoreType.REGULAR,
        ],
        compiler_params=pltpu.CompilerParams(
            collective_id=0, has_side_effects=True, vmem_limit_bytes=24 * 1024 * 1024
        ),
    )(*[pltpu.with_memory_space_constraint(jnp.asarray(a), pltpu.HBM) for a in (fields,) + fine + coarse])
    return out[None]


def solution(mesh):
    spec = P("cuts", None, "tile", None)
    body = functools.partial(per_device, mesh.shape["tile"], mesh.shape["cuts"])
    return jax.shard_map(body, mesh=mesh, in_specs=(spec,), out_specs=spec, check_vma=False)
```

```python
import functools

import ml_dtypes
import numpy as np
import jax
import jax.numpy as jnp
from jax import lax
from jax.experimental import pallas as pl
from jax.experimental.pallas import tpu as pltpu
from jax.sharding import PartitionSpec as P

STEPS = 3
FINE_SPACING = 0.05
COARSE_SPACING = 0.1
FINE_STEP = 0.015
COARSE_STEP = 0.045
LANES = 128
SUB = 8
HALO = (2, 2, 3)
OWN = 2 * SUB
SPILL = 5
FAR = 2 * HALO[-1]
MESH = pl.DeviceIdType.MESH


def line_tables(tiles, fine_tiles, stride, length, spacing, step):
    groups = LANES // fine_tiles
    lane = np.arange(LANES)
    chunk = (lane % fine_tiles) * groups + lane // fine_tiles
    columns = tiles * LANES
    centers = (np.arange(columns) + 0.5) * stride
    depth = (0.9 + 0.3 * np.sin(6.0 * np.pi * centers / length)).reshape(LANES, tiles).T
    beta = depth * depth / 3.0
    b = beta / spacing**2
    mid = 1.0 + 2.0 * b
    last = tiles - 1
    inv = np.zeros_like(b)
    cp = np.zeros_like(b)
    for j in range(last):
        inv[j] = 1.0 / (mid[j] - (b[j] * cp[j - 1] if j else 0.0))
        cp[j] = b[j] * inv[j]
    run = np.ones_like(b)
    for j in range(1, tiles):
        run[j] = run[j - 1] * cp[j - 1]
    p = np.zeros_like(b)
    q = np.zeros_like(b)
    q[last] = 1.0
    for j in range(last - 1, -1, -1):
        p[j] = run[j + 1] + cp[j] * p[j + 1]
        q[j] = cp[j] * q[j + 1]
    system = np.zeros((LANES, LANES))
    for k in range(LANES):
        system[k, k] = mid[last, k] - b[last, k] * q[last - 1, k]
        if k:
            system[k, k - 1] = -b[last, k] * p[last - 1, k]
        if k + 1 < LANES:
            system[k, k] -= b[last, k] * p[0, k + 1]
            system[k, k + 1] = -b[last, k] * q[0, k + 1]
    solve = np.linalg.inv(system).T[chunk][:, chunk]
    high = solve.astype(ml_dtypes.bfloat16)
    low = (solve - high.astype(np.float64)).astype(ml_dtypes.bfloat16)
    half = np.concatenate([high, low], axis=1)
    weights = np.concatenate([half, half], axis=0)
    slope = step * depth / (2.0 * spacing)
    weight = beta / (spacing**2 + 4.0 * beta)
    inv[last] = b[last]
    rows = np.stack([inv, cp, run, slope, weight])[:, :, chunk]
    return rows.astype(np.float32), weights


def relaid(tiles):
    tiles = list(tiles)
    lane = lax.broadcasted_iota(jnp.int32, tiles[0].shape, 1)
    bit = 1
    while bit < len(tiles):
        keep = (lane & bit) == 0
        for t in range(len(tiles)):
            if t & bit == 0:
                a, b = tiles[t], tiles[t | bit]
                tiles[t] = jnp.where(keep, a, pltpu.roll(b, bit, 1))
                tiles[t | bit] = jnp.where(keep, pltpu.roll(a, LANES - bit, 1), b)
        bit *= 2
    return tiles


def wave(state, held, change, rows, weights, inside, tiles, fine_tiles, wide, core):
    factor_in, slope_in, weight_in = inside
    h0, hn = wide
    t0, tn = core
    at = pl.ds(t0, tn)

    def lane(x):
        return lax.broadcasted_iota(jnp.int32, x.shape, 1)

    def chunk_before(x):
        wrapped = jnp.where(lane(x) == 0, 0.0, pltpu.roll(x, fine_tiles + 1, 1))
        return jnp.where(lane(x) >= fine_tiles, pltpu.roll(x, fine_tiles, 1), wrapped)

    def chunk_after(x):
        wrapped = jnp.where(lane(x) == LANES - 1, 0.0, pltpu.roll(x, LANES - fine_tiles - 1, 1))
        return jnp.where(
            lane(x) < LANES - fine_tiles, pltpu.roll(x, LANES - fine_tiles, 1), wrapped
        )

    def across(load, j):
        right = load(j + 1) if j + 1 < tiles else chunk_after(load(0))
        left = load(j - 1) if j else chunk_before(load(tiles - 1))
        return right - left

    def table(kind, j):
        return rows[kind, pl.ds(j, 1), :]

    last = tiles - 1
    near = pl.ds(h0, hn)
    factor = factor_in[near, :]
    for j in range(tiles):
        along = across(lambda i: state[1, i, near, :], j)
        down = state[2, j, pl.ds(h0 + 1, hn), :] - state[2, j, pl.ds(h0 - 1, hn), :]
        state[0, j, near, :] = state[0, j, near, :] - factor * (along + down)
    def forcing(part, j):
        if part == 0:
            along = across(lambda i: state[0, i, at, :], j)
            return state[1, j, at, :] - table(3, j) * along
        down = state[0, j, pl.ds(t0 + 1, tn), :] - state[0, j, pl.ds(t0 - 1, tn), :]
        return state[2, j, at, :] - slope_in[j, at, :] * down

    solved = []
    for part in range(2):
        spot = pl.ds(part * tn, tn)
        total = None
        inner = None
        for j in range(last):
            force = forcing(part, j)
            if j == 0:
                inner = force * table(0, j)
                total = inner
            else:
                inner = force * table(0, j) + table(1, j) * inner
                total = total + table(2, j) * inner
            held[j, spot, :] = inner
        edge = forcing(part, last) + table(0, last) * (inner + chunk_after(total))
        high = edge.astype(jnp.bfloat16)
        low = (edge - high.astype(jnp.float32)).astype(jnp.bfloat16)
        solved.append(
            jnp.dot(
                jnp.concatenate([high, low], axis=1),
                weights[...],
                preferred_element_type=jnp.float32,
            )
        )
    for part in range(2):
        spot = pl.ds(part * tn, tn)
        value = solved[part][:, :LANES] + solved[part][:, LANES:]
        before = chunk_before(value)
        for j in range(last, -1, -1):
            if j < last:
                value = held[j, spot, :] + table(2, j + 1) * before + table(1, j) * value
            moved = value - state[1 + part, j, at, :]
            change[j, part, at, :] = moved
            around = change[j, part, pl.ds(t0 + 1, tn), :] + change[j, part, pl.ds(t0 - 1, tn), :]
            state[1 + part, j, at, :] = value + weight_in[j, at, :] * (around - 2.0 * moved)


def kernel(
    tile_count, slices, x_hbm, fine_rows_hbm, fine_weights_hbm, coarse_rows_hbm,
    coarse_weights_hbm, out_ref,
    x_ref, fine_rows, fine_weights, coarse_rows, coarse_weights,
    up_edge, down_edge, from_up_edge, from_down_edge, state, held, change,
    from_up, from_down, up_spill, down_spill, from_up_spill, from_down_spill,
    c_state, c_held, c_change, factor_in, slope_in, weight_in, c_factor_in, c_slope_in,
    c_weight_in, offset, spread, start, low_start, start_above, start_below,
    end, arrived, leaving, low, above_in, below_in, far_in, far_leaving, far_low, gain,
    far_above, far_below, side_above, side_below, halo_up, halo_down, halo_above, halo_below,
    local, send, recv, ready, far_ready,
):
    cut = lax.axis_index("cuts")
    tile = lax.axis_index("tile")
    has_up = tile > 0
    has_down = tile < tile_count - 1
    has_before = cut > 0
    has_after = cut < slices - 1
    odd = cut % 2 == 1
    even = jnp.logical_not(odd)
    has_far_before = odd & (cut > 1)
    has_far_after = odd & (cut < slices - 2)
    planes, row_count, columns = x_ref.shape
    tiles = columns // LANES
    half = tiles // 2
    total_rows = row_count * tile_count
    coarse_count = row_count // 2
    last = planes - 1
    tail = OWN + row_count
    lead = SUB + SUB // 2
    deep = HALO[last]

    pairs = [(fine_rows_hbm, fine_rows)]
    pairs += [(x_hbm.at[plane], x_ref.at[plane]) for plane in range(planes)]
    pairs += [
        (fine_weights_hbm, fine_weights), (coarse_rows_hbm, coarse_rows),
        (coarse_weights_hbm, coarse_weights),
    ]
    loads = [pltpu.make_async_copy(a, b, local.at[i]) for i, (a, b) in enumerate(pairs)]
    for load in loads:
        load.start()

    zero = jnp.zeros((SUB, LANES), jnp.float32)

    def each_slab():
        return [(plane, j) for plane in range(planes) for j in range(half)]

    for plane, j in each_slab():
        from_up_spill[plane, j] = zero
        from_down_spill[plane, j, pl.ds(0, SUB), :] = zero
        from_down_spill[plane, j, pl.ds(SUB, SUB), :] = zero

    barrier = pltpu.get_barrier_semaphore()
    beside = [(has_up, cut, tile - 1), (has_down, cut, tile + 1)]

    def in_cut(there, other):
        return [
            (there, other, tile),
            (there & has_up, other, tile - 1),
            (there & has_down, other, tile + 1),
        ]

    before = in_cut(has_before, cut - 1)
    after = in_cut(has_after, cut + 1)
    far_before = in_cut(has_far_before, cut - 2)
    far_after = in_cut(has_far_after, cut + 2)

    def signal(semaphore, devices):
        for exists, to_cut, to_tile in devices:
            @pl.when(exists)
            def _():
                pl.semaphore_signal(
                    semaphore, inc=1, device_id=(to_cut, to_tile), device_id_type=MESH
                )

    def count(devices):
        return sum(exists.astype(jnp.int32) for exists, _, _ in devices)

    signal(barrier, beside + after + far_after)

    def remote(source, target, which, to_cut, to_tile):
        return pltpu.make_async_remote_copy(
            src_ref=source, dst_ref=target, send_sem=send.at[which], recv_sem=recv.at[which],
            device_id=(to_cut, to_tile), device_id_type=MESH,
        )

    def rows_at(ref, row, count):
        return ref.at[:, :, pl.ds(row, count), :]

    spill_up = remote(
        rows_at(up_spill, 0, SPILL), rows_at(from_down_spill, SUB, SPILL), 0, cut, tile - 1
    )
    spill_down = remote(
        rows_at(down_spill, 0, SPILL), rows_at(from_up_spill, 0, SPILL), 1, cut, tile + 1
    )
    rest_up = [
        remote(rows_at(state, SUB, SUB), from_down, 2, cut, tile - 1),
        remote(up_edge, from_down_edge, 3, cut, tile - 1),
    ]
    rest_down = [
        remote(rows_at(state, tail, SUB), from_up, 4, cut, tile + 1),
        remote(down_edge, from_up_edge, 5, cut, tile + 1),
    ]
    start_up = remote(rows_at(start, 0, deep), start_below, 6, cut, tile - 1)
    start_down = remote(rows_at(low_start, 0, deep), start_above, 7, cut, tile + 1)

    for j in range(tiles):
        for row in (0, SUB, tail, tail + SUB):
            for plane in range(planes):
                state[plane, j, pl.ds(row, SUB), :] = zero
            for part in range(2):
                change[j, part, pl.ds(row, SUB), :] = zero

    def mask(total, origin, shape):
        at = lax.broadcasted_iota(jnp.int32, shape, 0) + origin
        return ((at >= 0) & (at < total)).astype(jnp.float32)

    loads[0].wait()
    inside = mask(total_rows, tile * row_count - SUB, (row_count + 2 * SUB, LANES))
    window = pl.ds(SUB, row_count + 2 * SUB)
    factor_in[window, :] = inside * (FINE_STEP / (2.0 * FINE_SPACING))
    for j in range(tiles):
        slope_in[j, window, :] = inside * fine_rows[3, pl.ds(j, 1), :]
        weight_in[j, window, :] = inside * fine_rows[4, pl.ds(j, 1), :]

    for plane in range(planes):
        loads[1 + plane].wait()
        for row in range(0, row_count, SUB):
            values = x_ref[plane, pl.ds(row, SUB), :]
            parts = relaid([values[:, t * LANES : (t + 1) * LANES] for t in range(tiles)])
            for j in range(tiles):
                state[plane, j, pl.ds(OWN + row, SUB), :] = parts[j]

    def restricted(plane, j, row, count):
        parts = [
            state[plane, 2 * j + k, pl.ds(row + r, count, stride=2), :]
            for r in range(2)
            for k in range(2)
        ]
        return 0.25 * ((parts[0] + parts[1]) + (parts[2] + parts[3]))

    @pl.when(has_before)
    def _():
        for plane, j in each_slab():
            value = restricted(plane, j, OWN, coarse_count)
            start[plane, j] = value
            low_start[plane, j] = pltpu.roll(value, deep, 0)

    pl.semaphore_wait(barrier, count(beside + before + far_before))
    signal(ready, before)
    signal(far_ready, far_before)
    loads[1 + planes].wait()
    inner = (lead, row_count + SUB)
    outer = (SUB, row_count + 2 * SUB)
    for wide, core in ((inner, inner), (inner, outer), (outer, outer)):
        wave(
            state, held, change, fine_rows, fine_weights, (factor_in, slope_in, weight_in),
            tiles, tiles, wide, core,
        )
    for j in range(tiles):
        for row, near, edge in ((SUB - 1, SUB, up_edge), (tail + SUB, tail + SUB - 1, down_edge)):
            value = fine_rows[4, pl.ds(j, 1), :] * change[j, 1, pl.ds(near, 1), :]
            state[last, j, pl.ds(row, 1), :] = value
            edge[pl.ds(j, 1), :] = value

    @pl.when(has_after)
    def _():
        @pl.when(has_up)
        def _():
            for plane, j in each_slab():
                up_spill[plane, j, pl.ds(0, SPILL), :] = restricted(
                    plane, j, OWN - 2 * SPILL, SPILL
                )
            spill_up.start()

        @pl.when(has_down)
        def _():
            for plane, j in each_slab():
                down_spill[plane, j, pl.ds(0, SPILL), :] = restricted(plane, j, tail, SPILL)
            spill_down.start()

    @pl.when(has_before)
    def _():
        @pl.when(has_up)
        def _():
            start_up.start()

        @pl.when(has_down)
        def _():
            start_down.start()

    def pass_rest():
        @pl.when(has_up)
        def _():
            for copy in rest_up:
                copy.start()

        @pl.when(has_down)
        def _():
            for copy in rest_down:
                copy.start()

    pl.when(has_before)(pass_rest)
    for load in loads[2 + planes :]:
        load.wait()

    first_part = (pl.ds(0, last), slice(None), pl.ds(0, HALO[0]))
    last_part = (last, slice(None), pl.ds(0, HALO[last]))
    to_own = remote(leaving, arrived, 8, cut + 1, tile)
    to_above = [
        remote(leaving.at[part], below_in.at[part], 9 + i, cut + 1, tile - 1)
        for i, part in enumerate((first_part, last_part))
    ]
    to_below = [
        remote(low.at[part], above_in.at[part], 11 + i, cut + 1, tile + 1)
        for i, part in enumerate((first_part, last_part))
    ]

    far_own = remote(far_leaving, far_in, 13, cut + 2, tile)
    far_up = remote(rows_at(far_leaving, 0, FAR), far_below, 14, cut + 2, tile - 1)
    far_down = remote(rows_at(far_low, 0, FAR), far_above, 15, cut + 2, tile + 1)

    side_up = remote(rows_at(far_leaving, 0, deep), side_below, 16, cut, tile - 1)
    side_down = remote(rows_at(low, 0, deep), side_above, 17, cut, tile + 1)

    def far_launch():
        pl.semaphore_wait(far_ready, count(far_after))

        @pl.when(has_far_after & has_up)
        def _():
            far_up.start()

        @pl.when(has_far_after & has_down)
        def _():
            far_down.start()

        @pl.when(has_far_after)
        def _():
            far_own.start()

    def leave(plane, j, value):
        leaving[plane, j] = value
        low[plane, j] = pltpu.roll(value, HALO[plane], 0)

    first = cut == 0
    first_own = remote(far_leaving, arrived, 8, cut + 1, tile)
    first_halos = [
        remote(halo_up, halo_above, 18, cut + 1, tile),
        remote(halo_down, halo_below, 19, cut + 1, tile),
    ]

    def launch_edges():
        pl.semaphore_wait(ready, count(after))

        @pl.when(has_after & even & has_up)
        def _():
            for copy in to_above:
                copy.start()

        @pl.when(has_after & even & has_down)
        def _():
            for copy in to_below:
                copy.start()

    def launch():
        launch_edges()

        @pl.when(has_after)
        def _():
            to_own.start()

    def landed():
        for there, copies in (
            (has_after & even & has_up, to_above), (has_after & even & has_down, to_below),
            (has_before & has_after, [to_own]),
            (has_far_after & has_up, [far_up]), (has_far_after & has_down, [far_down]),
            (has_far_after, [far_own]),
            (odd & has_after & has_up, [side_up]), (odd & has_after & has_down, [side_down]),
        ):
            @pl.when(there)
            def _():
                for copy in copies:
                    copy.wait_send()

    def natural():
        for has, copies, into, edges, row, at in (
            (has_up, rest_down, from_up, from_up_edge, OWN, OWN + SUB),
            (has_down, rest_up, from_down, from_down_edge, tail - SUB, tail - SUB - 1),
        ):
            @pl.when(has)
            def _():
                for copy in copies:
                    copy.wait_recv()
                for j in range(tiles):
                    for plane in range(planes):
                        rows = pl.ds(row, SUB)
                        state[plane, j, rows, :] = state[plane, j, rows, :] + into[plane, j]
                for j in range(tiles):
                    one = pl.ds(at, 1)
                    state[last, j, one, :] = state[last, j, one, :] + edges[pl.ds(j, 1), :]

        for plane in range(planes):
            for row in range(0, row_count, SUB):
                parts = relaid([state[plane, j, pl.ds(OWN + row, SUB), :] for j in range(tiles)])
                for t in range(tiles):
                    out_ref[plane, pl.ds(row, SUB), pl.ds(t * LANES, LANES)] = parts[t]

    @pl.when(has_after)
    def _():
        for plane, j in each_slab():
            end[plane, j] = restricted(plane, j, OWN, coarse_count)

        @pl.when(first)
        def _():
            for plane, j in each_slab():
                leave(plane, j, end[plane, j])
                halo_up[plane, j] = restricted(plane, j, OWN - 2 * deep, deep)
                halo_down[plane, j] = restricted(plane, j, tail, deep)
            launch_edges()
            for copy in first_halos:
                copy.start()

        @pl.when(has_up)
        def _():
            spill_down.wait_recv()

        @pl.when(has_down)
        def _():
            spill_up.wait_recv()

        for plane, j in each_slab():
            value = (
                end[plane, j]
                + from_up_spill[plane, j]
                + from_down_spill[plane, j, pl.ds(SPILL, SUB), :]
            )
            end[plane, j] = value

    @pl.when(cut == 0)
    def _():
        for plane, j in each_slab():
            far_leaving[plane, j] = end[plane, j]
        first_own.start()
        for copy in first_halos + [first_own]:
            copy.wait_send()
        landed()
        pass_rest()

    own = pl.ds(lead, coarse_count)
    c_core = (SUB, 2 * SUB)

    def above(size):
        return pl.ds(lead - size, size)

    def below(size):
        return pl.ds(lead + coarse_count, size)

    def coarse_wave(wide):
        wave(
            c_state, c_held, c_change, coarse_rows, coarse_weights,
            (c_factor_in, c_slope_in, c_weight_in), half, tiles, wide, c_core,
        )

    @pl.when(has_before)
    def _():
        c_wide = pl.ds(SUB // 2, 3 * SUB)
        c_window = pl.ds(SUB, 2 * SUB)
        origin = tile * coarse_count - lead
        c_inside = mask(total_rows // 2, origin + SUB // 2, (3 * SUB, LANES))
        c_factor_in[c_wide, :] = c_inside * (COARSE_STEP / (2.0 * COARSE_SPACING))
        c_inside = mask(total_rows // 2, origin + SUB, (2 * SUB, LANES))
        for j in range(half):
            c_slope_in[j, c_window, :] = c_inside * coarse_rows[3, pl.ds(j, 1), :]
            c_weight_in[j, c_window, :] = c_inside * coarse_rows[4, pl.ds(j, 1), :]
            for row in range(0, 4 * SUB, SUB):
                for plane in range(planes):
                    c_state[plane, j, pl.ds(row, SUB), :] = zero
                for part in range(2):
                    c_change[j, part, pl.ds(row, SUB), :] = zero

        @pl.when(has_up)
        def _():
            start_down.wait_recv()

        @pl.when(has_down)
        def _():
            start_up.wait_recv()

    @pl.when(has_before & even)
    def _():
        @pl.when(has_up)
        def _():
            for plane, j in each_slab():
                c_state[plane, j, above(deep), :] = start_above[plane, j]

        @pl.when(has_down)
        def _():
            for plane, j in each_slab():
                c_state[plane, j, below(deep), :] = start_below[plane, j]

        for plane, j in each_slab():
            c_state[plane, j, own, :] = start[plane, j]
        coarse_wave(c_core)
        for plane, j in each_slab():
            gain[plane, j] = c_state[plane, j, own, :]

        @pl.when(has_after)
        def _():
            for plane, j in each_slab():
                leave(plane, j, end[plane, j] - gain[plane, j])
            launch()

    @pl.when((has_before & even) | jnp.logical_not(has_after))
    def _():
        natural()

    def joined(place, extra_above=lambda: None, extra_below=lambda: None):
        @pl.when(has_up)
        def _():
            for copy in to_below:
                copy.wait_recv()
            for plane, j in each_slab():
                size = HALO[plane]
                place(
                    plane, j, above(size),
                    above_in[plane, j, pl.ds(0, size), :]
                    - start_above[plane, j, pl.ds(deep - size, size), :],
                )
            extra_above()

        @pl.when(has_down)
        def _():
            for copy in to_above:
                copy.wait_recv()
            for plane, j in each_slab():
                size = HALO[plane]
                place(
                    plane, j, below(size),
                    below_in[plane, j, pl.ds(0, size), :]
                    - start_below[plane, j, pl.ds(0, size), :],
                )
            extra_below()

        to_own.wait_recv()
        for plane, j in each_slab():
            place(plane, j, own, arrived[plane, j] - start[plane, j])

    @pl.when(cut == 1)
    def _():
        def place(plane, j, rows, value):
            c_state[plane, j, rows, :] = value

        def widen(rows, halo, skip):
            for plane, j in each_slab():
                count = HALO[plane]
                at = rows(count)
                c_state[plane, j, at, :] = (
                    c_state[plane, j, at, :] + halo[plane, j, pl.ds(skip(count), count), :]
                )

        for copy in first_halos:
            copy.wait_recv()
        joined(place, lambda: (
            widen(above, halo_above, lambda count: deep - count),
        ), lambda: (
            widen(below, halo_below, lambda count: 0),
        ))

    @pl.when(has_far_before)
    def _():
        def hold(plane, j, rows, value):
            offset[plane, j, rows, :] = value

        def add(plane, j, rows):
            c_state[plane, j, rows, :] = c_state[plane, j, rows, :] + offset[plane, j, rows, :]

        joined(hold)

        @pl.when(has_up)
        def _():
            far_down.wait_recv()
            for plane, j in each_slab():
                c_state[plane, j, above(FAR), :] = far_above[plane, j]

        @pl.when(has_down)
        def _():
            far_up.wait_recv()
            for plane, j in each_slab():
                c_state[plane, j, below(FAR), :] = far_below[plane, j]

        far_own.wait_recv()
        for plane, j in each_slab():
            c_state[plane, j, own, :] = far_in[plane, j]
        coarse_wave((SUB // 2, 3 * SUB))

        @pl.when(has_up)
        def _():
            for plane, j in each_slab():
                add(plane, j, above(HALO[plane]))

        @pl.when(has_down)
        def _():
            for plane, j in each_slab():
                add(plane, j, below(HALO[plane]))

        for plane, j in each_slab():
            add(plane, j, own)

    @pl.when(odd)
    def _():
        coarse_wave(c_core)
        for plane, j in each_slab():
            gain[plane, j] = c_state[plane, j, own, :]

        @pl.when(has_after)
        def _():
            for plane, j in each_slab():
                value = gain[plane, j] + end[plane, j]
                far_leaving[plane, j] = value
                far_low[plane, j] = pltpu.roll(value, FAR, 0)
                low[plane, j] = pltpu.roll(value, deep, 0)
                c_state[plane, j, own, :] = value
            far_launch()

            @pl.when(has_up)
            def _():
                side_up.start()

            @pl.when(has_down)
            def _():
                side_down.start()

            @pl.when(has_up)
            def _():
                side_down.wait_recv()
                for plane, j in each_slab():
                    c_state[plane, j, above(deep), :] = side_above[plane, j]

            @pl.when(has_down)
            def _():
                side_up.wait_recv()
                for plane, j in each_slab():
                    c_state[plane, j, below(deep), :] = side_below[plane, j]

            coarse_wave(c_core)
            for plane, j in each_slab():
                leaving[plane, j] = c_state[plane, j, own, :]
            launch()

    @pl.when(has_after & ((cut == 0) | odd))
    def _():
        natural()

    @pl.when(has_before & even)
    def _():
        to_own.wait_recv()
        for plane, j in each_slab():
            gain[plane, j] = arrived[plane, j] - gain[plane, j]

    @pl.when(has_before)
    def _():
        for plane in range(planes):
            parts = relaid([gain[plane, j // 2] for j in range(tiles)])
            for t in range(tiles):
                for r in range(2):
                    spread[plane, t, pl.ds(r, coarse_count, stride=2), :] = parts[t]
            for t in range(tiles):
                at = (plane, slice(None), pl.ds(t * LANES, LANES))
                out_ref[at] = out_ref[at] + spread[plane, t]

    pl.when(has_before)(landed)
    for there, copies in (
        (has_up, rest_up), (has_down, rest_down),
        (has_after & has_up, [spill_up]), (has_after & has_down, [spill_down]),
        (has_before & has_up, [start_up]), (has_before & has_down, [start_down]),
    ):
        @pl.when(there)
        def _():
            for copy in copies:
                copy.wait_send()


def per_device(tile_count, slices, start_states):
    fields = start_states[0]
    planes, row_count, columns = fields.shape
    tiles = columns // LANES
    half = tiles // 2
    fine = line_tables(tiles, tiles, 1.0, columns, FINE_SPACING, FINE_STEP)
    coarse = line_tables(half, tiles, 2.0, columns, COARSE_SPACING, COARSE_STEP)
    fine_count = row_count + 4 * SUB
    coarse_count = row_count // 2
    c_count = coarse_count + 3 * SUB
    f32 = jnp.float32

    def vmem(*shape):
        return pltpu.VMEM(shape, f32)

    slab = vmem(planes, half, coarse_count, LANES)
    out = pl.pallas_call(
        functools.partial(kernel, tile_count, slices),
        out_shape=jax.ShapeDtypeStruct(fields.shape, f32),
        in_specs=[pl.BlockSpec(memory_space=pltpu.HBM)] * 5,
        out_specs=pl.BlockSpec(memory_space=pltpu.VMEM),
        scratch_shapes=[vmem(*fields.shape)]
        + [pltpu.VMEM(a.shape, a.dtype) for a in fine + coarse]
        + [vmem(tiles, LANES)] * 4
        + [
            vmem(planes, tiles, fine_count, LANES),
            vmem(tiles, 2 * (row_count + 2 * SUB), LANES),
            vmem(tiles, 2, fine_count, LANES),
        ]
        + [vmem(planes, tiles, SUB, LANES)] * 2
        + [slab] * 3
        + [
            vmem(planes, half, 2 * SUB, LANES),
            vmem(planes, half, c_count, LANES),
            vmem(half, 4 * SUB, LANES),
            vmem(half, 2, c_count, LANES),
            vmem(fine_count, LANES),
            vmem(tiles, fine_count, LANES),
            vmem(tiles, fine_count, LANES),
            vmem(c_count, LANES),
            vmem(half, c_count, LANES),
            vmem(half, c_count, LANES),
            vmem(planes, half, c_count, LANES),
            vmem(planes, tiles, row_count, LANES),
        ]
        + [slab] * 2
        + [vmem(planes, half, HALO[-1], LANES)] * 2
        + [slab] * 10
        + [vmem(planes, half, FAR, LANES)] * 2
        + [vmem(planes, half, HALO[-1], LANES)] * 6
        + [
            pltpu.SemaphoreType.DMA((len(fine + coarse) + planes,)),
            pltpu.SemaphoreType.DMA((20,)),
            pltpu.SemaphoreType.DMA((20,)),
            pltpu.SemaphoreType.REGULAR,
            pltpu.SemaphoreType.REGULAR,
        ],
        compiler_params=pltpu.CompilerParams(
            collective_id=0, has_side_effects=True, vmem_limit_bytes=24 * 1024 * 1024
        ),
    )(*[pltpu.with_memory_space_constraint(jnp.asarray(a), pltpu.HBM) for a in (fields,) + fine + coarse])
    return out[None]


def solution(mesh):
    spec = P("cuts", None, "tile", None)
    body = functools.partial(per_device, mesh.shape["tile"], mesh.shape["cuts"])
    return jax.shard_map(body, mesh=mesh, in_specs=(spec,), out_specs=spec, check_vma=False)
```

```python
import functools

import ml_dtypes
import numpy as np
import jax
import jax.numpy as jnp
from jax import lax
from jax.experimental import pallas as pl
from jax.experimental.pallas import tpu as pltpu
from jax.sharding import PartitionSpec as P

STEPS = 3
FINE_SPACING = 0.05
COARSE_SPACING = 0.1
FINE_STEP = 0.015
COARSE_STEP = 0.045
LANES = 128
SUB = 8
HALO = (2, 2, 3)
OWN = 2 * SUB
SPILL = 5
FAR = 2 * HALO[-1]
MESH = pl.DeviceIdType.MESH


def line_tables(tiles, fine_tiles, stride, length, spacing, step):
    groups = LANES // fine_tiles
    lane = np.arange(LANES)
    chunk = (lane % fine_tiles) * groups + lane // fine_tiles
    columns = tiles * LANES
    centers = (np.arange(columns) + 0.5) * stride
    depth = (0.9 + 0.3 * np.sin(6.0 * np.pi * centers / length)).reshape(LANES, tiles).T
    beta = depth * depth / 3.0
    b = beta / spacing**2
    mid = 1.0 + 2.0 * b
    last = tiles - 1
    inv = np.zeros_like(b)
    cp = np.zeros_like(b)
    for j in range(last):
        inv[j] = 1.0 / (mid[j] - (b[j] * cp[j - 1] if j else 0.0))
        cp[j] = b[j] * inv[j]
    run = np.ones_like(b)
    for j in range(1, tiles):
        run[j] = run[j - 1] * cp[j - 1]
    p = np.zeros_like(b)
    q = np.zeros_like(b)
    q[last] = 1.0
    for j in range(last - 1, -1, -1):
        p[j] = run[j + 1] + cp[j] * p[j + 1]
        q[j] = cp[j] * q[j + 1]
    system = np.zeros((LANES, LANES))
    for k in range(LANES):
        system[k, k] = mid[last, k] - b[last, k] * q[last - 1, k]
        if k:
            system[k, k - 1] = -b[last, k] * p[last - 1, k]
        if k + 1 < LANES:
            system[k, k] -= b[last, k] * p[0, k + 1]
            system[k, k + 1] = -b[last, k] * q[0, k + 1]
    solve = np.linalg.inv(system).T[chunk][:, chunk]
    high = solve.astype(ml_dtypes.bfloat16)
    low = (solve - high.astype(np.float64)).astype(ml_dtypes.bfloat16)
    half = np.concatenate([high, low], axis=1)
    weights = np.concatenate([half, half], axis=0)
    slope = step * depth / (2.0 * spacing)
    weight = beta / (spacing**2 + 4.0 * beta)
    inv[last] = b[last]
    rows = np.stack([inv, cp, run, slope, weight])[:, :, chunk]
    return rows.astype(np.float32), weights


def relaid(tiles):
    tiles = list(tiles)
    lane = lax.broadcasted_iota(jnp.int32, tiles[0].shape, 1)
    bit = 1
    while bit < len(tiles):
        keep = (lane & bit) == 0
        for t in range(len(tiles)):
            if t & bit == 0:
                a, b = tiles[t], tiles[t | bit]
                tiles[t] = jnp.where(keep, a, pltpu.roll(b, bit, 1))
                tiles[t | bit] = jnp.where(keep, pltpu.roll(a, LANES - bit, 1), b)
        bit *= 2
    return tiles


def wave(state, held, change, rows, weights, inside, tiles, fine_tiles, wide, core):
    factor_in, slope_in, weight_in = inside
    h0, hn = wide
    t0, tn = core
    at = pl.ds(t0, tn)

    def lane(x):
        return lax.broadcasted_iota(jnp.int32, x.shape, 1)

    def chunk_before(x):
        wrapped = jnp.where(lane(x) == 0, 0.0, pltpu.roll(x, fine_tiles + 1, 1))
        return jnp.where(lane(x) >= fine_tiles, pltpu.roll(x, fine_tiles, 1), wrapped)

    def chunk_after(x):
        wrapped = jnp.where(lane(x) == LANES - 1, 0.0, pltpu.roll(x, LANES - fine_tiles - 1, 1))
        return jnp.where(
            lane(x) < LANES - fine_tiles, pltpu.roll(x, LANES - fine_tiles, 1), wrapped
        )

    def across(load, j):
        right = load(j + 1) if j + 1 < tiles else chunk_after(load(0))
        left = load(j - 1) if j else chunk_before(load(tiles - 1))
        return right - left

    def table(kind, j):
        return rows[kind, pl.ds(j, 1), :]

    last = tiles - 1
    near = pl.ds(h0, hn)
    factor = factor_in[near, :]
    for j in range(tiles):
        along = across(lambda i: state[1, i, near, :], j)
        down = state[2, j, pl.ds(h0 + 1, hn), :] - state[2, j, pl.ds(h0 - 1, hn), :]
        state[0, j, near, :] = state[0, j, near, :] - factor * (along + down)
    def forcing(part, j):
        if part == 0:
            along = across(lambda i: state[0, i, at, :], j)
            return state[1, j, at, :] - table(3, j) * along
        down = state[0, j, pl.ds(t0 + 1, tn), :] - state[0, j, pl.ds(t0 - 1, tn), :]
        return state[2, j, at, :] - slope_in[j, at, :] * down

    solved = []
    for part in range(2):
        spot = pl.ds(part * tn, tn)
        total = None
        inner = None
        for j in range(last):
            force = forcing(part, j)
            if j == 0:
                inner = force * table(0, j)
                total = inner
            else:
                inner = force * table(0, j) + table(1, j) * inner
                total = total + table(2, j) * inner
            held[j, spot, :] = inner
        edge = forcing(part, last) + table(0, last) * (inner + chunk_after(total))
        high = edge.astype(jnp.bfloat16)
        low = (edge - high.astype(jnp.float32)).astype(jnp.bfloat16)
        solved.append(
            jnp.dot(
                jnp.concatenate([high, low], axis=1),
                weights[...],
                preferred_element_type=jnp.float32,
            )
        )
    for part in range(2):
        spot = pl.ds(part * tn, tn)
        value = solved[part][:, :LANES] + solved[part][:, LANES:]
        before = chunk_before(value)
        for j in range(last, -1, -1):
            if j < last:
                value = held[j, spot, :] + table(2, j + 1) * before + table(1, j) * value
            moved = value - state[1 + part, j, at, :]
            change[j, part, at, :] = moved
            around = change[j, part, pl.ds(t0 + 1, tn), :] + change[j, part, pl.ds(t0 - 1, tn), :]
            state[1 + part, j, at, :] = value + weight_in[j, at, :] * (around - 2.0 * moved)


def kernel(
    tile_count, slices, x_hbm, fine_rows_hbm, fine_weights_hbm, coarse_rows_hbm,
    coarse_weights_hbm, out_ref,
    x_ref, fine_rows, fine_weights, coarse_rows, coarse_weights,
    up_edge, down_edge, from_up_edge, from_down_edge, state, held, change,
    from_up, from_down, up_spill, down_spill, from_up_spill, from_down_spill,
    c_state, c_held, c_change, factor_in, slope_in, weight_in, c_factor_in, c_slope_in,
    c_weight_in, offset, spread, start, low_start, start_above, start_below,
    end, arrived, leaving, low, above_in, below_in, far_in, far_leaving, far_low, near_low, gain,
    far_above, far_below, side_above, side_below, halo_up, halo_down, halo_above, halo_below,
    local, send, recv, ready, far_ready,
):
    cut = lax.axis_index("cuts")
    tile = lax.axis_index("tile")
    has_up = tile > 0
    has_down = tile < tile_count - 1
    has_before = cut > 0
    has_after = cut < slices - 1
    odd = cut % 2 == 1
    even = jnp.logical_not(odd)
    has_far_before = odd & (cut > 1)
    has_far_after = odd & (cut < slices - 2)
    planes, row_count, columns = x_ref.shape
    tiles = columns // LANES
    half = tiles // 2
    total_rows = row_count * tile_count
    coarse_count = row_count // 2
    last = planes - 1
    tail = OWN + row_count
    lead = SUB + SUB // 2
    deep = HALO[last]

    pairs = [(fine_rows_hbm, fine_rows)]
    pairs += [(x_hbm.at[plane], x_ref.at[plane]) for plane in range(planes)]
    pairs += [
        (fine_weights_hbm, fine_weights), (coarse_rows_hbm, coarse_rows),
        (coarse_weights_hbm, coarse_weights),
    ]
    loads = [pltpu.make_async_copy(a, b, local.at[i]) for i, (a, b) in enumerate(pairs)]
    for load in loads:
        load.start()

    zero = jnp.zeros((SUB, LANES), jnp.float32)

    def each_slab():
        return [(plane, j) for plane in range(planes) for j in range(half)]

    for plane, j in each_slab():
        from_up_spill[plane, j] = zero
        from_down_spill[plane, j, pl.ds(0, SUB), :] = zero
        from_down_spill[plane, j, pl.ds(SUB, SUB), :] = zero

    right = tile % 2 == 1
    left = jnp.logical_not(right)
    pair_up, pair_down = has_up & right, has_down & left
    cross_up, cross_down = has_up & left, has_down & right

    barrier = pltpu.get_barrier_semaphore()
    beside = [(has_up, cut, tile - 1), (has_down, cut, tile + 1)]

    def in_cut(there, other):
        return [
            (there, other, tile),
            (there & has_up, other, tile - 1),
            (there & has_down, other, tile + 1),
        ]

    before = in_cut(has_before, cut - 1)
    after = in_cut(has_after, cut + 1)
    far_before = in_cut(has_far_before, cut - 2)
    far_after = in_cut(has_far_after, cut + 2)

    def signal(semaphore, devices):
        for exists, to_cut, to_tile in devices:
            @pl.when(exists)
            def _():
                pl.semaphore_signal(
                    semaphore, inc=1, device_id=(to_cut, to_tile), device_id_type=MESH
                )

    def count(devices):
        return sum(exists.astype(jnp.int32) for exists, _, _ in devices)

    signal(barrier, beside + after + far_after)

    def remote(source, target, which, to_cut, to_tile):
        return pltpu.make_async_remote_copy(
            src_ref=source, dst_ref=target, send_sem=send.at[which], recv_sem=recv.at[which],
            device_id=(to_cut, to_tile), device_id_type=MESH,
        )

    def rows_at(ref, row, count):
        return ref.at[:, :, pl.ds(row, count), :]

    spill_up = remote(
        rows_at(up_spill, 0, SPILL), rows_at(from_down_spill, SUB, SPILL), 0, cut, tile - 1
    )
    spill_down = remote(
        rows_at(down_spill, 0, SPILL), rows_at(from_up_spill, 0, SPILL), 1, cut, tile + 1
    )
    rest_up = [
        remote(rows_at(state, SUB, SUB), from_down, 2, cut, tile - 1),
        remote(up_edge, from_down_edge, 3, cut, tile - 1),
    ]
    rest_down = [
        remote(rows_at(state, tail, SUB), from_up, 4, cut, tile + 1),
        remote(down_edge, from_up_edge, 5, cut, tile + 1),
    ]
    start_up = remote(rows_at(start, 0, deep), start_below, 6, cut, tile - 1)
    start_down = remote(rows_at(low_start, 0, deep), start_above, 7, cut, tile + 1)

    for j in range(tiles):
        for row in (0, SUB, tail, tail + SUB):
            for plane in range(planes):
                state[plane, j, pl.ds(row, SUB), :] = zero
            for part in range(2):
                change[j, part, pl.ds(row, SUB), :] = zero

    def mask(total, origin, shape):
        at = lax.broadcasted_iota(jnp.int32, shape, 0) + origin
        return ((at >= 0) & (at < total)).astype(jnp.float32)

    loads[0].wait()
    inside = mask(total_rows, tile * row_count - SUB, (row_count + 2 * SUB, LANES))
    window = pl.ds(SUB, row_count + 2 * SUB)
    factor_in[window, :] = inside * (FINE_STEP / (2.0 * FINE_SPACING))
    for j in range(tiles):
        slope_in[j, window, :] = inside * fine_rows[3, pl.ds(j, 1), :]
        weight_in[j, window, :] = inside * fine_rows[4, pl.ds(j, 1), :]

    for plane in range(planes):
        loads[1 + plane].wait()
        for row in range(0, row_count, SUB):
            values = x_ref[plane, pl.ds(row, SUB), :]
            parts = relaid([values[:, t * LANES : (t + 1) * LANES] for t in range(tiles)])
            for j in range(tiles):
                state[plane, j, pl.ds(OWN + row, SUB), :] = parts[j]

    def restricted(plane, j, row, count):
        parts = [
            state[plane, 2 * j + k, pl.ds(row + r, count, stride=2), :]
            for r in range(2)
            for k in range(2)
        ]
        return 0.25 * ((parts[0] + parts[1]) + (parts[2] + parts[3]))

    @pl.when(has_before)
    def _():
        for plane, j in each_slab():
            value = restricted(plane, j, OWN, coarse_count)
            start[plane, j] = value
            low_start[plane, j] = pltpu.roll(value, deep, 0)

    pl.semaphore_wait(barrier, count(beside + before + far_before))
    signal(ready, before)
    signal(far_ready, far_before)
    loads[1 + planes].wait()
    inner = (lead, row_count + SUB)
    outer = (SUB, row_count + 2 * SUB)
    for wide, core in ((inner, inner), (inner, outer), (outer, outer)):
        wave(
            state, held, change, fine_rows, fine_weights, (factor_in, slope_in, weight_in),
            tiles, tiles, wide, core,
        )
    for j in range(tiles):
        for row, near, edge in ((SUB - 1, SUB, up_edge), (tail + SUB, tail + SUB - 1, down_edge)):
            value = fine_rows[4, pl.ds(j, 1), :] * change[j, 1, pl.ds(near, 1), :]
            state[last, j, pl.ds(row, 1), :] = value
            edge[pl.ds(j, 1), :] = value

    @pl.when(has_after)
    def _():
        @pl.when(has_up)
        def _():
            for plane, j in each_slab():
                up_spill[plane, j, pl.ds(0, SPILL), :] = restricted(
                    plane, j, OWN - 2 * SPILL, SPILL
                )
            spill_up.start()

        @pl.when(has_down)
        def _():
            for plane, j in each_slab():
                down_spill[plane, j, pl.ds(0, SPILL), :] = restricted(plane, j, tail, SPILL)
            spill_down.start()

    @pl.when(has_before)
    def _():
        @pl.when(has_up)
        def _():
            start_up.start()

        @pl.when(has_down)
        def _():
            start_down.start()

    def pass_rest():
        @pl.when(has_up)
        def _():
            for copy in rest_up:
                copy.start()

        @pl.when(has_down)
        def _():
            for copy in rest_down:
                copy.start()

    pl.when(has_before)(pass_rest)
    for load in loads[2 + planes :]:
        load.wait()

    first_part = (pl.ds(0, last), slice(None), pl.ds(0, HALO[0]))
    last_part = (last, slice(None), pl.ds(0, HALO[last]))
    to_own = remote(leaving, arrived, 8, cut + 1, tile)
    to_above = [
        remote(leaving.at[part], below_in.at[part], 9 + i, cut + 1, tile - 1)
        for i, part in enumerate((first_part, last_part))
    ]
    to_below = [
        remote(low.at[part], above_in.at[part], 11 + i, cut + 1, tile + 1)
        for i, part in enumerate((first_part, last_part))
    ]

    far_own = remote(far_leaving, far_in, 13, cut + 2, tile)
    far_up = remote(rows_at(far_leaving, 0, FAR), far_below, 14, cut + 2, tile - 1)
    far_down = remote(rows_at(far_low, 0, FAR), far_above, 15, cut + 2, tile + 1)

    near_up = remote(rows_at(far_in, 0, FAR), far_below, 20, cut, tile - 1)
    near_down = remote(rows_at(near_low, 0, FAR), far_above, 21, cut, tile + 1)
    side_up = remote(rows_at(far_leaving, 0, deep), side_below, 16, cut, tile - 1)
    side_down = remote(rows_at(low, 0, deep), side_above, 17, cut, tile + 1)

    def far_launch():
        pl.semaphore_wait(far_ready, count(far_after))

        @pl.when(has_far_after & cross_up)
        def _():
            far_up.start()

        @pl.when(has_far_after & cross_down)
        def _():
            far_down.start()

        @pl.when(has_far_after)
        def _():
            far_own.start()

    def leave(plane, j, value):
        leaving[plane, j] = value
        low[plane, j] = pltpu.roll(value, HALO[plane], 0)

    first = cut == 0
    first_own = remote(far_leaving, arrived, 8, cut + 1, tile)
    first_halos = [
        remote(halo_up, halo_above, 18, cut + 1, tile),
        remote(halo_down, halo_below, 19, cut + 1, tile),
    ]

    def launch_edges():
        pl.semaphore_wait(ready, count(after))

        @pl.when(has_after & even & has_up)
        def _():
            for copy in to_above:
                copy.start()

        @pl.when(has_after & even & has_down)
        def _():
            for copy in to_below:
                copy.start()

    def launch():
        launch_edges()

        @pl.when(has_after)
        def _():
            to_own.start()

    def landed():
        for there, copies in (
            (has_after & even & has_up, to_above), (has_after & even & has_down, to_below),
            (has_before & has_after, [to_own]),
            (has_far_after & cross_up, [far_up]), (has_far_after & cross_down, [far_down]),
            (has_far_before & pair_up, [near_up]), (has_far_before & pair_down, [near_down]),
            (has_far_after, [far_own]),
            (odd & has_after & has_up, [side_up]), (odd & has_after & has_down, [side_down]),
        ):
            @pl.when(there)
            def _():
                for copy in copies:
                    copy.wait_send()

    def natural():
        for has, copies, into, edges, row, at in (
            (has_up, rest_down, from_up, from_up_edge, OWN, OWN + SUB),
            (has_down, rest_up, from_down, from_down_edge, tail - SUB, tail - SUB - 1),
        ):
            @pl.when(has)
            def _():
                for copy in copies:
                    copy.wait_recv()
                for j in range(tiles):
                    for plane in range(planes):
                        rows = pl.ds(row, SUB)
                        state[plane, j, rows, :] = state[plane, j, rows, :] + into[plane, j]
                for j in range(tiles):
                    one = pl.ds(at, 1)
                    state[last, j, one, :] = state[last, j, one, :] + edges[pl.ds(j, 1), :]

        for plane in range(planes):
            for row in range(0, row_count, SUB):
                parts = relaid([state[plane, j, pl.ds(OWN + row, SUB), :] for j in range(tiles)])
                for t in range(tiles):
                    out_ref[plane, pl.ds(row, SUB), pl.ds(t * LANES, LANES)] = parts[t]

    @pl.when(has_after)
    def _():
        for plane, j in each_slab():
            end[plane, j] = restricted(plane, j, OWN, coarse_count)

        @pl.when(first)
        def _():
            for plane, j in each_slab():
                leave(plane, j, end[plane, j])
                halo_up[plane, j] = restricted(plane, j, OWN - 2 * deep, deep)
                halo_down[plane, j] = restricted(plane, j, tail, deep)
            launch_edges()
            for copy in first_halos:
                copy.start()

        @pl.when(has_up)
        def _():
            spill_down.wait_recv()

        @pl.when(has_down)
        def _():
            spill_up.wait_recv()

        for plane, j in each_slab():
            value = (
                end[plane, j]
                + from_up_spill[plane, j]
                + from_down_spill[plane, j, pl.ds(SPILL, SUB), :]
            )
            end[plane, j] = value

    @pl.when(cut == 0)
    def _():
        for plane, j in each_slab():
            far_leaving[plane, j] = end[plane, j]
        first_own.start()
        for copy in first_halos + [first_own]:
            copy.wait_send()
        landed()
        pass_rest()

    own = pl.ds(lead, coarse_count)
    c_core = (SUB, 2 * SUB)

    def above(size):
        return pl.ds(lead - size, size)

    def below(size):
        return pl.ds(lead + coarse_count, size)

    def coarse_wave(wide):
        wave(
            c_state, c_held, c_change, coarse_rows, coarse_weights,
            (c_factor_in, c_slope_in, c_weight_in), half, tiles, wide, c_core,
        )

    @pl.when(has_before)
    def _():
        c_wide = pl.ds(SUB // 2, 3 * SUB)
        c_window = pl.ds(SUB, 2 * SUB)
        origin = tile * coarse_count - lead
        c_inside = mask(total_rows // 2, origin + SUB // 2, (3 * SUB, LANES))
        c_factor_in[c_wide, :] = c_inside * (COARSE_STEP / (2.0 * COARSE_SPACING))
        c_inside = mask(total_rows // 2, origin + SUB, (2 * SUB, LANES))
        for j in range(half):
            c_slope_in[j, c_window, :] = c_inside * coarse_rows[3, pl.ds(j, 1), :]
            c_weight_in[j, c_window, :] = c_inside * coarse_rows[4, pl.ds(j, 1), :]
            for row in range(0, 4 * SUB, SUB):
                for plane in range(planes):
                    c_state[plane, j, pl.ds(row, SUB), :] = zero
                for part in range(2):
                    c_change[j, part, pl.ds(row, SUB), :] = zero

        @pl.when(has_up)
        def _():
            start_down.wait_recv()

        @pl.when(has_down)
        def _():
            start_up.wait_recv()

    @pl.when(has_before & even)
    def _():
        @pl.when(has_up)
        def _():
            for plane, j in each_slab():
                c_state[plane, j, above(deep), :] = start_above[plane, j]

        @pl.when(has_down)
        def _():
            for plane, j in each_slab():
                c_state[plane, j, below(deep), :] = start_below[plane, j]

        for plane, j in each_slab():
            c_state[plane, j, own, :] = start[plane, j]
        coarse_wave(c_core)
        for plane, j in each_slab():
            gain[plane, j] = c_state[plane, j, own, :]

        @pl.when(has_after)
        def _():
            for plane, j in each_slab():
                leave(plane, j, end[plane, j] - gain[plane, j])
            launch()

    @pl.when((has_before & even) | jnp.logical_not(has_after))
    def _():
        natural()

    def joined(place, extra_above=lambda: None, extra_below=lambda: None):
        @pl.when(has_up)
        def _():
            for copy in to_below:
                copy.wait_recv()
            for plane, j in each_slab():
                size = HALO[plane]
                place(
                    plane, j, above(size),
                    above_in[plane, j, pl.ds(0, size), :]
                    - start_above[plane, j, pl.ds(deep - size, size), :],
                )
            extra_above()

        @pl.when(has_down)
        def _():
            for copy in to_above:
                copy.wait_recv()
            for plane, j in each_slab():
                size = HALO[plane]
                place(
                    plane, j, below(size),
                    below_in[plane, j, pl.ds(0, size), :]
                    - start_below[plane, j, pl.ds(0, size), :],
                )
            extra_below()

        to_own.wait_recv()
        for plane, j in each_slab():
            place(plane, j, own, arrived[plane, j] - start[plane, j])

    @pl.when(cut == 1)
    def _():
        def place(plane, j, rows, value):
            c_state[plane, j, rows, :] = value

        def widen(rows, halo, skip):
            for plane, j in each_slab():
                count = HALO[plane]
                at = rows(count)
                c_state[plane, j, at, :] = (
                    c_state[plane, j, at, :] + halo[plane, j, pl.ds(skip(count), count), :]
                )

        for copy in first_halos:
            copy.wait_recv()
        joined(place, lambda: (
            widen(above, halo_above, lambda count: deep - count),
        ), lambda: (
            widen(below, halo_below, lambda count: 0),
        ))

    @pl.when(has_far_before)
    def _():
        def hold(plane, j, rows, value):
            offset[plane, j, rows, :] = value

        def add(plane, j, rows):
            c_state[plane, j, rows, :] = c_state[plane, j, rows, :] + offset[plane, j, rows, :]

        joined(hold)
        far_own.wait_recv()

        @pl.when(pair_up)
        def _():
            near_up.start()

        @pl.when(pair_down)
        def _():
            for plane, j in each_slab():
                near_low[plane, j] = pltpu.roll(far_in[plane, j], FAR, 0)
            near_down.start()

        for plane, j in each_slab():
            c_state[plane, j, own, :] = far_in[plane, j]

        @pl.when(cross_up)
        def _():
            far_down.wait_recv()

        @pl.when(cross_down)
        def _():
            far_up.wait_recv()

        @pl.when(pair_up)
        def _():
            near_down.wait_recv()

        @pl.when(pair_down)
        def _():
            near_up.wait_recv()

        @pl.when(has_up)
        def _():
            for plane, j in each_slab():
                c_state[plane, j, above(FAR), :] = far_above[plane, j]

        @pl.when(has_down)
        def _():
            for plane, j in each_slab():
                c_state[plane, j, below(FAR), :] = far_below[plane, j]

        coarse_wave((SUB // 2, 3 * SUB))

        @pl.when(has_up)
        def _():
            for plane, j in each_slab():
                add(plane, j, above(HALO[plane]))

        @pl.when(has_down)
        def _():
            for plane, j in each_slab():
                add(plane, j, below(HALO[plane]))

        for plane, j in each_slab():
            add(plane, j, own)

    @pl.when(odd)
    def _():
        coarse_wave(c_core)
        for plane, j in each_slab():
            gain[plane, j] = c_state[plane, j, own, :]

        @pl.when(has_after)
        def _():
            for plane, j in each_slab():
                value = gain[plane, j] + end[plane, j]
                far_leaving[plane, j] = value
                far_low[plane, j] = pltpu.roll(value, FAR, 0)
                low[plane, j] = pltpu.roll(value, deep, 0)
                c_state[plane, j, own, :] = value
            far_launch()

            @pl.when(has_up)
            def _():
                side_up.start()

            @pl.when(has_down)
            def _():
                side_down.start()

            @pl.when(has_up)
            def _():
                side_down.wait_recv()
                for plane, j in each_slab():
                    c_state[plane, j, above(deep), :] = side_above[plane, j]

            @pl.when(has_down)
            def _():
                side_up.wait_recv()
                for plane, j in each_slab():
                    c_state[plane, j, below(deep), :] = side_below[plane, j]

            coarse_wave(c_core)
            for plane, j in each_slab():
                leaving[plane, j] = c_state[plane, j, own, :]
            launch()

    @pl.when(has_after & ((cut == 0) | odd))
    def _():
        natural()

    @pl.when(has_before & even)
    def _():
        to_own.wait_recv()
        for plane, j in each_slab():
            gain[plane, j] = arrived[plane, j] - gain[plane, j]

    @pl.when(has_before)
    def _():
        for plane in range(planes):
            parts = relaid([gain[plane, j // 2] for j in range(tiles)])
            for t in range(tiles):
                for r in range(2):
                    spread[plane, t, pl.ds(r, coarse_count, stride=2), :] = parts[t]
            for t in range(tiles):
                at = (plane, slice(None), pl.ds(t * LANES, LANES))
                out_ref[at] = out_ref[at] + spread[plane, t]

    pl.when(has_before)(landed)
    for there, copies in (
        (has_up, rest_up), (has_down, rest_down),
        (has_after & has_up, [spill_up]), (has_after & has_down, [spill_down]),
        (has_before & has_up, [start_up]), (has_before & has_down, [start_down]),
    ):
        @pl.when(there)
        def _():
            for copy in copies:
                copy.wait_send()


def per_device(tile_count, slices, start_states):
    fields = start_states[0]
    planes, row_count, columns = fields.shape
    tiles = columns // LANES
    half = tiles // 2
    fine = line_tables(tiles, tiles, 1.0, columns, FINE_SPACING, FINE_STEP)
    coarse = line_tables(half, tiles, 2.0, columns, COARSE_SPACING, COARSE_STEP)
    fine_count = row_count + 4 * SUB
    coarse_count = row_count // 2
    c_count = coarse_count + 3 * SUB
    f32 = jnp.float32

    def vmem(*shape):
        return pltpu.VMEM(shape, f32)

    slab = vmem(planes, half, coarse_count, LANES)
    out = pl.pallas_call(
        functools.partial(kernel, tile_count, slices),
        out_shape=jax.ShapeDtypeStruct(fields.shape, f32),
        in_specs=[pl.BlockSpec(memory_space=pltpu.HBM)] * 5,
        out_specs=pl.BlockSpec(memory_space=pltpu.VMEM),
        scratch_shapes=[vmem(*fields.shape)]
        + [pltpu.VMEM(a.shape, a.dtype) for a in fine + coarse]
        + [vmem(tiles, LANES)] * 4
        + [
            vmem(planes, tiles, fine_count, LANES),
            vmem(tiles, 2 * (row_count + 2 * SUB), LANES),
            vmem(tiles, 2, fine_count, LANES),
        ]
        + [vmem(planes, tiles, SUB, LANES)] * 2
        + [slab] * 3
        + [
            vmem(planes, half, 2 * SUB, LANES),
            vmem(planes, half, c_count, LANES),
            vmem(half, 4 * SUB, LANES),
            vmem(half, 2, c_count, LANES),
            vmem(fine_count, LANES),
            vmem(tiles, fine_count, LANES),
            vmem(tiles, fine_count, LANES),
            vmem(c_count, LANES),
            vmem(half, c_count, LANES),
            vmem(half, c_count, LANES),
            vmem(planes, half, c_count, LANES),
            vmem(planes, tiles, row_count, LANES),
        ]
        + [slab] * 2
        + [vmem(planes, half, HALO[-1], LANES)] * 2
        + [slab] * 11
        + [vmem(planes, half, FAR, LANES)] * 2
        + [vmem(planes, half, HALO[-1], LANES)] * 6
        + [
            pltpu.SemaphoreType.DMA((len(fine + coarse) + planes,)),
            pltpu.SemaphoreType.DMA((22,)),
            pltpu.SemaphoreType.DMA((22,)),
            pltpu.SemaphoreType.REGULAR,
            pltpu.SemaphoreType.REGULAR,
        ],
        compiler_params=pltpu.CompilerParams(
            collective_id=0, has_side_effects=True, vmem_limit_bytes=24 * 1024 * 1024
        ),
    )(*[pltpu.with_memory_space_constraint(jnp.asarray(a), pltpu.HBM) for a in (fields,) + fine + coarse])
    return out[None]


def solution(mesh):
    spec = P("cuts", None, "tile", None)
    body = functools.partial(per_device, mesh.shape["tile"], mesh.shape["cuts"])
    return jax.shard_map(body, mesh=mesh, in_specs=(spec,), out_specs=spec, check_vma=False)
```

```python
import functools

import ml_dtypes
import numpy as np
import jax
import jax.numpy as jnp
from jax import lax
from jax.experimental import pallas as pl
from jax.experimental.pallas import tpu as pltpu
from jax.sharding import PartitionSpec as P

STEPS = 3
FINE_SPACING = 0.05
COARSE_SPACING = 0.1
FINE_STEP = 0.015
COARSE_STEP = 0.045
LANES = 128
SUB = 8
HALO = (2, 2, 3)
OWN = 2 * SUB
SPILL = 5
FAR = 2 * HALO[-1]
MESH = pl.DeviceIdType.MESH


def line_tables(tiles, fine_tiles, stride, length, spacing, step):
    groups = LANES // fine_tiles
    lane = np.arange(LANES)
    chunk = (lane % fine_tiles) * groups + lane // fine_tiles
    columns = tiles * LANES
    centers = (np.arange(columns) + 0.5) * stride
    depth = (0.9 + 0.3 * np.sin(6.0 * np.pi * centers / length)).reshape(LANES, tiles).T
    beta = depth * depth / 3.0
    b = beta / spacing**2
    mid = 1.0 + 2.0 * b
    last = tiles - 1
    inv = np.zeros_like(b)
    cp = np.zeros_like(b)
    for j in range(last):
        inv[j] = 1.0 / (mid[j] - (b[j] * cp[j - 1] if j else 0.0))
        cp[j] = b[j] * inv[j]
    run = np.ones_like(b)
    for j in range(1, tiles):
        run[j] = run[j - 1] * cp[j - 1]
    p = np.zeros_like(b)
    q = np.zeros_like(b)
    q[last] = 1.0
    for j in range(last - 1, -1, -1):
        p[j] = run[j + 1] + cp[j] * p[j + 1]
        q[j] = cp[j] * q[j + 1]
    system = np.zeros((LANES, LANES))
    for k in range(LANES):
        system[k, k] = mid[last, k] - b[last, k] * q[last - 1, k]
        if k:
            system[k, k - 1] = -b[last, k] * p[last - 1, k]
        if k + 1 < LANES:
            system[k, k] -= b[last, k] * p[0, k + 1]
            system[k, k + 1] = -b[last, k] * q[0, k + 1]
    solve = np.linalg.inv(system).T[chunk][:, chunk]
    high = solve.astype(ml_dtypes.bfloat16)
    low = (solve - high.astype(np.float64)).astype(ml_dtypes.bfloat16)
    half = np.concatenate([high, low], axis=1)
    weights = np.concatenate([half, half], axis=0)
    slope = step * depth / (2.0 * spacing)
    weight = beta / (spacing**2 + 4.0 * beta)
    inv[last] = b[last]
    rows = np.stack([inv, cp, run, slope, weight])[:, :, chunk]
    return rows.astype(np.float32), weights


def relaid(tiles):
    tiles = list(tiles)
    lane = lax.broadcasted_iota(jnp.int32, tiles[0].shape, 1)
    bit = 1
    while bit < len(tiles):
        keep = (lane & bit) == 0
        for t in range(len(tiles)):
            if t & bit == 0:
                a, b = tiles[t], tiles[t | bit]
                tiles[t] = jnp.where(keep, a, pltpu.roll(b, bit, 1))
                tiles[t | bit] = jnp.where(keep, pltpu.roll(a, LANES - bit, 1), b)
        bit *= 2
    return tiles


def wave(state, held, change, rows, weights, inside, tiles, fine_tiles, wide, core):
    factor_in, slope_in, weight_in = inside
    h0, hn = wide
    t0, tn = core
    at = pl.ds(t0, tn)

    def lane(x):
        return lax.broadcasted_iota(jnp.int32, x.shape, 1)

    def chunk_before(x):
        wrapped = jnp.where(lane(x) == 0, 0.0, pltpu.roll(x, fine_tiles + 1, 1))
        return jnp.where(lane(x) >= fine_tiles, pltpu.roll(x, fine_tiles, 1), wrapped)

    def chunk_after(x):
        wrapped = jnp.where(lane(x) == LANES - 1, 0.0, pltpu.roll(x, LANES - fine_tiles - 1, 1))
        return jnp.where(
            lane(x) < LANES - fine_tiles, pltpu.roll(x, LANES - fine_tiles, 1), wrapped
        )

    def across(load, j):
        right = load(j + 1) if j + 1 < tiles else chunk_after(load(0))
        left = load(j - 1) if j else chunk_before(load(tiles - 1))
        return right - left

    def table(kind, j):
        return rows[kind, pl.ds(j, 1), :]

    last = tiles - 1
    near = pl.ds(h0, hn)
    factor = factor_in[near, :]
    for j in range(tiles):
        along = across(lambda i: state[1, i, near, :], j)
        down = state[2, j, pl.ds(h0 + 1, hn), :] - state[2, j, pl.ds(h0 - 1, hn), :]
        state[0, j, near, :] = state[0, j, near, :] - factor * (along + down)
    def forcing(part, j):
        if part == 0:
            along = across(lambda i: state[0, i, at, :], j)
            return state[1, j, at, :] - table(3, j) * along
        down = state[0, j, pl.ds(t0 + 1, tn), :] - state[0, j, pl.ds(t0 - 1, tn), :]
        return state[2, j, at, :] - slope_in[j, at, :] * down

    solved = []
    for part in range(2):
        spot = pl.ds(part * tn, tn)
        total = None
        inner = None
        for j in range(last):
            force = forcing(part, j)
            if j == 0:
                inner = force * table(0, j)
                total = inner
            else:
                inner = force * table(0, j) + table(1, j) * inner
                total = total + table(2, j) * inner
            held[j, spot, :] = inner
        edge = forcing(part, last) + table(0, last) * (inner + chunk_after(total))
        high = edge.astype(jnp.bfloat16)
        low = (edge - high.astype(jnp.float32)).astype(jnp.bfloat16)
        solved.append(
            jnp.dot(
                jnp.concatenate([high, low], axis=1),
                weights[...],
                preferred_element_type=jnp.float32,
            )
        )
    for part in range(2):
        spot = pl.ds(part * tn, tn)
        value = solved[part][:, :LANES] + solved[part][:, LANES:]
        before = chunk_before(value)
        for j in range(last, -1, -1):
            if j < last:
                value = held[j, spot, :] + table(2, j + 1) * before + table(1, j) * value
            moved = value - state[1 + part, j, at, :]
            change[j, part, at, :] = moved
            around = change[j, part, pl.ds(t0 + 1, tn), :] + change[j, part, pl.ds(t0 - 1, tn), :]
            state[1 + part, j, at, :] = value + weight_in[j, at, :] * (around - 2.0 * moved)


def kernel(
    tile_count, slices, x_hbm, fine_rows_hbm, fine_weights_hbm, coarse_rows_hbm,
    coarse_weights_hbm, out_ref,
    x_ref, fine_rows, fine_weights, coarse_rows, coarse_weights,
    up_edge, down_edge, from_up_edge, from_down_edge, state, held, change,
    from_up, from_down, up_spill, down_spill, from_up_spill, from_down_spill,
    c_state, c_held, c_change, factor_in, slope_in, weight_in, c_factor_in, c_slope_in,
    c_weight_in, offset, spread, start, low_start, start_above, start_below,
    end, arrived, leaving, low, above_in, below_in, far_in, far_leaving, far_low, near_low, gain,
    far_above, far_below, side_above, side_below, halo_up, halo_down, halo_above, halo_below,
    local, send, recv, ready, far_ready,
):
    cut = lax.axis_index("cuts")
    tile = lax.axis_index("tile")
    has_up = tile > 0
    has_down = tile < tile_count - 1
    has_before = cut > 0
    has_after = cut < slices - 1
    odd = cut % 2 == 1
    even = jnp.logical_not(odd)
    has_far_before = odd & (cut > 1)
    has_far_after = odd & (cut < slices - 2)
    planes, row_count, columns = x_ref.shape
    tiles = columns // LANES
    half = tiles // 2
    total_rows = row_count * tile_count
    coarse_count = row_count // 2
    last = planes - 1
    tail = OWN + row_count
    lead = SUB + SUB // 2
    deep = HALO[last]

    pairs = [(fine_rows_hbm, fine_rows)]
    pairs += [(x_hbm.at[plane], x_ref.at[plane]) for plane in range(planes)]
    pairs += [
        (fine_weights_hbm, fine_weights), (coarse_rows_hbm, coarse_rows),
        (coarse_weights_hbm, coarse_weights),
    ]
    loads = [pltpu.make_async_copy(a, b, local.at[i]) for i, (a, b) in enumerate(pairs)]
    for load in loads:
        load.start()

    zero = jnp.zeros((SUB, LANES), jnp.float32)

    def each_slab():
        return [(plane, j) for plane in range(planes) for j in range(half)]

    for plane, j in each_slab():
        from_up_spill[plane, j] = zero
        from_down_spill[plane, j, pl.ds(0, SUB), :] = zero
        from_down_spill[plane, j, pl.ds(SUB, SUB), :] = zero

    right = tile % 2 == 1
    left = jnp.logical_not(right)
    pair_up, pair_down = has_up & right, has_down & left
    cross_up, cross_down = has_up & left, has_down & right

    barrier = pltpu.get_barrier_semaphore()
    beside = [(has_up, cut, tile - 1), (has_down, cut, tile + 1)]

    def in_cut(there, other):
        return [
            (there, other, tile),
            (there & has_up, other, tile - 1),
            (there & has_down, other, tile + 1),
        ]

    before = in_cut(has_before, cut - 1)
    after = in_cut(has_after, cut + 1)
    far_before = in_cut(has_far_before, cut - 2)
    far_after = in_cut(has_far_after, cut + 2)

    def signal(semaphore, devices):
        for exists, to_cut, to_tile in devices:
            @pl.when(exists)
            def _():
                pl.semaphore_signal(
                    semaphore, inc=1, device_id=(to_cut, to_tile), device_id_type=MESH
                )

    def count(devices):
        return sum(exists.astype(jnp.int32) for exists, _, _ in devices)

    signal(barrier, beside + after + far_after)

    def remote(source, target, which, to_cut, to_tile):
        return pltpu.make_async_remote_copy(
            src_ref=source, dst_ref=target, send_sem=send.at[which], recv_sem=recv.at[which],
            device_id=(to_cut, to_tile), device_id_type=MESH,
        )

    def rows_at(ref, row, count):
        return ref.at[:, :, pl.ds(row, count), :]

    spill_up = remote(
        rows_at(up_spill, 0, SPILL), rows_at(from_down_spill, SUB, SPILL), 0, cut, tile - 1
    )
    spill_down = remote(
        rows_at(down_spill, 0, SPILL), rows_at(from_up_spill, 0, SPILL), 1, cut, tile + 1
    )
    rest_up = [
        remote(rows_at(state, SUB, SUB), from_down, 2, cut, tile - 1),
        remote(up_edge, from_down_edge, 3, cut, tile - 1),
    ]
    rest_down = [
        remote(rows_at(state, tail, SUB), from_up, 4, cut, tile + 1),
        remote(down_edge, from_up_edge, 5, cut, tile + 1),
    ]
    start_up = remote(rows_at(start, 0, deep), start_below, 6, cut, tile - 1)
    start_down = remote(rows_at(low_start, 0, deep), start_above, 7, cut, tile + 1)

    for j in range(tiles):
        for row in (0, SUB, tail, tail + SUB):
            for plane in range(planes):
                state[plane, j, pl.ds(row, SUB), :] = zero
            for part in range(2):
                change[j, part, pl.ds(row, SUB), :] = zero

    def mask(total, origin, shape):
        at = lax.broadcasted_iota(jnp.int32, shape, 0) + origin
        return ((at >= 0) & (at < total)).astype(jnp.float32)

    loads[0].wait()
    inside = mask(total_rows, tile * row_count - SUB, (row_count + 2 * SUB, LANES))
    window = pl.ds(SUB, row_count + 2 * SUB)
    factor_in[window, :] = inside * (FINE_STEP / (2.0 * FINE_SPACING))
    for j in range(tiles):
        slope_in[j, window, :] = inside * fine_rows[3, pl.ds(j, 1), :]
        weight_in[j, window, :] = inside * fine_rows[4, pl.ds(j, 1), :]

    for plane in range(planes):
        loads[1 + plane].wait()
        for row in range(0, row_count, SUB):
            values = x_ref[plane, pl.ds(row, SUB), :]
            parts = relaid([values[:, t * LANES : (t + 1) * LANES] for t in range(tiles)])
            for j in range(tiles):
                state[plane, j, pl.ds(OWN + row, SUB), :] = parts[j]

    def restricted(plane, j, row, count):
        parts = [
            state[plane, 2 * j + k, pl.ds(row + r, count, stride=2), :]
            for r in range(2)
            for k in range(2)
        ]
        return 0.25 * ((parts[0] + parts[1]) + (parts[2] + parts[3]))

    @pl.when(has_before)
    def _():
        for plane, j in each_slab():
            value = restricted(plane, j, OWN, coarse_count)
            start[plane, j] = value
            low_start[plane, j] = pltpu.roll(value, deep, 0)

    pl.semaphore_wait(barrier, count(beside + before + far_before))
    signal(ready, before)
    signal(far_ready, far_before)
    loads[1 + planes].wait()
    inner = (lead, row_count + SUB)
    outer = (SUB, row_count + 2 * SUB)
    for wide, core in ((inner, inner), (inner, outer), (outer, outer)):
        wave(
            state, held, change, fine_rows, fine_weights, (factor_in, slope_in, weight_in),
            tiles, tiles, wide, core,
        )
    for j in range(tiles):
        for row, near, edge in ((SUB - 1, SUB, up_edge), (tail + SUB, tail + SUB - 1, down_edge)):
            value = fine_rows[4, pl.ds(j, 1), :] * change[j, 1, pl.ds(near, 1), :]
            state[last, j, pl.ds(row, 1), :] = value
            edge[pl.ds(j, 1), :] = value

    @pl.when(has_after)
    def _():
        @pl.when(has_up)
        def _():
            for plane, j in each_slab():
                up_spill[plane, j, pl.ds(0, SPILL), :] = restricted(
                    plane, j, OWN - 2 * SPILL, SPILL
                )
            spill_up.start()

        @pl.when(has_down)
        def _():
            for plane, j in each_slab():
                down_spill[plane, j, pl.ds(0, SPILL), :] = restricted(plane, j, tail, SPILL)
            spill_down.start()

    @pl.when(has_before)
    def _():
        @pl.when(has_up)
        def _():
            start_up.start()

        @pl.when(has_down)
        def _():
            start_down.start()

    def pass_rest():
        @pl.when(has_up)
        def _():
            for copy in rest_up:
                copy.start()

        @pl.when(has_down)
        def _():
            for copy in rest_down:
                copy.start()

    pl.when(has_before)(pass_rest)
    for load in loads[2 + planes :]:
        load.wait()

    first_part = (pl.ds(0, last), slice(None), pl.ds(0, HALO[0]))
    last_part = (last, slice(None), pl.ds(0, HALO[last]))
    to_own = remote(leaving, arrived, 8, cut + 1, tile)
    to_above = [
        remote(leaving.at[part], below_in.at[part], 9 + i, cut + 1, tile - 1)
        for i, part in enumerate((first_part, last_part))
    ]
    to_below = [
        remote(low.at[part], above_in.at[part], 11 + i, cut + 1, tile + 1)
        for i, part in enumerate((first_part, last_part))
    ]

    far_own = remote(far_leaving, far_in, 13, cut + 2, tile)
    far_up = remote(rows_at(far_leaving, 0, FAR), far_below, 14, cut + 2, tile - 1)
    far_down = remote(rows_at(far_low, 0, FAR), far_above, 15, cut + 2, tile + 1)

    near_up = remote(rows_at(far_in, 0, FAR), far_below, 20, cut, tile - 1)
    near_down = remote(rows_at(near_low, 0, FAR), far_above, 21, cut, tile + 1)
    side_up = remote(rows_at(far_leaving, 0, deep), side_below, 16, cut, tile - 1)
    side_down = remote(rows_at(low, 0, deep), side_above, 17, cut, tile + 1)

    def far_launch():
        @pl.when(has_far_after & cross_up)
        def _():
            far_up.start()

        @pl.when(has_far_after & cross_down)
        def _():
            far_down.start()

    def leave(plane, j, value):
        leaving[plane, j] = value
        low[plane, j] = pltpu.roll(value, HALO[plane], 0)

    first = cut == 0
    first_own = remote(far_leaving, arrived, 8, cut + 1, tile)
    first_halos = [
        remote(halo_up, halo_above, 18, cut + 1, tile),
        remote(halo_down, halo_below, 19, cut + 1, tile),
    ]

    def launch_edges():
        pl.semaphore_wait(ready, count(after))

        @pl.when(has_after & even & has_up)
        def _():
            for copy in to_above:
                copy.start()

        @pl.when(has_after & even & has_down)
        def _():
            for copy in to_below:
                copy.start()

    def launch():
        launch_edges()

        @pl.when(has_after)
        def _():
            to_own.start()

    def landed():
        for there, copies in (
            (has_after & even & has_up, to_above), (has_after & even & has_down, to_below),
            (has_before & has_after, [to_own]),
            (has_far_after & cross_up, [far_up]), (has_far_after & cross_down, [far_down]),
            (has_far_before & pair_up, [near_up]), (has_far_before & pair_down, [near_down]),
            (has_far_after, [far_own]),
            (odd & has_after & has_up, [side_up]), (odd & has_after & has_down, [side_down]),
        ):
            @pl.when(there)
            def _():
                for copy in copies:
                    copy.wait_send()

    def natural():
        for has, copies, into, edges, row, at in (
            (has_up, rest_down, from_up, from_up_edge, OWN, OWN + SUB),
            (has_down, rest_up, from_down, from_down_edge, tail - SUB, tail - SUB - 1),
        ):
            @pl.when(has)
            def _():
                for copy in copies:
                    copy.wait_recv()
                for j in range(tiles):
                    for plane in range(planes):
                        rows = pl.ds(row, SUB)
                        state[plane, j, rows, :] = state[plane, j, rows, :] + into[plane, j]
                for j in range(tiles):
                    one = pl.ds(at, 1)
                    state[last, j, one, :] = state[last, j, one, :] + edges[pl.ds(j, 1), :]

        for plane in range(planes):
            for row in range(0, row_count, SUB):
                parts = relaid([state[plane, j, pl.ds(OWN + row, SUB), :] for j in range(tiles)])
                for t in range(tiles):
                    out_ref[plane, pl.ds(row, SUB), pl.ds(t * LANES, LANES)] = parts[t]

    @pl.when(has_after)
    def _():
        for plane, j in each_slab():
            end[plane, j] = restricted(plane, j, OWN, coarse_count)

        @pl.when(first)
        def _():
            for plane, j in each_slab():
                leave(plane, j, end[plane, j])
                halo_up[plane, j] = restricted(plane, j, OWN - 2 * deep, deep)
                halo_down[plane, j] = restricted(plane, j, tail, deep)
            launch_edges()
            for copy in first_halos:
                copy.start()

        @pl.when(has_up)
        def _():
            spill_down.wait_recv()

        @pl.when(has_down)
        def _():
            spill_up.wait_recv()

        for plane, j in each_slab():
            value = (
                end[plane, j]
                + from_up_spill[plane, j]
                + from_down_spill[plane, j, pl.ds(SPILL, SUB), :]
            )
            end[plane, j] = value
            far_leaving[plane, j] = value

    @pl.when(cut == 0)
    def _():
        first_own.start()
        for copy in first_halos + [first_own]:
            copy.wait_send()
        landed()
        pass_rest()

    own = pl.ds(lead, coarse_count)
    c_core = (SUB, 2 * SUB)

    def above(size):
        return pl.ds(lead - size, size)

    def below(size):
        return pl.ds(lead + coarse_count, size)

    def coarse_wave(wide):
        wave(
            c_state, c_held, c_change, coarse_rows, coarse_weights,
            (c_factor_in, c_slope_in, c_weight_in), half, tiles, wide, c_core,
        )

    @pl.when(has_before)
    def _():
        c_wide = pl.ds(SUB // 2, 3 * SUB)
        c_window = pl.ds(SUB, 2 * SUB)
        origin = tile * coarse_count - lead
        c_inside = mask(total_rows // 2, origin + SUB // 2, (3 * SUB, LANES))
        c_factor_in[c_wide, :] = c_inside * (COARSE_STEP / (2.0 * COARSE_SPACING))
        c_inside = mask(total_rows // 2, origin + SUB, (2 * SUB, LANES))
        for j in range(half):
            c_slope_in[j, c_window, :] = c_inside * coarse_rows[3, pl.ds(j, 1), :]
            c_weight_in[j, c_window, :] = c_inside * coarse_rows[4, pl.ds(j, 1), :]
            for row in range(0, 4 * SUB, SUB):
                for plane in range(planes):
                    c_state[plane, j, pl.ds(row, SUB), :] = zero
                for part in range(2):
                    c_change[j, part, pl.ds(row, SUB), :] = zero

        @pl.when(has_up)
        def _():
            start_down.wait_recv()

        @pl.when(has_down)
        def _():
            start_up.wait_recv()

    @pl.when(has_before & even)
    def _():
        @pl.when(has_up)
        def _():
            for plane, j in each_slab():
                c_state[plane, j, above(deep), :] = start_above[plane, j]

        @pl.when(has_down)
        def _():
            for plane, j in each_slab():
                c_state[plane, j, below(deep), :] = start_below[plane, j]

        for plane, j in each_slab():
            c_state[plane, j, own, :] = start[plane, j]
        coarse_wave(c_core)
        for plane, j in each_slab():
            gain[plane, j] = c_state[plane, j, own, :]

        @pl.when(has_after)
        def _():
            for plane, j in each_slab():
                leave(plane, j, end[plane, j] - gain[plane, j])
            launch()

    @pl.when((has_before & even) | jnp.logical_not(has_after))
    def _():
        natural()

    def joined(place, extra_above=lambda: None, extra_below=lambda: None):
        @pl.when(has_up)
        def _():
            for copy in to_below:
                copy.wait_recv()
            for plane, j in each_slab():
                size = HALO[plane]
                place(
                    plane, j, above(size),
                    above_in[plane, j, pl.ds(0, size), :]
                    - start_above[plane, j, pl.ds(deep - size, size), :],
                )
            extra_above()

        @pl.when(has_down)
        def _():
            for copy in to_above:
                copy.wait_recv()
            for plane, j in each_slab():
                size = HALO[plane]
                place(
                    plane, j, below(size),
                    below_in[plane, j, pl.ds(0, size), :]
                    - start_below[plane, j, pl.ds(0, size), :],
                )
            extra_below()

        to_own.wait_recv()
        for plane, j in each_slab():
            place(plane, j, own, arrived[plane, j] - start[plane, j])

    @pl.when(cut == 1)
    def _():
        def place(plane, j, rows, value):
            c_state[plane, j, rows, :] = value

        def widen(rows, halo, skip):
            for plane, j in each_slab():
                count = HALO[plane]
                at = rows(count)
                c_state[plane, j, at, :] = (
                    c_state[plane, j, at, :] + halo[plane, j, pl.ds(skip(count), count), :]
                )

        for copy in first_halos:
            copy.wait_recv()
        joined(place, lambda: (
            widen(above, halo_above, lambda count: deep - count),
        ), lambda: (
            widen(below, halo_below, lambda count: 0),
        ))

    @pl.when(has_far_before)
    def _():
        def hold(plane, j, rows, value):
            offset[plane, j, rows, :] = value

        def add(plane, j, rows):
            c_state[plane, j, rows, :] = c_state[plane, j, rows, :] + offset[plane, j, rows, :]

        joined(hold)
        far_own.wait_recv()

        @pl.when(pair_up)
        def _():
            near_up.start()

        @pl.when(pair_down)
        def _():
            for plane, j in each_slab():
                near_low[plane, j] = pltpu.roll(far_in[plane, j], FAR, 0)
            near_down.start()

        for plane, j in each_slab():
            c_state[plane, j, own, :] = far_in[plane, j]

        @pl.when(cross_up)
        def _():
            far_down.wait_recv()

        @pl.when(cross_down)
        def _():
            far_up.wait_recv()

        @pl.when(pair_up)
        def _():
            near_down.wait_recv()

        @pl.when(pair_down)
        def _():
            near_up.wait_recv()

        @pl.when(has_up)
        def _():
            for plane, j in each_slab():
                c_state[plane, j, above(FAR), :] = far_above[plane, j]

        @pl.when(has_down)
        def _():
            for plane, j in each_slab():
                c_state[plane, j, below(FAR), :] = far_below[plane, j]

        coarse_wave((SUB // 2, 3 * SUB))

        @pl.when(has_up)
        def _():
            for plane, j in each_slab():
                add(plane, j, above(HALO[plane]))

        @pl.when(has_down)
        def _():
            for plane, j in each_slab():
                add(plane, j, below(HALO[plane]))

        for plane, j in each_slab():
            add(plane, j, own)

    @pl.when(odd)
    def _():
        coarse_wave(c_core)

        @pl.when(jnp.logical_not(has_after))
        def _():
            for plane, j in each_slab():
                gain[plane, j] = c_state[plane, j, own, :]

        @pl.when(has_after)
        def _():
            for plane, j in each_slab():
                far_leaving[plane, j] = c_state[plane, j, own, :] + end[plane, j]
            pl.semaphore_wait(far_ready, count(far_after))

            @pl.when(has_far_after)
            def _():
                far_own.start()

            for plane, j in each_slab():
                value = far_leaving[plane, j]
                far_low[plane, j] = pltpu.roll(value, FAR, 0)
                low[plane, j] = pltpu.roll(value, deep, 0)
                gain[plane, j] = c_state[plane, j, own, :]
                c_state[plane, j, own, :] = value
            far_launch()

            @pl.when(has_up)
            def _():
                side_up.start()

            @pl.when(has_down)
            def _():
                side_down.start()

            @pl.when(has_up)
            def _():
                side_down.wait_recv()
                for plane, j in each_slab():
                    c_state[plane, j, above(deep), :] = side_above[plane, j]

            @pl.when(has_down)
            def _():
                side_up.wait_recv()
                for plane, j in each_slab():
                    c_state[plane, j, below(deep), :] = side_below[plane, j]

            coarse_wave(c_core)
            for plane, j in each_slab():
                leaving[plane, j] = c_state[plane, j, own, :]
            launch()

    @pl.when(has_after & ((cut == 0) | odd))
    def _():
        natural()

    @pl.when(has_before & even)
    def _():
        to_own.wait_recv()
        for plane, j in each_slab():
            gain[plane, j] = arrived[plane, j] - gain[plane, j]

    @pl.when(has_before)
    def _():
        for plane in range(planes):
            parts = relaid([gain[plane, j // 2] for j in range(tiles)])
            for t in range(tiles):
                for r in range(2):
                    spread[plane, t, pl.ds(r, coarse_count, stride=2), :] = parts[t]
            for t in range(tiles):
                at = (plane, slice(None), pl.ds(t * LANES, LANES))
                out_ref[at] = out_ref[at] + spread[plane, t]

    pl.when(has_before)(landed)
    for there, copies in (
        (has_up, rest_up), (has_down, rest_down),
        (has_after & has_up, [spill_up]), (has_after & has_down, [spill_down]),
        (has_before & has_up, [start_up]), (has_before & has_down, [start_down]),
    ):
        @pl.when(there)
        def _():
            for copy in copies:
                copy.wait_send()


def per_device(tile_count, slices, start_states):
    fields = start_states[0]
    planes, row_count, columns = fields.shape
    tiles = columns // LANES
    half = tiles // 2
    fine = line_tables(tiles, tiles, 1.0, columns, FINE_SPACING, FINE_STEP)
    coarse = line_tables(half, tiles, 2.0, columns, COARSE_SPACING, COARSE_STEP)
    fine_count = row_count + 4 * SUB
    coarse_count = row_count // 2
    c_count = coarse_count + 3 * SUB
    f32 = jnp.float32

    def vmem(*shape):
        return pltpu.VMEM(shape, f32)

    slab = vmem(planes, half, coarse_count, LANES)
    out = pl.pallas_call(
        functools.partial(kernel, tile_count, slices),
        out_shape=jax.ShapeDtypeStruct(fields.shape, f32),
        in_specs=[pl.BlockSpec(memory_space=pltpu.HBM)] * 5,
        out_specs=pl.BlockSpec(memory_space=pltpu.VMEM),
        scratch_shapes=[vmem(*fields.shape)]
        + [pltpu.VMEM(a.shape, a.dtype) for a in fine + coarse]
        + [vmem(tiles, LANES)] * 4
        + [
            vmem(planes, tiles, fine_count, LANES),
            vmem(tiles, 2 * (row_count + 2 * SUB), LANES),
            vmem(tiles, 2, fine_count, LANES),
        ]
        + [vmem(planes, tiles, SUB, LANES)] * 2
        + [slab] * 3
        + [
            vmem(planes, half, 2 * SUB, LANES),
            vmem(planes, half, c_count, LANES),
            vmem(half, 4 * SUB, LANES),
            vmem(half, 2, c_count, LANES),
            vmem(fine_count, LANES),
            vmem(tiles, fine_count, LANES),
            vmem(tiles, fine_count, LANES),
            vmem(c_count, LANES),
            vmem(half, c_count, LANES),
            vmem(half, c_count, LANES),
            vmem(planes, half, c_count, LANES),
            vmem(planes, tiles, row_count, LANES),
        ]
        + [slab] * 2
        + [vmem(planes, half, HALO[-1], LANES)] * 2
        + [slab] * 11
        + [vmem(planes, half, FAR, LANES)] * 2
        + [vmem(planes, half, HALO[-1], LANES)] * 6
        + [
            pltpu.SemaphoreType.DMA((len(fine + coarse) + planes,)),
            pltpu.SemaphoreType.DMA((22,)),
            pltpu.SemaphoreType.DMA((22,)),
            pltpu.SemaphoreType.REGULAR,
            pltpu.SemaphoreType.REGULAR,
        ],
        compiler_params=pltpu.CompilerParams(
            collective_id=0, has_side_effects=True, vmem_limit_bytes=24 * 1024 * 1024
        ),
    )(*[pltpu.with_memory_space_constraint(jnp.asarray(a), pltpu.HBM) for a in (fields,) + fine + coarse])
    return out[None]


def solution(mesh):
    spec = P("cuts", None, "tile", None)
    body = functools.partial(per_device, mesh.shape["tile"], mesh.shape["cuts"])
    return jax.shard_map(body, mesh=mesh, in_specs=(spec,), out_specs=spec, check_vma=False)
```

```python
import functools

import ml_dtypes
import numpy as np
import jax
import jax.numpy as jnp
from jax import lax
from jax.experimental import pallas as pl
from jax.experimental.pallas import tpu as pltpu
from jax.sharding import PartitionSpec as P

STEPS = 3
FINE_SPACING = 0.05
COARSE_SPACING = 0.1
FINE_STEP = 0.015
COARSE_STEP = 0.045
LANES = 128
SUB = 8
HALO = (2, 2, 3)
OWN = 2 * SUB
SPILL = 5
FAR = 2 * HALO[-1]
MESH = pl.DeviceIdType.MESH


def line_tables(tiles, fine_tiles, stride, length, spacing, step):
    groups = LANES // fine_tiles
    lane = np.arange(LANES)
    chunk = (lane % fine_tiles) * groups + lane // fine_tiles
    columns = tiles * LANES
    centers = (np.arange(columns) + 0.5) * stride
    depth = (0.9 + 0.3 * np.sin(6.0 * np.pi * centers / length)).reshape(LANES, tiles).T
    beta = depth * depth / 3.0
    b = beta / spacing**2
    mid = 1.0 + 2.0 * b
    last = tiles - 1
    inv = np.zeros_like(b)
    cp = np.zeros_like(b)
    for j in range(last):
        inv[j] = 1.0 / (mid[j] - (b[j] * cp[j - 1] if j else 0.0))
        cp[j] = b[j] * inv[j]
    run = np.ones_like(b)
    for j in range(1, tiles):
        run[j] = run[j - 1] * cp[j - 1]
    p = np.zeros_like(b)
    q = np.zeros_like(b)
    q[last] = 1.0
    for j in range(last - 1, -1, -1):
        p[j] = run[j + 1] + cp[j] * p[j + 1]
        q[j] = cp[j] * q[j + 1]
    system = np.zeros((LANES, LANES))
    for k in range(LANES):
        system[k, k] = mid[last, k] - b[last, k] * q[last - 1, k]
        if k:
            system[k, k - 1] = -b[last, k] * p[last - 1, k]
        if k + 1 < LANES:
            system[k, k] -= b[last, k] * p[0, k + 1]
            system[k, k + 1] = -b[last, k] * q[0, k + 1]
    solve = np.linalg.inv(system).T[chunk][:, chunk]
    high = solve.astype(ml_dtypes.bfloat16)
    low = (solve - high.astype(np.float64)).astype(ml_dtypes.bfloat16)
    half = np.concatenate([high, low], axis=1)
    weights = np.concatenate([half, half], axis=0)
    slope = step * depth / (2.0 * spacing)
    weight = beta / (spacing**2 + 4.0 * beta)
    inv[last] = b[last]
    rows = np.stack([inv, cp, run, slope, weight])[:, :, chunk]
    return rows.astype(np.float32), weights


def relaid(tiles):
    tiles = list(tiles)
    lane = lax.broadcasted_iota(jnp.int32, tiles[0].shape, 1)
    bit = 1
    while bit < len(tiles):
        keep = (lane & bit) == 0
        for t in range(len(tiles)):
            if t & bit == 0:
                a, b = tiles[t], tiles[t | bit]
                tiles[t] = jnp.where(keep, a, pltpu.roll(b, bit, 1))
                tiles[t | bit] = jnp.where(keep, pltpu.roll(a, LANES - bit, 1), b)
        bit *= 2
    return tiles


def wave(state, held, change, rows, weights, inside, tiles, fine_tiles, wide, core):
    factor_in, slope_in, weight_in = inside
    h0, hn = wide
    t0, tn = core
    at = pl.ds(t0, tn)

    def lane(x):
        return lax.broadcasted_iota(jnp.int32, x.shape, 1)

    def chunk_before(x):
        wrapped = jnp.where(lane(x) == 0, 0.0, pltpu.roll(x, fine_tiles + 1, 1))
        return jnp.where(lane(x) >= fine_tiles, pltpu.roll(x, fine_tiles, 1), wrapped)

    def chunk_after(x):
        wrapped = jnp.where(lane(x) == LANES - 1, 0.0, pltpu.roll(x, LANES - fine_tiles - 1, 1))
        return jnp.where(
            lane(x) < LANES - fine_tiles, pltpu.roll(x, LANES - fine_tiles, 1), wrapped
        )

    def across(load, j):
        right = load(j + 1) if j + 1 < tiles else chunk_after(load(0))
        left = load(j - 1) if j else chunk_before(load(tiles - 1))
        return right - left

    def table(kind, j):
        return rows[kind, pl.ds(j, 1), :]

    last = tiles - 1
    near = pl.ds(h0, hn)
    factor = factor_in[near, :]
    for j in range(tiles):
        along = across(lambda i: state[1, i, near, :], j)
        down = state[2, j, pl.ds(h0 + 1, hn), :] - state[2, j, pl.ds(h0 - 1, hn), :]
        state[0, j, near, :] = state[0, j, near, :] - factor * (along + down)
    def forcing(part, j):
        if part == 0:
            along = across(lambda i: state[0, i, at, :], j)
            return state[1, j, at, :] - table(3, j) * along
        down = state[0, j, pl.ds(t0 + 1, tn), :] - state[0, j, pl.ds(t0 - 1, tn), :]
        return state[2, j, at, :] - slope_in[j, at, :] * down

    solved = []
    for part in range(2):
        spot = pl.ds(part * tn, tn)
        total = None
        inner = None
        for j in range(last):
            force = forcing(part, j)
            if j == 0:
                inner = force * table(0, j)
                total = inner
            else:
                inner = force * table(0, j) + table(1, j) * inner
                total = total + table(2, j) * inner
            held[j, spot, :] = inner
        edge = forcing(part, last) + table(0, last) * (inner + chunk_after(total))
        high = edge.astype(jnp.bfloat16)
        low = (edge - high.astype(jnp.float32)).astype(jnp.bfloat16)
        solved.append(
            jnp.dot(
                jnp.concatenate([high, low], axis=1),
                weights[...],
                preferred_element_type=jnp.float32,
            )
        )
    for part in range(2):
        spot = pl.ds(part * tn, tn)
        value = solved[part][:, :LANES] + solved[part][:, LANES:]
        before = chunk_before(value)
        for j in range(last, -1, -1):
            if j < last:
                value = held[j, spot, :] + table(2, j + 1) * before + table(1, j) * value
            moved = value - state[1 + part, j, at, :]
            change[j, part, at, :] = moved
            around = change[j, part, pl.ds(t0 + 1, tn), :] + change[j, part, pl.ds(t0 - 1, tn), :]
            state[1 + part, j, at, :] = value + weight_in[j, at, :] * (around - 2.0 * moved)


def kernel(
    tile_count, slices, x_hbm, fine_rows_hbm, fine_weights_hbm, coarse_rows_hbm,
    coarse_weights_hbm, out_ref,
    x_ref, fine_rows, fine_weights, coarse_rows, coarse_weights,
    up_edge, down_edge, from_up_edge, from_down_edge, state, held, change,
    from_up, from_down, up_spill, down_spill, from_up_spill, from_down_spill,
    c_state, c_held, c_change, factor_in, slope_in, weight_in, c_factor_in, c_slope_in,
    c_weight_in, offset, spread, start, low_start, start_above, start_below,
    end, arrived, leaving, low, above_in, below_in, far_in, far_leaving, far_low, near_low, gain,
    far_above, far_below, side_above, side_below, halo_up, halo_down, halo_above, halo_below,
    local, send, recv, ready, far_ready,
):
    cut = lax.axis_index("cuts")
    tile = lax.axis_index("tile")
    has_up = tile > 0
    has_down = tile < tile_count - 1
    has_before = cut > 0
    has_after = cut < slices - 1
    odd = cut % 2 == 1
    even = jnp.logical_not(odd)
    has_far_before = odd & (cut > 1)
    has_far_after = odd & (cut < slices - 2)
    planes, row_count, columns = x_ref.shape
    tiles = columns // LANES
    half = tiles // 2
    total_rows = row_count * tile_count
    coarse_count = row_count // 2
    last = planes - 1
    tail = OWN + row_count
    lead = SUB + SUB // 2
    deep = HALO[last]

    pairs = [(fine_rows_hbm, fine_rows)]
    pairs += [(x_hbm.at[plane], x_ref.at[plane]) for plane in range(planes)]
    pairs += [
        (fine_weights_hbm, fine_weights), (coarse_rows_hbm, coarse_rows),
        (coarse_weights_hbm, coarse_weights),
    ]
    loads = [pltpu.make_async_copy(a, b, local.at[i]) for i, (a, b) in enumerate(pairs)]
    for load in loads:
        load.start()

    zero = jnp.zeros((SUB, LANES), jnp.float32)

    def each_slab():
        return [(plane, j) for plane in range(planes) for j in range(half)]

    for plane, j in each_slab():
        from_up_spill[plane, j] = zero
        from_down_spill[plane, j, pl.ds(0, SUB), :] = zero
        from_down_spill[plane, j, pl.ds(SUB, SUB), :] = zero

    right = tile % 2 == 1
    left = jnp.logical_not(right)
    pair_up, pair_down = has_up & right, has_down & left
    cross_up, cross_down = has_up & left, has_down & right

    barrier = pltpu.get_barrier_semaphore()
    beside = [(has_up, cut, tile - 1), (has_down, cut, tile + 1)]

    def in_cut(there, other):
        return [
            (there, other, tile),
            (there & has_up, other, tile - 1),
            (there & has_down, other, tile + 1),
        ]

    before = in_cut(has_before, cut - 1)
    after = in_cut(has_after, cut + 1)
    far_before = in_cut(has_far_before, cut - 2)
    far_after = in_cut(has_far_after, cut + 2)

    def signal(semaphore, devices):
        for exists, to_cut, to_tile in devices:
            @pl.when(exists)
            def _():
                pl.semaphore_signal(
                    semaphore, inc=1, device_id=(to_cut, to_tile), device_id_type=MESH
                )

    def count(devices):
        return sum(exists.astype(jnp.int32) for exists, _, _ in devices)

    signal(barrier, beside + after + far_after)

    def remote(source, target, which, to_cut, to_tile):
        return pltpu.make_async_remote_copy(
            src_ref=source, dst_ref=target, send_sem=send.at[which], recv_sem=recv.at[which],
            device_id=(to_cut, to_tile), device_id_type=MESH,
        )

    def rows_at(ref, row, count):
        return ref.at[:, :, pl.ds(row, count), :]

    spill_up = remote(
        rows_at(up_spill, 0, SPILL), rows_at(from_down_spill, SUB, SPILL), 0, cut, tile - 1
    )
    spill_down = remote(
        rows_at(down_spill, 0, SPILL), rows_at(from_up_spill, 0, SPILL), 1, cut, tile + 1
    )
    rest_up = [
        remote(rows_at(state, SUB, SUB), from_down, 2, cut, tile - 1),
        remote(up_edge, from_down_edge, 3, cut, tile - 1),
    ]
    rest_down = [
        remote(rows_at(state, tail, SUB), from_up, 4, cut, tile + 1),
        remote(down_edge, from_up_edge, 5, cut, tile + 1),
    ]
    start_up = remote(rows_at(start, 0, deep), start_below, 6, cut, tile - 1)
    start_down = remote(rows_at(low_start, 0, deep), start_above, 7, cut, tile + 1)

    for j in range(tiles):
        for row in (0, SUB, tail, tail + SUB):
            for plane in range(planes):
                state[plane, j, pl.ds(row, SUB), :] = zero
            for part in range(2):
                change[j, part, pl.ds(row, SUB), :] = zero

    def mask(total, origin, shape):
        at = lax.broadcasted_iota(jnp.int32, shape, 0) + origin
        return ((at >= 0) & (at < total)).astype(jnp.float32)

    loads[0].wait()
    inside = mask(total_rows, tile * row_count - SUB, (row_count + 2 * SUB, LANES))
    window = pl.ds(SUB, row_count + 2 * SUB)
    factor_in[window, :] = inside * (FINE_STEP / (2.0 * FINE_SPACING))
    for j in range(tiles):
        slope_in[j, window, :] = inside * fine_rows[3, pl.ds(j, 1), :]
        weight_in[j, window, :] = inside * fine_rows[4, pl.ds(j, 1), :]

    for plane in range(planes):
        loads[1 + plane].wait()
        for row in range(0, row_count, SUB):
            values = x_ref[plane, pl.ds(row, SUB), :]
            parts = relaid([values[:, t * LANES : (t + 1) * LANES] for t in range(tiles)])
            for j in range(tiles):
                state[plane, j, pl.ds(OWN + row, SUB), :] = parts[j]

    def restricted(plane, j, row, count):
        parts = [
            state[plane, 2 * j + k, pl.ds(row + r, count, stride=2), :]
            for r in range(2)
            for k in range(2)
        ]
        return 0.25 * ((parts[0] + parts[1]) + (parts[2] + parts[3]))

    @pl.when(has_before)
    def _():
        for plane, j in each_slab():
            value = restricted(plane, j, OWN, coarse_count)
            start[plane, j] = value
            low_start[plane, j] = pltpu.roll(value, deep, 0)

    pl.semaphore_wait(barrier, count(beside + before + far_before))
    signal(ready, before)
    signal(far_ready, far_before)
    loads[1 + planes].wait()
    inner = (lead, row_count + SUB)
    outer = (SUB, row_count + 2 * SUB)
    for wide, core in ((inner, inner), (inner, outer), (outer, outer)):
        wave(
            state, held, change, fine_rows, fine_weights, (factor_in, slope_in, weight_in),
            tiles, tiles, wide, core,
        )
    for j in range(tiles):
        for row, near, edge in ((SUB - 1, SUB, up_edge), (tail + SUB, tail + SUB - 1, down_edge)):
            value = fine_rows[4, pl.ds(j, 1), :] * change[j, 1, pl.ds(near, 1), :]
            state[last, j, pl.ds(row, 1), :] = value
            edge[pl.ds(j, 1), :] = value

    @pl.when(has_after)
    def _():
        def spill_to_up():
            for plane, j in each_slab():
                up_spill[plane, j, pl.ds(0, SPILL), :] = restricted(
                    plane, j, OWN - 2 * SPILL, SPILL
                )
            spill_up.start()

        def spill_to_down():
            for plane, j in each_slab():
                down_spill[plane, j, pl.ds(0, SPILL), :] = restricted(plane, j, tail, SPILL)
            spill_down.start()

        pl.when(cross_up)(spill_to_up)
        pl.when(cross_down)(spill_to_down)
        pl.when(pair_up)(spill_to_up)
        pl.when(pair_down)(spill_to_down)

    @pl.when(has_before)
    def _():
        @pl.when(has_up)
        def _():
            start_up.start()

        @pl.when(has_down)
        def _():
            start_down.start()

    def pass_rest():
        @pl.when(has_up)
        def _():
            for copy in rest_up:
                copy.start()

        @pl.when(has_down)
        def _():
            for copy in rest_down:
                copy.start()

    pl.when(has_before)(pass_rest)
    for load in loads[2 + planes :]:
        load.wait()

    first_part = (pl.ds(0, last), slice(None), pl.ds(0, HALO[0]))
    last_part = (last, slice(None), pl.ds(0, HALO[last]))
    to_own = remote(leaving, arrived, 8, cut + 1, tile)
    to_above = [
        remote(leaving.at[part], below_in.at[part], 9 + i, cut + 1, tile - 1)
        for i, part in enumerate((first_part, last_part))
    ]
    to_below = [
        remote(low.at[part], above_in.at[part], 11 + i, cut + 1, tile + 1)
        for i, part in enumerate((first_part, last_part))
    ]

    far_own = remote(far_leaving, far_in, 13, cut + 2, tile)
    far_up = remote(rows_at(far_leaving, 0, FAR), far_below, 14, cut + 2, tile - 1)
    far_down = remote(rows_at(far_low, 0, FAR), far_above, 15, cut + 2, tile + 1)

    near_up = remote(rows_at(far_in, 0, FAR), far_below, 20, cut, tile - 1)
    near_down = remote(rows_at(near_low, 0, FAR), far_above, 21, cut, tile + 1)
    side_up = remote(rows_at(far_leaving, 0, deep), side_below, 16, cut, tile - 1)
    side_down = remote(rows_at(low, 0, deep), side_above, 17, cut, tile + 1)

    def far_launch():
        @pl.when(has_far_after & cross_up)
        def _():
            far_up.start()

        @pl.when(has_far_after & cross_down)
        def _():
            far_down.start()

    def leave(plane, j, value):
        leaving[plane, j] = value
        low[plane, j] = pltpu.roll(value, HALO[plane], 0)

    first = cut == 0
    first_own = remote(far_leaving, arrived, 8, cut + 1, tile)
    first_halos = [
        remote(halo_up, halo_above, 18, cut + 1, tile),
        remote(halo_down, halo_below, 19, cut + 1, tile),
    ]

    def launch_edges():
        pl.semaphore_wait(ready, count(after))

        @pl.when(has_after & even & has_up)
        def _():
            for copy in to_above:
                copy.start()

        @pl.when(has_after & even & has_down)
        def _():
            for copy in to_below:
                copy.start()

    def launch():
        launch_edges()

        @pl.when(has_after)
        def _():
            to_own.start()

    def landed():
        for there, copies in (
            (has_after & even & has_up, to_above), (has_after & even & has_down, to_below),
            (has_before & has_after, [to_own]),
            (has_far_after & cross_up, [far_up]), (has_far_after & cross_down, [far_down]),
            (has_far_before & pair_up, [near_up]), (has_far_before & pair_down, [near_down]),
            (has_far_after, [far_own]),
            (odd & has_after & has_up, [side_up]), (odd & has_after & has_down, [side_down]),
        ):
            @pl.when(there)
            def _():
                for copy in copies:
                    copy.wait_send()

    def natural():
        for has, copies, into, edges, row, at in (
            (has_up, rest_down, from_up, from_up_edge, OWN, OWN + SUB),
            (has_down, rest_up, from_down, from_down_edge, tail - SUB, tail - SUB - 1),
        ):
            @pl.when(has)
            def _():
                for copy in copies:
                    copy.wait_recv()
                for j in range(tiles):
                    for plane in range(planes):
                        rows = pl.ds(row, SUB)
                        state[plane, j, rows, :] = state[plane, j, rows, :] + into[plane, j]
                for j in range(tiles):
                    one = pl.ds(at, 1)
                    state[last, j, one, :] = state[last, j, one, :] + edges[pl.ds(j, 1), :]

        for plane in range(planes):
            for row in range(0, row_count, SUB):
                parts = relaid([state[plane, j, pl.ds(OWN + row, SUB), :] for j in range(tiles)])
                for t in range(tiles):
                    out_ref[plane, pl.ds(row, SUB), pl.ds(t * LANES, LANES)] = parts[t]

    @pl.when(has_after)
    def _():
        for plane, j in each_slab():
            end[plane, j] = restricted(plane, j, OWN, coarse_count)

        @pl.when(first)
        def _():
            for plane, j in each_slab():
                leave(plane, j, end[plane, j])
                halo_up[plane, j] = restricted(plane, j, OWN - 2 * deep, deep)
                halo_down[plane, j] = restricted(plane, j, tail, deep)
            launch_edges()
            for copy in first_halos:
                copy.start()

        @pl.when(has_up)
        def _():
            spill_down.wait_recv()

        @pl.when(has_down)
        def _():
            spill_up.wait_recv()

        for plane, j in each_slab():
            value = (
                end[plane, j]
                + from_up_spill[plane, j]
                + from_down_spill[plane, j, pl.ds(SPILL, SUB), :]
            )
            end[plane, j] = value
            far_leaving[plane, j] = value

    @pl.when(cut == 0)
    def _():
        first_own.start()
        for copy in first_halos + [first_own]:
            copy.wait_send()
        landed()
        pass_rest()

    own = pl.ds(lead, coarse_count)
    c_core = (SUB, 2 * SUB)

    def above(size):
        return pl.ds(lead - size, size)

    def below(size):
        return pl.ds(lead + coarse_count, size)

    def coarse_wave(wide):
        wave(
            c_state, c_held, c_change, coarse_rows, coarse_weights,
            (c_factor_in, c_slope_in, c_weight_in), half, tiles, wide, c_core,
        )

    @pl.when(has_before)
    def _():
        c_wide = pl.ds(SUB // 2, 3 * SUB)
        c_window = pl.ds(SUB, 2 * SUB)
        origin = tile * coarse_count - lead
        c_inside = mask(total_rows // 2, origin + SUB // 2, (3 * SUB, LANES))
        c_factor_in[c_wide, :] = c_inside * (COARSE_STEP / (2.0 * COARSE_SPACING))
        c_inside = mask(total_rows // 2, origin + SUB, (2 * SUB, LANES))
        for j in range(half):
            c_slope_in[j, c_window, :] = c_inside * coarse_rows[3, pl.ds(j, 1), :]
            c_weight_in[j, c_window, :] = c_inside * coarse_rows[4, pl.ds(j, 1), :]
            for row in range(0, 4 * SUB, SUB):
                for plane in range(planes):
                    c_state[plane, j, pl.ds(row, SUB), :] = zero
                for part in range(2):
                    c_change[j, part, pl.ds(row, SUB), :] = zero

        @pl.when(has_up)
        def _():
            start_down.wait_recv()

        @pl.when(has_down)
        def _():
            start_up.wait_recv()

    @pl.when(has_before & even)
    def _():
        @pl.when(has_up)
        def _():
            for plane, j in each_slab():
                c_state[plane, j, above(deep), :] = start_above[plane, j]

        @pl.when(has_down)
        def _():
            for plane, j in each_slab():
                c_state[plane, j, below(deep), :] = start_below[plane, j]

        for plane, j in each_slab():
            c_state[plane, j, own, :] = start[plane, j]
        coarse_wave(c_core)
        for plane, j in each_slab():
            gain[plane, j] = c_state[plane, j, own, :]

        @pl.when(has_after)
        def _():
            for plane, j in each_slab():
                leave(plane, j, end[plane, j] - gain[plane, j])
            launch()

    @pl.when((has_before & even) | jnp.logical_not(has_after))
    def _():
        natural()

    def joined(place, extra_above=lambda: None, extra_below=lambda: None):
        @pl.when(has_up)
        def _():
            for copy in to_below:
                copy.wait_recv()
            for plane, j in each_slab():
                size = HALO[plane]
                place(
                    plane, j, above(size),
                    above_in[plane, j, pl.ds(0, size), :]
                    - start_above[plane, j, pl.ds(deep - size, size), :],
                )
            extra_above()

        @pl.when(has_down)
        def _():
            for copy in to_above:
                copy.wait_recv()
            for plane, j in each_slab():
                size = HALO[plane]
                place(
                    plane, j, below(size),
                    below_in[plane, j, pl.ds(0, size), :]
                    - start_below[plane, j, pl.ds(0, size), :],
                )
            extra_below()

        to_own.wait_recv()
        for plane, j in each_slab():
            place(plane, j, own, arrived[plane, j] - start[plane, j])

    @pl.when(cut == 1)
    def _():
        def place(plane, j, rows, value):
            c_state[plane, j, rows, :] = value

        def widen(rows, halo, skip):
            for plane, j in each_slab():
                count = HALO[plane]
                at = rows(count)
                c_state[plane, j, at, :] = (
                    c_state[plane, j, at, :] + halo[plane, j, pl.ds(skip(count), count), :]
                )

        for copy in first_halos:
            copy.wait_recv()
        joined(place, lambda: (
            widen(above, halo_above, lambda count: deep - count),
        ), lambda: (
            widen(below, halo_below, lambda count: 0),
        ))

    @pl.when(has_far_before)
    def _():
        def hold(plane, j, rows, value):
            offset[plane, j, rows, :] = value

        def add(plane, j, rows):
            c_state[plane, j, rows, :] = c_state[plane, j, rows, :] + offset[plane, j, rows, :]

        joined(hold)
        far_own.wait_recv()

        @pl.when(pair_up)
        def _():
            near_up.start()

        @pl.when(pair_down)
        def _():
            for plane, j in each_slab():
                near_low[plane, j] = pltpu.roll(far_in[plane, j], FAR, 0)
            near_down.start()

        for plane, j in each_slab():
            c_state[plane, j, own, :] = far_in[plane, j]

        @pl.when(cross_up)
        def _():
            far_down.wait_recv()

        @pl.when(cross_down)
        def _():
            far_up.wait_recv()

        @pl.when(pair_up)
        def _():
            near_down.wait_recv()

        @pl.when(pair_down)
        def _():
            near_up.wait_recv()

        @pl.when(has_up)
        def _():
            for plane, j in each_slab():
                c_state[plane, j, above(FAR), :] = far_above[plane, j]

        @pl.when(has_down)
        def _():
            for plane, j in each_slab():
                c_state[plane, j, below(FAR), :] = far_below[plane, j]

        coarse_wave((SUB // 2, 3 * SUB))

        @pl.when(has_up)
        def _():
            for plane, j in each_slab():
                add(plane, j, above(HALO[plane]))

        @pl.when(has_down)
        def _():
            for plane, j in each_slab():
                add(plane, j, below(HALO[plane]))

        for plane, j in each_slab():
            add(plane, j, own)

    @pl.when(odd)
    def _():
        coarse_wave(c_core)

        @pl.when(jnp.logical_not(has_after))
        def _():
            for plane, j in each_slab():
                gain[plane, j] = c_state[plane, j, own, :]

        @pl.when(has_after)
        def _():
            for plane, j in each_slab():
                far_leaving[plane, j] = c_state[plane, j, own, :] + end[plane, j]
            pl.semaphore_wait(far_ready, count(far_after))

            @pl.when(has_far_after)
            def _():
                far_own.start()

            for plane, j in each_slab():
                value = far_leaving[plane, j]
                far_low[plane, j] = pltpu.roll(value, FAR, 0)
                low[plane, j] = pltpu.roll(value, deep, 0)
                gain[plane, j] = c_state[plane, j, own, :]
                c_state[plane, j, own, :] = value
            far_launch()

            @pl.when(has_up)
            def _():
                side_up.start()

            @pl.when(has_down)
            def _():
                side_down.start()

            @pl.when(has_up)
            def _():
                side_down.wait_recv()
                for plane, j in each_slab():
                    c_state[plane, j, above(deep), :] = side_above[plane, j]

            @pl.when(has_down)
            def _():
                side_up.wait_recv()
                for plane, j in each_slab():
                    c_state[plane, j, below(deep), :] = side_below[plane, j]

            coarse_wave(c_core)
            for plane, j in each_slab():
                leaving[plane, j] = c_state[plane, j, own, :]
            launch()

    @pl.when(has_after & ((cut == 0) | odd))
    def _():
        natural()

    @pl.when(has_before & even)
    def _():
        to_own.wait_recv()
        for plane, j in each_slab():
            gain[plane, j] = arrived[plane, j] - gain[plane, j]

    @pl.when(has_before)
    def _():
        for plane in range(planes):
            parts = relaid([gain[plane, j // 2] for j in range(tiles)])
            for t in range(tiles):
                for r in range(2):
                    spread[plane, t, pl.ds(r, coarse_count, stride=2), :] = parts[t]
            for t in range(tiles):
                at = (plane, slice(None), pl.ds(t * LANES, LANES))
                out_ref[at] = out_ref[at] + spread[plane, t]

    pl.when(has_before)(landed)
    for there, copies in (
        (has_up, rest_up), (has_down, rest_down),
        (has_after & has_up, [spill_up]), (has_after & has_down, [spill_down]),
        (has_before & has_up, [start_up]), (has_before & has_down, [start_down]),
    ):
        @pl.when(there)
        def _():
            for copy in copies:
                copy.wait_send()


def per_device(tile_count, slices, start_states):
    fields = start_states[0]
    planes, row_count, columns = fields.shape
    tiles = columns // LANES
    half = tiles // 2
    fine = line_tables(tiles, tiles, 1.0, columns, FINE_SPACING, FINE_STEP)
    coarse = line_tables(half, tiles, 2.0, columns, COARSE_SPACING, COARSE_STEP)
    fine_count = row_count + 4 * SUB
    coarse_count = row_count // 2
    c_count = coarse_count + 3 * SUB
    f32 = jnp.float32

    def vmem(*shape):
        return pltpu.VMEM(shape, f32)

    slab = vmem(planes, half, coarse_count, LANES)
    out = pl.pallas_call(
        functools.partial(kernel, tile_count, slices),
        out_shape=jax.ShapeDtypeStruct(fields.shape, f32),
        in_specs=[pl.BlockSpec(memory_space=pltpu.HBM)] * 5,
        out_specs=pl.BlockSpec(memory_space=pltpu.VMEM),
        scratch_shapes=[vmem(*fields.shape)]
        + [pltpu.VMEM(a.shape, a.dtype) for a in fine + coarse]
        + [vmem(tiles, LANES)] * 4
        + [
            vmem(planes, tiles, fine_count, LANES),
            vmem(tiles, 2 * (row_count + 2 * SUB), LANES),
            vmem(tiles, 2, fine_count, LANES),
        ]
        + [vmem(planes, tiles, SUB, LANES)] * 2
        + [slab] * 3
        + [
            vmem(planes, half, 2 * SUB, LANES),
            vmem(planes, half, c_count, LANES),
            vmem(half, 4 * SUB, LANES),
            vmem(half, 2, c_count, LANES),
            vmem(fine_count, LANES),
            vmem(tiles, fine_count, LANES),
            vmem(tiles, fine_count, LANES),
            vmem(c_count, LANES),
            vmem(half, c_count, LANES),
            vmem(half, c_count, LANES),
            vmem(planes, half, c_count, LANES),
            vmem(planes, tiles, row_count, LANES),
        ]
        + [slab] * 2
        + [vmem(planes, half, HALO[-1], LANES)] * 2
        + [slab] * 11
        + [vmem(planes, half, FAR, LANES)] * 2
        + [vmem(planes, half, HALO[-1], LANES)] * 6
        + [
            pltpu.SemaphoreType.DMA((len(fine + coarse) + planes,)),
            pltpu.SemaphoreType.DMA((22,)),
            pltpu.SemaphoreType.DMA((22,)),
            pltpu.SemaphoreType.REGULAR,
            pltpu.SemaphoreType.REGULAR,
        ],
        compiler_params=pltpu.CompilerParams(
            collective_id=0, has_side_effects=True, vmem_limit_bytes=24 * 1024 * 1024
        ),
    )(*[pltpu.with_memory_space_constraint(jnp.asarray(a), pltpu.HBM) for a in (fields,) + fine + coarse])
    return out[None]


def solution(mesh):
    spec = P("cuts", None, "tile", None)
    body = functools.partial(per_device, mesh.shape["tile"], mesh.shape["cuts"])
    return jax.shard_map(body, mesh=mesh, in_specs=(spec,), out_specs=spec, check_vma=False)
```

```python
import functools

import ml_dtypes
import numpy as np
import jax
import jax.numpy as jnp
from jax import lax
from jax.experimental import pallas as pl
from jax.experimental.pallas import tpu as pltpu
from jax.sharding import PartitionSpec as P

STEPS = 3
FINE_SPACING = 0.05
COARSE_SPACING = 0.1
FINE_STEP = 0.015
COARSE_STEP = 0.045
LANES = 128
SUB = 8
HALO = (2, 2, 3)
OWN = 2 * SUB
SPILL = 5
FAR = 2 * HALO[-1]
MESH = pl.DeviceIdType.MESH


def line_tables(tiles, fine_tiles, stride, length, spacing, step):
    groups = LANES // fine_tiles
    lane = np.arange(LANES)
    chunk = (lane % fine_tiles) * groups + lane // fine_tiles
    columns = tiles * LANES
    centers = (np.arange(columns) + 0.5) * stride
    depth = (0.9 + 0.3 * np.sin(6.0 * np.pi * centers / length)).reshape(LANES, tiles).T
    beta = depth * depth / 3.0
    b = beta / spacing**2
    mid = 1.0 + 2.0 * b
    last = tiles - 1
    inv = np.zeros_like(b)
    cp = np.zeros_like(b)
    for j in range(last):
        inv[j] = 1.0 / (mid[j] - (b[j] * cp[j - 1] if j else 0.0))
        cp[j] = b[j] * inv[j]
    run = np.ones_like(b)
    for j in range(1, tiles):
        run[j] = run[j - 1] * cp[j - 1]
    p = np.zeros_like(b)
    q = np.zeros_like(b)
    q[last] = 1.0
    for j in range(last - 1, -1, -1):
        p[j] = run[j + 1] + cp[j] * p[j + 1]
        q[j] = cp[j] * q[j + 1]
    system = np.zeros((LANES, LANES))
    for k in range(LANES):
        system[k, k] = mid[last, k] - b[last, k] * q[last - 1, k]
        if k:
            system[k, k - 1] = -b[last, k] * p[last - 1, k]
        if k + 1 < LANES:
            system[k, k] -= b[last, k] * p[0, k + 1]
            system[k, k + 1] = -b[last, k] * q[0, k + 1]
    solve = np.linalg.inv(system).T[chunk][:, chunk]
    high = solve.astype(ml_dtypes.bfloat16)
    low = (solve - high.astype(np.float64)).astype(ml_dtypes.bfloat16)
    half = np.concatenate([high, low], axis=1)
    weights = np.concatenate([half, half], axis=0)
    slope = step * depth / (2.0 * spacing)
    weight = beta / (spacing**2 + 4.0 * beta)
    inv[last] = b[last]
    rows = np.stack([inv, cp, run, slope, weight])[:, :, chunk]
    return rows.astype(np.float32), weights


def relaid(tiles):
    tiles = list(tiles)
    lane = lax.broadcasted_iota(jnp.int32, tiles[0].shape, 1)
    bit = 1
    while bit < len(tiles):
        keep = (lane & bit) == 0
        for t in range(len(tiles)):
            if t & bit == 0:
                a, b = tiles[t], tiles[t | bit]
                tiles[t] = jnp.where(keep, a, pltpu.roll(b, bit, 1))
                tiles[t | bit] = jnp.where(keep, pltpu.roll(a, LANES - bit, 1), b)
        bit *= 2
    return tiles


def wave(state, held, change, rows, weights, inside, tiles, fine_tiles, wide, core):
    factor_in, slope_in, weight_in = inside
    h0, hn = wide
    t0, tn = core
    at = pl.ds(t0, tn)

    def lane(x):
        return lax.broadcasted_iota(jnp.int32, x.shape, 1)

    def chunk_before(x):
        wrapped = jnp.where(lane(x) == 0, 0.0, pltpu.roll(x, fine_tiles + 1, 1))
        return jnp.where(lane(x) >= fine_tiles, pltpu.roll(x, fine_tiles, 1), wrapped)

    def chunk_after(x):
        wrapped = jnp.where(lane(x) == LANES - 1, 0.0, pltpu.roll(x, LANES - fine_tiles - 1, 1))
        return jnp.where(
            lane(x) < LANES - fine_tiles, pltpu.roll(x, LANES - fine_tiles, 1), wrapped
        )

    def across(load, j):
        right = load(j + 1) if j + 1 < tiles else chunk_after(load(0))
        left = load(j - 1) if j else chunk_before(load(tiles - 1))
        return right - left

    def table(kind, j):
        return rows[kind, pl.ds(j, 1), :]

    last = tiles - 1
    near = pl.ds(h0, hn)
    factor = factor_in[near, :]
    for j in range(tiles):
        along = across(lambda i: state[1, i, near, :], j)
        down = state[2, j, pl.ds(h0 + 1, hn), :] - state[2, j, pl.ds(h0 - 1, hn), :]
        state[0, j, near, :] = state[0, j, near, :] - factor * (along + down)
    def forcing(part, j):
        if part == 0:
            along = across(lambda i: state[0, i, at, :], j)
            return state[1, j, at, :] - table(3, j) * along
        down = state[0, j, pl.ds(t0 + 1, tn), :] - state[0, j, pl.ds(t0 - 1, tn), :]
        return state[2, j, at, :] - slope_in[j, at, :] * down

    solved = []
    for part in range(2):
        spot = pl.ds(part * tn, tn)
        total = None
        inner = None
        for j in range(last):
            force = forcing(part, j)
            if j == 0:
                inner = force * table(0, j)
                total = inner
            else:
                inner = force * table(0, j) + table(1, j) * inner
                total = total + table(2, j) * inner
            held[j, spot, :] = inner
        edge = forcing(part, last) + table(0, last) * (inner + chunk_after(total))
        high = edge.astype(jnp.bfloat16)
        low = (edge - high.astype(jnp.float32)).astype(jnp.bfloat16)
        solved.append(
            jnp.dot(
                jnp.concatenate([high, low], axis=1),
                weights[...],
                preferred_element_type=jnp.float32,
            )
        )
    for part in range(2):
        spot = pl.ds(part * tn, tn)
        value = solved[part][:, :LANES] + solved[part][:, LANES:]
        before = chunk_before(value)
        for j in range(last, -1, -1):
            if j < last:
                value = held[j, spot, :] + table(2, j + 1) * before + table(1, j) * value
            moved = value - state[1 + part, j, at, :]
            change[j, part, at, :] = moved
            around = change[j, part, pl.ds(t0 + 1, tn), :] + change[j, part, pl.ds(t0 - 1, tn), :]
            state[1 + part, j, at, :] = value + weight_in[j, at, :] * (around - 2.0 * moved)


def kernel(
    tile_count, slices, x_hbm, fine_rows_hbm, fine_weights_hbm, coarse_rows_hbm,
    coarse_weights_hbm, out_ref,
    x_ref, fine_rows, fine_weights, coarse_rows, coarse_weights,
    up_edge, down_edge, from_up_edge, from_down_edge, state, held, change,
    from_up, from_down, up_spill, down_spill, from_up_spill, from_down_spill,
    c_state, c_held, c_change, factor_in, slope_in, weight_in, c_factor_in, c_slope_in,
    c_weight_in, offset, spread, start, low_start, start_above, start_below,
    end, arrived, leaving, low, above_in, below_in, far_in, far_leaving, far_low, near_low, gain,
    far_above, far_below, side_above, side_below, halo_up, halo_down, halo_above, halo_below,
    local, send, recv, ready, far_ready,
):
    cut = lax.axis_index("cuts")
    tile = lax.axis_index("tile")
    has_up = tile > 0
    has_down = tile < tile_count - 1
    has_before = cut > 0
    has_after = cut < slices - 1
    odd = cut % 2 == 1
    even = jnp.logical_not(odd)
    has_far_before = odd & (cut > 1)
    has_far_after = odd & (cut < slices - 2)
    planes, row_count, columns = x_ref.shape
    tiles = columns // LANES
    half = tiles // 2
    total_rows = row_count * tile_count
    coarse_count = row_count // 2
    last = planes - 1
    tail = OWN + row_count
    lead = SUB + SUB // 2
    deep = HALO[last]

    pairs = [(fine_rows_hbm, fine_rows)]
    pairs += [(x_hbm.at[plane], x_ref.at[plane]) for plane in range(planes)]
    pairs += [
        (fine_weights_hbm, fine_weights), (coarse_rows_hbm, coarse_rows),
        (coarse_weights_hbm, coarse_weights),
    ]
    loads = [pltpu.make_async_copy(a, b, local.at[i]) for i, (a, b) in enumerate(pairs)]
    for load in loads:
        load.start()

    zero = jnp.zeros((SUB, LANES), jnp.float32)

    def each_slab():
        return [(plane, j) for plane in range(planes) for j in range(half)]

    for plane, j in each_slab():
        from_up_spill[plane, j] = zero
        from_down_spill[plane, j, pl.ds(0, SUB), :] = zero
        from_down_spill[plane, j, pl.ds(SUB, SUB), :] = zero

    right = tile % 2 == 1
    left = jnp.logical_not(right)
    pair_up, pair_down = has_up & right, has_down & left
    cross_up, cross_down = has_up & left, has_down & right

    barrier = pltpu.get_barrier_semaphore()
    beside = [(has_up, cut, tile - 1), (has_down, cut, tile + 1)]

    def in_cut(there, other):
        return [
            (there, other, tile),
            (there & has_up, other, tile - 1),
            (there & has_down, other, tile + 1),
        ]

    before = in_cut(has_before, cut - 1)
    after = in_cut(has_after, cut + 1)
    far_before = in_cut(has_far_before, cut - 2)
    far_after = in_cut(has_far_after, cut + 2)

    def signal(semaphore, devices):
        for exists, to_cut, to_tile in devices:
            @pl.when(exists)
            def _():
                pl.semaphore_signal(
                    semaphore, inc=1, device_id=(to_cut, to_tile), device_id_type=MESH
                )

    def count(devices):
        return sum(exists.astype(jnp.int32) for exists, _, _ in devices)

    signal(barrier, beside + after + far_after)

    def remote(source, target, which, to_cut, to_tile):
        return pltpu.make_async_remote_copy(
            src_ref=source, dst_ref=target, send_sem=send.at[which], recv_sem=recv.at[which],
            device_id=(to_cut, to_tile), device_id_type=MESH,
        )

    def rows_at(ref, row, count):
        return ref.at[:, :, pl.ds(row, count), :]

    spill_up = remote(
        rows_at(up_spill, 0, SPILL), rows_at(from_down_spill, SUB, SPILL), 0, cut, tile - 1
    )
    spill_down = remote(
        rows_at(down_spill, 0, SPILL), rows_at(from_up_spill, 0, SPILL), 1, cut, tile + 1
    )
    rest_up = [
        remote(rows_at(state, SUB, SUB), from_down, 2, cut, tile - 1),
        remote(up_edge, from_down_edge, 3, cut, tile - 1),
    ]
    rest_down = [
        remote(rows_at(state, tail, SUB), from_up, 4, cut, tile + 1),
        remote(down_edge, from_up_edge, 5, cut, tile + 1),
    ]
    start_up = remote(rows_at(start, 0, deep), start_below, 6, cut, tile - 1)
    start_down = remote(rows_at(low_start, 0, deep), start_above, 7, cut, tile + 1)

    for j in range(tiles):
        for row in (0, SUB, tail, tail + SUB):
            for plane in range(planes):
                state[plane, j, pl.ds(row, SUB), :] = zero
            for part in range(2):
                change[j, part, pl.ds(row, SUB), :] = zero

    def mask(total, origin, shape):
        at = lax.broadcasted_iota(jnp.int32, shape, 0) + origin
        return ((at >= 0) & (at < total)).astype(jnp.float32)

    loads[0].wait()
    inside = mask(total_rows, tile * row_count - SUB, (row_count + 2 * SUB, LANES))
    window = pl.ds(SUB, row_count + 2 * SUB)
    factor_in[window, :] = inside * (FINE_STEP / (2.0 * FINE_SPACING))
    for j in range(tiles):
        slope_in[j, window, :] = inside * fine_rows[3, pl.ds(j, 1), :]
        weight_in[j, window, :] = inside * fine_rows[4, pl.ds(j, 1), :]

    for plane in range(planes):
        loads[1 + plane].wait()
        for row in range(0, row_count, SUB):
            values = x_ref[plane, pl.ds(row, SUB), :]
            parts = relaid([values[:, t * LANES : (t + 1) * LANES] for t in range(tiles)])
            for j in range(tiles):
                state[plane, j, pl.ds(OWN + row, SUB), :] = parts[j]

    def restricted(plane, j, row, count):
        parts = [
            state[plane, 2 * j + k, pl.ds(row + r, count, stride=2), :]
            for r in range(2)
            for k in range(2)
        ]
        return 0.25 * ((parts[0] + parts[1]) + (parts[2] + parts[3]))

    @pl.when(has_before)
    def _():
        for plane, j in each_slab():
            value = restricted(plane, j, OWN, coarse_count)
            start[plane, j] = value
            low_start[plane, j] = pltpu.roll(value, deep, 0)

    pl.semaphore_wait(barrier, count(beside + before + far_before))
    signal(ready, before)
    signal(far_ready, far_before)

    @pl.when(has_before)
    def _():
        @pl.when(has_up)
        def _():
            start_up.start()

        @pl.when(has_down)
        def _():
            start_down.start()

    loads[1 + planes].wait()
    inner = (lead, row_count + SUB)
    outer = (SUB, row_count + 2 * SUB)
    for wide, core in ((inner, inner), (inner, outer), (outer, outer)):
        wave(
            state, held, change, fine_rows, fine_weights, (factor_in, slope_in, weight_in),
            tiles, tiles, wide, core,
        )
    for j in range(tiles):
        for row, near, edge in ((SUB - 1, SUB, up_edge), (tail + SUB, tail + SUB - 1, down_edge)):
            value = fine_rows[4, pl.ds(j, 1), :] * change[j, 1, pl.ds(near, 1), :]
            state[last, j, pl.ds(row, 1), :] = value
            edge[pl.ds(j, 1), :] = value

    @pl.when(has_after)
    def _():
        def spill_to_up():
            for plane, j in each_slab():
                up_spill[plane, j, pl.ds(0, SPILL), :] = restricted(
                    plane, j, OWN - 2 * SPILL, SPILL
                )
            spill_up.start()

        def spill_to_down():
            for plane, j in each_slab():
                down_spill[plane, j, pl.ds(0, SPILL), :] = restricted(plane, j, tail, SPILL)
            spill_down.start()

        pl.when(cross_up)(spill_to_up)
        pl.when(cross_down)(spill_to_down)
        pl.when(pair_up)(spill_to_up)
        pl.when(pair_down)(spill_to_down)

    def pass_rest():
        @pl.when(has_up)
        def _():
            for copy in rest_up:
                copy.start()

        @pl.when(has_down)
        def _():
            for copy in rest_down:
                copy.start()

    pl.when(jnp.logical_not(has_after))(pass_rest)
    for load in loads[2 + planes :]:
        load.wait()

    first_part = (pl.ds(0, last), slice(None), pl.ds(0, HALO[0]))
    last_part = (last, slice(None), pl.ds(0, HALO[last]))
    to_own = remote(leaving, arrived, 8, cut + 1, tile)
    to_above = [
        remote(leaving.at[part], below_in.at[part], 9 + i, cut + 1, tile - 1)
        for i, part in enumerate((first_part, last_part))
    ]
    to_below = [
        remote(low.at[part], above_in.at[part], 11 + i, cut + 1, tile + 1)
        for i, part in enumerate((first_part, last_part))
    ]

    far_own = remote(far_leaving, far_in, 13, cut + 2, tile)
    far_up = remote(rows_at(far_leaving, 0, FAR), far_below, 14, cut + 2, tile - 1)
    far_down = remote(rows_at(far_low, 0, FAR), far_above, 15, cut + 2, tile + 1)

    near_up = remote(rows_at(far_in, 0, FAR), far_below, 20, cut, tile - 1)
    near_down = remote(rows_at(near_low, 0, FAR), far_above, 21, cut, tile + 1)
    side_up = remote(rows_at(far_leaving, 0, deep), side_below, 16, cut, tile - 1)
    side_down = remote(rows_at(low, 0, deep), side_above, 17, cut, tile + 1)

    def far_launch():
        @pl.when(has_far_after & cross_up)
        def _():
            far_up.start()

        @pl.when(has_far_after & cross_down)
        def _():
            far_down.start()

    def leave(plane, j, value):
        leaving[plane, j] = value
        low[plane, j] = pltpu.roll(value, HALO[plane], 0)

    first = cut == 0
    first_own = remote(far_leaving, arrived, 8, cut + 1, tile)
    first_halos = [
        remote(halo_up, halo_above, 18, cut + 1, tile),
        remote(halo_down, halo_below, 19, cut + 1, tile),
    ]

    def launch_edges():
        pl.semaphore_wait(ready, count(after))

        @pl.when(has_after & even & has_up)
        def _():
            for copy in to_above:
                copy.start()

        @pl.when(has_after & even & has_down)
        def _():
            for copy in to_below:
                copy.start()

    def launch():
        launch_edges()

        @pl.when(has_after)
        def _():
            to_own.start()

    def landed():
        for there, copies in (
            (has_after & even & has_up, to_above), (has_after & even & has_down, to_below),
            (has_before & has_after, [to_own]),
            (has_far_after & cross_up, [far_up]), (has_far_after & cross_down, [far_down]),
            (has_far_before & pair_up, [near_up]), (has_far_before & pair_down, [near_down]),
            (has_far_after, [far_own]),
            (odd & has_after & has_up, [side_up]), (odd & has_after & has_down, [side_down]),
        ):
            @pl.when(there)
            def _():
                for copy in copies:
                    copy.wait_send()

    def natural():
        for has, copies, into, edges, row, at in (
            (has_up, rest_down, from_up, from_up_edge, OWN, OWN + SUB),
            (has_down, rest_up, from_down, from_down_edge, tail - SUB, tail - SUB - 1),
        ):
            @pl.when(has)
            def _():
                for copy in copies:
                    copy.wait_recv()
                for j in range(tiles):
                    for plane in range(planes):
                        rows = pl.ds(row, SUB)
                        state[plane, j, rows, :] = state[plane, j, rows, :] + into[plane, j]
                for j in range(tiles):
                    one = pl.ds(at, 1)
                    state[last, j, one, :] = state[last, j, one, :] + edges[pl.ds(j, 1), :]

        for plane in range(planes):
            for row in range(0, row_count, SUB):
                parts = relaid([state[plane, j, pl.ds(OWN + row, SUB), :] for j in range(tiles)])
                for t in range(tiles):
                    out_ref[plane, pl.ds(row, SUB), pl.ds(t * LANES, LANES)] = parts[t]

    @pl.when(has_after)
    def _():
        for plane, j in each_slab():
            end[plane, j] = restricted(plane, j, OWN, coarse_count)

        @pl.when(first)
        def _():
            for plane, j in each_slab():
                leave(plane, j, end[plane, j])
                halo_up[plane, j] = restricted(plane, j, OWN - 2 * deep, deep)
                halo_down[plane, j] = restricted(plane, j, tail, deep)
            launch_edges()
            for copy in first_halos:
                copy.start()

        @pl.when(has_up)
        def _():
            spill_down.wait_recv()

        @pl.when(has_down)
        def _():
            spill_up.wait_recv()

        for plane, j in each_slab():
            value = (
                end[plane, j]
                + from_up_spill[plane, j]
                + from_down_spill[plane, j, pl.ds(SPILL, SUB), :]
            )
            end[plane, j] = value
            far_leaving[plane, j] = value

    pl.when(has_before & has_after)(pass_rest)

    @pl.when(cut == 0)
    def _():
        first_own.start()
        for copy in first_halos + [first_own]:
            copy.wait_send()
        landed()
        pass_rest()

    own = pl.ds(lead, coarse_count)
    c_core = (SUB, 2 * SUB)

    def above(size):
        return pl.ds(lead - size, size)

    def below(size):
        return pl.ds(lead + coarse_count, size)

    def coarse_wave(wide):
        wave(
            c_state, c_held, c_change, coarse_rows, coarse_weights,
            (c_factor_in, c_slope_in, c_weight_in), half, tiles, wide, c_core,
        )

    @pl.when(has_before)
    def _():
        c_wide = pl.ds(SUB // 2, 3 * SUB)
        c_window = pl.ds(SUB, 2 * SUB)
        origin = tile * coarse_count - lead
        c_inside = mask(total_rows // 2, origin + SUB // 2, (3 * SUB, LANES))
        c_factor_in[c_wide, :] = c_inside * (COARSE_STEP / (2.0 * COARSE_SPACING))
        c_inside = mask(total_rows // 2, origin + SUB, (2 * SUB, LANES))
        for j in range(half):
            c_slope_in[j, c_window, :] = c_inside * coarse_rows[3, pl.ds(j, 1), :]
            c_weight_in[j, c_window, :] = c_inside * coarse_rows[4, pl.ds(j, 1), :]
            for row in range(0, 4 * SUB, SUB):
                for plane in range(planes):
                    c_state[plane, j, pl.ds(row, SUB), :] = zero
                for part in range(2):
                    c_change[j, part, pl.ds(row, SUB), :] = zero

        @pl.when(has_up)
        def _():
            start_down.wait_recv()

        @pl.when(has_down)
        def _():
            start_up.wait_recv()

    @pl.when(has_before & even)
    def _():
        @pl.when(has_up)
        def _():
            for plane, j in each_slab():
                c_state[plane, j, above(deep), :] = start_above[plane, j]

        @pl.when(has_down)
        def _():
            for plane, j in each_slab():
                c_state[plane, j, below(deep), :] = start_below[plane, j]

        for plane, j in each_slab():
            c_state[plane, j, own, :] = start[plane, j]
        coarse_wave(c_core)
        for plane, j in each_slab():
            gain[plane, j] = c_state[plane, j, own, :]

        @pl.when(has_after)
        def _():
            for plane, j in each_slab():
                leave(plane, j, end[plane, j] - gain[plane, j])
            launch()

    @pl.when((has_before & even) | jnp.logical_not(has_after))
    def _():
        natural()

    def joined(place, extra_above=lambda: None, extra_below=lambda: None):
        @pl.when(has_up)
        def _():
            for copy in to_below:
                copy.wait_recv()
            for plane, j in each_slab():
                size = HALO[plane]
                place(
                    plane, j, above(size),
                    above_in[plane, j, pl.ds(0, size), :]
                    - start_above[plane, j, pl.ds(deep - size, size), :],
                )
            extra_above()

        @pl.when(has_down)
        def _():
            for copy in to_above:
                copy.wait_recv()
            for plane, j in each_slab():
                size = HALO[plane]
                place(
                    plane, j, below(size),
                    below_in[plane, j, pl.ds(0, size), :]
                    - start_below[plane, j, pl.ds(0, size), :],
                )
            extra_below()

        to_own.wait_recv()
        for plane, j in each_slab():
            place(plane, j, own, arrived[plane, j] - start[plane, j])

    @pl.when(cut == 1)
    def _():
        def place(plane, j, rows, value):
            c_state[plane, j, rows, :] = value

        def widen(rows, halo, skip):
            for plane, j in each_slab():
                count = HALO[plane]
                at = rows(count)
                c_state[plane, j, at, :] = (
                    c_state[plane, j, at, :] + halo[plane, j, pl.ds(skip(count), count), :]
                )

        for copy in first_halos:
            copy.wait_recv()
        joined(place, lambda: (
            widen(above, halo_above, lambda count: deep - count),
        ), lambda: (
            widen(below, halo_below, lambda count: 0),
        ))

    @pl.when(has_far_before)
    def _():
        def hold(plane, j, rows, value):
            offset[plane, j, rows, :] = value

        def add(plane, j, rows):
            c_state[plane, j, rows, :] = c_state[plane, j, rows, :] + offset[plane, j, rows, :]

        joined(hold)
        far_own.wait_recv()

        @pl.when(pair_up)
        def _():
            near_up.start()

        @pl.when(pair_down)
        def _():
            for plane, j in each_slab():
                near_low[plane, j] = pltpu.roll(far_in[plane, j], FAR, 0)
            near_down.start()

        for plane, j in each_slab():
            c_state[plane, j, own, :] = far_in[plane, j]

        @pl.when(cross_up)
        def _():
            far_down.wait_recv()

        @pl.when(cross_down)
        def _():
            far_up.wait_recv()

        @pl.when(pair_up)
        def _():
            near_down.wait_recv()

        @pl.when(pair_down)
        def _():
            near_up.wait_recv()

        @pl.when(has_up)
        def _():
            for plane, j in each_slab():
                c_state[plane, j, above(FAR), :] = far_above[plane, j]

        @pl.when(has_down)
        def _():
            for plane, j in each_slab():
                c_state[plane, j, below(FAR), :] = far_below[plane, j]

        coarse_wave((SUB // 2, 3 * SUB))

        @pl.when(has_up)
        def _():
            for plane, j in each_slab():
                add(plane, j, above(HALO[plane]))

        @pl.when(has_down)
        def _():
            for plane, j in each_slab():
                add(plane, j, below(HALO[plane]))

        for plane, j in each_slab():
            add(plane, j, own)

    @pl.when(odd)
    def _():
        coarse_wave(c_core)

        @pl.when(jnp.logical_not(has_after))
        def _():
            for plane, j in each_slab():
                gain[plane, j] = c_state[plane, j, own, :]

        @pl.when(has_after)
        def _():
            for plane, j in each_slab():
                far_leaving[plane, j] = c_state[plane, j, own, :] + end[plane, j]
            pl.semaphore_wait(far_ready, count(far_after))

            @pl.when(has_far_after)
            def _():
                far_own.start()

            for plane, j in each_slab():
                value = far_leaving[plane, j]
                far_low[plane, j] = pltpu.roll(value, FAR, 0)
                low[plane, j] = pltpu.roll(value, deep, 0)
                gain[plane, j] = c_state[plane, j, own, :]
                c_state[plane, j, own, :] = value
            far_launch()

            for there, copy in (
                (cross_up, side_up), (cross_down, side_down),
                (pair_up, side_up), (pair_down, side_down),
            ):
                pl.when(there)(copy.start)

            @pl.when(has_up)
            def _():
                side_down.wait_recv()
                for plane, j in each_slab():
                    c_state[plane, j, above(deep), :] = side_above[plane, j]

            @pl.when(has_down)
            def _():
                side_up.wait_recv()
                for plane, j in each_slab():
                    c_state[plane, j, below(deep), :] = side_below[plane, j]

            coarse_wave(c_core)
            for plane, j in each_slab():
                leaving[plane, j] = c_state[plane, j, own, :]
            launch()

    @pl.when(has_after & ((cut == 0) | odd))
    def _():
        natural()

    @pl.when(has_before & even)
    def _():
        to_own.wait_recv()
        for plane, j in each_slab():
            gain[plane, j] = arrived[plane, j] - gain[plane, j]

    @pl.when(has_before)
    def _():
        for plane in range(planes):
            parts = relaid([gain[plane, j // 2] for j in range(tiles)])
            for t in range(tiles):
                for r in range(2):
                    spread[plane, t, pl.ds(r, coarse_count, stride=2), :] = parts[t]
            for t in range(tiles):
                at = (plane, slice(None), pl.ds(t * LANES, LANES))
                out_ref[at] = out_ref[at] + spread[plane, t]

    pl.when(has_before)(landed)
    for there, copies in (
        (has_up, rest_up), (has_down, rest_down),
        (has_after & has_up, [spill_up]), (has_after & has_down, [spill_down]),
        (has_before & has_up, [start_up]), (has_before & has_down, [start_down]),
    ):
        @pl.when(there)
        def _():
            for copy in copies:
                copy.wait_send()


def per_device(tile_count, slices, start_states):
    fields = start_states[0]
    planes, row_count, columns = fields.shape
    tiles = columns // LANES
    half = tiles // 2
    fine = line_tables(tiles, tiles, 1.0, columns, FINE_SPACING, FINE_STEP)
    coarse = line_tables(half, tiles, 2.0, columns, COARSE_SPACING, COARSE_STEP)
    fine_count = row_count + 4 * SUB
    coarse_count = row_count // 2
    c_count = coarse_count + 3 * SUB
    f32 = jnp.float32

    def vmem(*shape):
        return pltpu.VMEM(shape, f32)

    slab = vmem(planes, half, coarse_count, LANES)
    out = pl.pallas_call(
        functools.partial(kernel, tile_count, slices),
        out_shape=jax.ShapeDtypeStruct(fields.shape, f32),
        in_specs=[pl.BlockSpec(memory_space=pltpu.HBM)] * 5,
        out_specs=pl.BlockSpec(memory_space=pltpu.VMEM),
        scratch_shapes=[vmem(*fields.shape)]
        + [pltpu.VMEM(a.shape, a.dtype) for a in fine + coarse]
        + [vmem(tiles, LANES)] * 4
        + [
            vmem(planes, tiles, fine_count, LANES),
            vmem(tiles, 2 * (row_count + 2 * SUB), LANES),
            vmem(tiles, 2, fine_count, LANES),
        ]
        + [vmem(planes, tiles, SUB, LANES)] * 2
        + [slab] * 3
        + [
            vmem(planes, half, 2 * SUB, LANES),
            vmem(planes, half, c_count, LANES),
            vmem(half, 4 * SUB, LANES),
            vmem(half, 2, c_count, LANES),
            vmem(fine_count, LANES),
            vmem(tiles, fine_count, LANES),
            vmem(tiles, fine_count, LANES),
            vmem(c_count, LANES),
            vmem(half, c_count, LANES),
            vmem(half, c_count, LANES),
            vmem(planes, half, c_count, LANES),
            vmem(planes, tiles, row_count, LANES),
        ]
        + [slab] * 2
        + [vmem(planes, half, HALO[-1], LANES)] * 2
        + [slab] * 11
        + [vmem(planes, half, FAR, LANES)] * 2
        + [vmem(planes, half, HALO[-1], LANES)] * 6
        + [
            pltpu.SemaphoreType.DMA((len(fine + coarse) + planes,)),
            pltpu.SemaphoreType.DMA((22,)),
            pltpu.SemaphoreType.DMA((22,)),
            pltpu.SemaphoreType.REGULAR,
            pltpu.SemaphoreType.REGULAR,
        ],
        compiler_params=pltpu.CompilerParams(
            collective_id=0, has_side_effects=True, vmem_limit_bytes=24 * 1024 * 1024
        ),
    )(*[pltpu.with_memory_space_constraint(jnp.asarray(a), pltpu.HBM) for a in (fields,) + fine + coarse])
    return out[None]


def solution(mesh):
    spec = P("cuts", None, "tile", None)
    body = functools.partial(per_device, mesh.shape["tile"], mesh.shape["cuts"])
    return jax.shard_map(body, mesh=mesh, in_specs=(spec,), out_specs=spec, check_vma=False)
```

```python
import functools

import ml_dtypes
import numpy as np
import jax
import jax.numpy as jnp
from jax import lax
from jax.experimental import pallas as pl
from jax.experimental.pallas import tpu as pltpu
from jax.sharding import PartitionSpec as P

STEPS = 3
FINE_SPACING = 0.05
COARSE_SPACING = 0.1
FINE_STEP = 0.015
COARSE_STEP = 0.045
LANES = 128
SUB = 8
HALO = (2, 2, 3)
OWN = 2 * SUB
SPILL = 5
FAR = 2 * HALO[-1]
MESH = pl.DeviceIdType.MESH


def line_tables(tiles, fine_tiles, stride, length, spacing, step):
    groups = LANES // fine_tiles
    lane = np.arange(LANES)
    chunk = (lane % fine_tiles) * groups + lane // fine_tiles
    columns = tiles * LANES
    centers = (np.arange(columns) + 0.5) * stride
    depth = (0.9 + 0.3 * np.sin(6.0 * np.pi * centers / length)).reshape(LANES, tiles).T
    beta = depth * depth / 3.0
    b = beta / spacing**2
    mid = 1.0 + 2.0 * b
    last = tiles - 1
    inv = np.zeros_like(b)
    cp = np.zeros_like(b)
    for j in range(last):
        inv[j] = 1.0 / (mid[j] - (b[j] * cp[j - 1] if j else 0.0))
        cp[j] = b[j] * inv[j]
    run = np.ones_like(b)
    for j in range(1, tiles):
        run[j] = run[j - 1] * cp[j - 1]
    p = np.zeros_like(b)
    q = np.zeros_like(b)
    q[last] = 1.0
    for j in range(last - 1, -1, -1):
        p[j] = run[j + 1] + cp[j] * p[j + 1]
        q[j] = cp[j] * q[j + 1]
    system = np.zeros((LANES, LANES))
    for k in range(LANES):
        system[k, k] = mid[last, k] - b[last, k] * q[last - 1, k]
        if k:
            system[k, k - 1] = -b[last, k] * p[last - 1, k]
        if k + 1 < LANES:
            system[k, k] -= b[last, k] * p[0, k + 1]
            system[k, k + 1] = -b[last, k] * q[0, k + 1]
    solve = np.linalg.inv(system).T[chunk][:, chunk]
    high = solve.astype(ml_dtypes.bfloat16)
    low = (solve - high.astype(np.float64)).astype(ml_dtypes.bfloat16)
    half = np.concatenate([high, low], axis=1)
    weights = np.concatenate([half, half], axis=0)
    slope = step * depth / (2.0 * spacing)
    weight = beta / (spacing**2 + 4.0 * beta)
    inv[last] = b[last]
    rows = np.stack([inv, cp, run, slope, weight])[:, :, chunk]
    return rows.astype(np.float32), weights


def relaid(tiles):
    tiles = list(tiles)
    lane = lax.broadcasted_iota(jnp.int32, tiles[0].shape, 1)
    bit = 1
    while bit < len(tiles):
        keep = (lane & bit) == 0
        for t in range(len(tiles)):
            if t & bit == 0:
                a, b = tiles[t], tiles[t | bit]
                tiles[t] = jnp.where(keep, a, pltpu.roll(b, bit, 1))
                tiles[t | bit] = jnp.where(keep, pltpu.roll(a, LANES - bit, 1), b)
        bit *= 2
    return tiles


def wave(state, held, change, rows, weights, inside, tiles, fine_tiles, wide, core):
    factor_in, slope_in, weight_in = inside
    h0, hn = wide
    t0, tn = core
    at = pl.ds(t0, tn)

    def lane(x):
        return lax.broadcasted_iota(jnp.int32, x.shape, 1)

    def chunk_before(x):
        wrapped = jnp.where(lane(x) == 0, 0.0, pltpu.roll(x, fine_tiles + 1, 1))
        return jnp.where(lane(x) >= fine_tiles, pltpu.roll(x, fine_tiles, 1), wrapped)

    def chunk_after(x):
        wrapped = jnp.where(lane(x) == LANES - 1, 0.0, pltpu.roll(x, LANES - fine_tiles - 1, 1))
        return jnp.where(
            lane(x) < LANES - fine_tiles, pltpu.roll(x, LANES - fine_tiles, 1), wrapped
        )

    def across(load, j):
        right = load(j + 1) if j + 1 < tiles else chunk_after(load(0))
        left = load(j - 1) if j else chunk_before(load(tiles - 1))
        return right - left

    def table(kind, j):
        return rows[kind, pl.ds(j, 1), :]

    last = tiles - 1
    near = pl.ds(h0, hn)
    factor = factor_in[near, :]
    for j in range(tiles):
        along = across(lambda i: state[1, i, near, :], j)
        down = state[2, j, pl.ds(h0 + 1, hn), :] - state[2, j, pl.ds(h0 - 1, hn), :]
        state[0, j, near, :] = state[0, j, near, :] - factor * (along + down)
    def forcing(part, j):
        if part == 0:
            along = across(lambda i: state[0, i, at, :], j)
            return state[1, j, at, :] - table(3, j) * along
        down = state[0, j, pl.ds(t0 + 1, tn), :] - state[0, j, pl.ds(t0 - 1, tn), :]
        return state[2, j, at, :] - slope_in[j, at, :] * down

    solved = []
    for part in range(2):
        spot = pl.ds(part * tn, tn)
        total = None
        inner = None
        for j in range(last):
            force = forcing(part, j)
            if j == 0:
                inner = force * table(0, j)
                total = inner
            else:
                inner = force * table(0, j) + table(1, j) * inner
                total = total + table(2, j) * inner
            held[j, spot, :] = inner
        edge = forcing(part, last) + table(0, last) * (inner + chunk_after(total))
        high = edge.astype(jnp.bfloat16)
        low = (edge - high.astype(jnp.float32)).astype(jnp.bfloat16)
        solved.append(
            jnp.dot(
                jnp.concatenate([high, low], axis=1),
                weights[...],
                preferred_element_type=jnp.float32,
            )
        )
    for part in range(2):
        spot = pl.ds(part * tn, tn)
        value = solved[part][:, :LANES] + solved[part][:, LANES:]
        before = chunk_before(value)
        for j in range(last, -1, -1):
            if j < last:
                value = held[j, spot, :] + table(2, j + 1) * before + table(1, j) * value
            moved = value - state[1 + part, j, at, :]
            change[j, part, at, :] = moved
            around = change[j, part, pl.ds(t0 + 1, tn), :] + change[j, part, pl.ds(t0 - 1, tn), :]
            state[1 + part, j, at, :] = value + weight_in[j, at, :] * (around - 2.0 * moved)


def kernel(
    tile_count, slices, x_hbm, fine_rows_hbm, fine_weights_hbm, coarse_rows_hbm,
    coarse_weights_hbm, out_ref,
    x_ref, fine_rows, fine_weights, coarse_rows, coarse_weights,
    up_edge, down_edge, from_up_edge, from_down_edge, state, held, change,
    from_up, from_down, up_spill, down_spill, from_up_spill, from_down_spill,
    c_state, c_held, c_change, factor_in, slope_in, weight_in, c_factor_in, c_slope_in,
    c_weight_in, offset, spread, start, low_start, start_above, start_below,
    end, arrived, leaving, low, above_in, below_in, far_in, far_leaving, far_low, near_low, gain,
    far_above, far_below, side_above, side_below, halo_up, halo_down, halo_above, halo_below,
    local, send, recv, ready, far_ready,
):
    cut = lax.axis_index("cuts")
    tile = lax.axis_index("tile")
    has_up = tile > 0
    has_down = tile < tile_count - 1
    has_before = cut > 0
    has_after = cut < slices - 1
    odd = cut % 2 == 1
    even = jnp.logical_not(odd)
    has_far_before = odd & (cut > 1)
    has_far_after = odd & (cut < slices - 2)
    planes, row_count, columns = x_ref.shape
    tiles = columns // LANES
    half = tiles // 2
    total_rows = row_count * tile_count
    coarse_count = row_count // 2
    last = planes - 1
    tail = OWN + row_count
    lead = SUB + SUB // 2
    deep = HALO[last]

    pairs = [(fine_rows_hbm, fine_rows)]
    pairs += [(x_hbm.at[plane], x_ref.at[plane]) for plane in range(planes)]
    pairs += [
        (fine_weights_hbm, fine_weights), (coarse_rows_hbm, coarse_rows),
        (coarse_weights_hbm, coarse_weights),
    ]
    loads = [pltpu.make_async_copy(a, b, local.at[i]) for i, (a, b) in enumerate(pairs)]
    for load in loads:
        load.start()

    zero = jnp.zeros((SUB, LANES), jnp.float32)

    def each_slab():
        return [(plane, j) for plane in range(planes) for j in range(half)]

    for plane, j in each_slab():
        from_up_spill[plane, j] = zero
        from_down_spill[plane, j, pl.ds(0, SUB), :] = zero
        from_down_spill[plane, j, pl.ds(SUB, SUB), :] = zero

    right = tile % 2 == 1
    left = jnp.logical_not(right)
    pair_up, pair_down = has_up & right, has_down & left
    cross_up, cross_down = has_up & left, has_down & right

    barrier = pltpu.get_barrier_semaphore()
    beside = [(has_up, cut, tile - 1), (has_down, cut, tile + 1)]

    def in_cut(there, other):
        return [
            (there, other, tile),
            (there & has_up, other, tile - 1),
            (there & has_down, other, tile + 1),
        ]

    before = in_cut(has_before, cut - 1)
    after = in_cut(has_after, cut + 1)
    far_before = in_cut(has_far_before, cut - 2)
    far_after = in_cut(has_far_after, cut + 2)

    def signal(semaphore, devices):
        for exists, to_cut, to_tile in devices:
            @pl.when(exists)
            def _():
                pl.semaphore_signal(
                    semaphore, inc=1, device_id=(to_cut, to_tile), device_id_type=MESH
                )

    def count(devices):
        return sum(exists.astype(jnp.int32) for exists, _, _ in devices)

    signal(barrier, beside + after + far_after)

    def remote(source, target, which, to_cut, to_tile):
        return pltpu.make_async_remote_copy(
            src_ref=source, dst_ref=target, send_sem=send.at[which], recv_sem=recv.at[which],
            device_id=(to_cut, to_tile), device_id_type=MESH,
        )

    def rows_at(ref, row, count):
        return ref.at[:, :, pl.ds(row, count), :]

    spill_up = remote(
        rows_at(up_spill, 0, SPILL), rows_at(from_down_spill, SUB, SPILL), 0, cut, tile - 1
    )
    spill_down = remote(
        rows_at(down_spill, 0, SPILL), rows_at(from_up_spill, 0, SPILL), 1, cut, tile + 1
    )
    rest_up = [
        remote(rows_at(state, SUB, SUB), from_down, 2, cut, tile - 1),
        remote(up_edge, from_down_edge, 3, cut, tile - 1),
    ]
    rest_down = [
        remote(rows_at(state, tail, SUB), from_up, 4, cut, tile + 1),
        remote(down_edge, from_up_edge, 5, cut, tile + 1),
    ]
    start_up = remote(rows_at(start, 0, deep), start_below, 6, cut, tile - 1)
    start_down = remote(rows_at(low_start, 0, deep), start_above, 7, cut, tile + 1)

    for j in range(tiles):
        for row in (0, SUB, tail, tail + SUB):
            for plane in range(planes):
                state[plane, j, pl.ds(row, SUB), :] = zero
            for part in range(2):
                change[j, part, pl.ds(row, SUB), :] = zero

    def mask(total, origin, shape):
        at = lax.broadcasted_iota(jnp.int32, shape, 0) + origin
        return ((at >= 0) & (at < total)).astype(jnp.float32)

    loads[0].wait()
    inside = mask(total_rows, tile * row_count - SUB, (row_count + 2 * SUB, LANES))
    window = pl.ds(SUB, row_count + 2 * SUB)
    factor_in[window, :] = inside * (FINE_STEP / (2.0 * FINE_SPACING))
    for j in range(tiles):
        slope_in[j, window, :] = inside * fine_rows[3, pl.ds(j, 1), :]
        weight_in[j, window, :] = inside * fine_rows[4, pl.ds(j, 1), :]

    for plane in range(planes):
        loads[1 + plane].wait()
        for row in range(0, row_count, SUB):
            values = x_ref[plane, pl.ds(row, SUB), :]
            parts = relaid([values[:, t * LANES : (t + 1) * LANES] for t in range(tiles)])
            for j in range(tiles):
                state[plane, j, pl.ds(OWN + row, SUB), :] = parts[j]

    def restricted(plane, j, row, count):
        parts = [
            state[plane, 2 * j + k, pl.ds(row + r, count, stride=2), :]
            for r in range(2)
            for k in range(2)
        ]
        return 0.25 * ((parts[0] + parts[1]) + (parts[2] + parts[3]))

    @pl.when(has_before)
    def _():
        for plane, j in each_slab():
            value = restricted(plane, j, OWN, coarse_count)
            start[plane, j] = value
            low_start[plane, j] = pltpu.roll(value, deep, 0)

    pl.semaphore_wait(barrier, count(beside + before + far_before))
    signal(ready, before)
    signal(far_ready, far_before)

    @pl.when(has_before)
    def _():
        @pl.when(has_up)
        def _():
            start_up.start()

        @pl.when(has_down)
        def _():
            start_down.start()

    loads[1 + planes].wait()
    inner = (lead, row_count + SUB)
    outer = (SUB, row_count + 2 * SUB)
    for wide, core in ((inner, inner), (inner, outer), (outer, outer)):
        wave(
            state, held, change, fine_rows, fine_weights, (factor_in, slope_in, weight_in),
            tiles, tiles, wide, core,
        )
    for j in range(tiles):
        for row, near, edge in ((SUB - 1, SUB, up_edge), (tail + SUB, tail + SUB - 1, down_edge)):
            value = fine_rows[4, pl.ds(j, 1), :] * change[j, 1, pl.ds(near, 1), :]
            state[last, j, pl.ds(row, 1), :] = value
            edge[pl.ds(j, 1), :] = value

    @pl.when(has_after)
    def _():
        def spill_to_up():
            for plane, j in each_slab():
                up_spill[plane, j, pl.ds(0, SPILL), :] = restricted(
                    plane, j, OWN - 2 * SPILL, SPILL
                )
            spill_up.start()

        def spill_to_down():
            for plane, j in each_slab():
                down_spill[plane, j, pl.ds(0, SPILL), :] = restricted(plane, j, tail, SPILL)
            spill_down.start()

        pl.when(cross_up)(spill_to_up)
        pl.when(cross_down)(spill_to_down)
        pl.when(pair_up)(spill_to_up)
        pl.when(pair_down)(spill_to_down)

    def pass_rest():
        @pl.when(has_up)
        def _():
            for copy in rest_up:
                copy.start()

        @pl.when(has_down)
        def _():
            for copy in rest_down:
                copy.start()

    pl.when(jnp.logical_not(has_after))(pass_rest)
    for load in loads[2 + planes :]:
        load.wait()

    first_part = (pl.ds(0, last), slice(None), pl.ds(0, HALO[0]))
    last_part = (last, slice(None), pl.ds(0, HALO[last]))
    to_own = remote(leaving, arrived, 8, cut + 1, tile)
    to_above = [
        remote(leaving.at[part], below_in.at[part], 9 + i, cut + 1, tile - 1)
        for i, part in enumerate((first_part, last_part))
    ]
    to_below = [
        remote(low.at[part], above_in.at[part], 11 + i, cut + 1, tile + 1)
        for i, part in enumerate((first_part, last_part))
    ]

    far_own = remote(far_leaving, far_in, 13, cut + 2, tile)
    far_up = remote(rows_at(far_leaving, 0, FAR), far_below, 14, cut + 2, tile - 1)
    far_down = remote(rows_at(far_low, 0, FAR), far_above, 15, cut + 2, tile + 1)

    near_up = remote(rows_at(far_in, 0, FAR), far_below, 20, cut, tile - 1)
    near_down = remote(rows_at(near_low, 0, FAR), far_above, 21, cut, tile + 1)
    side_up = remote(rows_at(far_leaving, 0, deep), side_below, 16, cut, tile - 1)
    side_down = remote(rows_at(low, 0, deep), side_above, 17, cut, tile + 1)

    def far_launch():
        @pl.when(has_far_after & cross_up)
        def _():
            far_up.start()

        @pl.when(has_far_after & cross_down)
        def _():
            far_down.start()

    def leave(plane, j, value):
        leaving[plane, j] = value
        low[plane, j] = pltpu.roll(value, HALO[plane], 0)

    first = cut == 0
    first_own = remote(far_leaving, arrived, 8, cut + 1, tile)
    first_halos = [
        remote(halo_up, halo_above, 18, cut + 1, tile),
        remote(halo_down, halo_below, 19, cut + 1, tile),
    ]

    def launch_edges():
        pl.semaphore_wait(ready, count(after))

        @pl.when(has_after & even & has_up)
        def _():
            for copy in to_above:
                copy.start()

        @pl.when(has_after & even & has_down)
        def _():
            for copy in to_below:
                copy.start()

    def launch():
        launch_edges()

        @pl.when(has_after)
        def _():
            to_own.start()

    def landed():
        for there, copies in (
            (has_after & even & has_up, to_above), (has_after & even & has_down, to_below),
            (has_before & has_after, [to_own]),
            (has_far_after & cross_up, [far_up]), (has_far_after & cross_down, [far_down]),
            (has_far_before & pair_up, [near_up]), (has_far_before & pair_down, [near_down]),
            (has_far_after, [far_own]),
            (odd & has_after & has_up, [side_up]), (odd & has_after & has_down, [side_down]),
        ):
            @pl.when(there)
            def _():
                for copy in copies:
                    copy.wait_send()

    def natural():
        for has, copies, into, edges, row, at in (
            (has_up, rest_down, from_up, from_up_edge, OWN, OWN + SUB),
            (has_down, rest_up, from_down, from_down_edge, tail - SUB, tail - SUB - 1),
        ):
            @pl.when(has)
            def _():
                for copy in copies:
                    copy.wait_recv()
                for j in range(tiles):
                    for plane in range(planes):
                        rows = pl.ds(row, SUB)
                        state[plane, j, rows, :] = state[plane, j, rows, :] + into[plane, j]
                for j in range(tiles):
                    one = pl.ds(at, 1)
                    state[last, j, one, :] = state[last, j, one, :] + edges[pl.ds(j, 1), :]

        for plane in range(planes):
            for row in range(0, row_count, SUB):
                parts = relaid([state[plane, j, pl.ds(OWN + row, SUB), :] for j in range(tiles)])
                for t in range(tiles):
                    out_ref[plane, pl.ds(row, SUB), pl.ds(t * LANES, LANES)] = parts[t]

    @pl.when(has_after)
    def _():
        for plane, j in each_slab():
            end[plane, j] = restricted(plane, j, OWN, coarse_count)

        @pl.when(first)
        def _():
            for plane, j in each_slab():
                leave(plane, j, end[plane, j])
                halo_up[plane, j] = restricted(plane, j, OWN - 2 * deep, deep)
                halo_down[plane, j] = restricted(plane, j, tail, deep)
            launch_edges()
            for copy in first_halos:
                copy.start()

        @pl.when(has_up)
        def _():
            spill_down.wait_recv()

        @pl.when(has_down)
        def _():
            spill_up.wait_recv()

        for plane, j in each_slab():
            value = (
                end[plane, j]
                + from_up_spill[plane, j]
                + from_down_spill[plane, j, pl.ds(SPILL, SUB), :]
            )
            end[plane, j] = value
            far_leaving[plane, j] = value

    pl.when(has_before & has_after)(pass_rest)

    @pl.when(cut == 0)
    def _():
        first_own.start()
        for copy in first_halos + [first_own]:
            copy.wait_send()
        landed()
        pass_rest()

    own = pl.ds(lead, coarse_count)
    c_core = (SUB, 2 * SUB)

    def above(size):
        return pl.ds(lead - size, size)

    def below(size):
        return pl.ds(lead + coarse_count, size)

    def coarse_wave(wide):
        wave(
            c_state, c_held, c_change, coarse_rows, coarse_weights,
            (c_factor_in, c_slope_in, c_weight_in), half, tiles, wide, c_core,
        )

    @pl.when(has_before)
    def _():
        c_wide = pl.ds(SUB // 2, 3 * SUB)
        c_window = pl.ds(SUB, 2 * SUB)
        origin = tile * coarse_count - lead
        c_inside = mask(total_rows // 2, origin + SUB // 2, (3 * SUB, LANES))
        c_factor_in[c_wide, :] = c_inside * (COARSE_STEP / (2.0 * COARSE_SPACING))
        c_inside = mask(total_rows // 2, origin + SUB, (2 * SUB, LANES))
        for j in range(half):
            c_slope_in[j, c_window, :] = c_inside * coarse_rows[3, pl.ds(j, 1), :]
            c_weight_in[j, c_window, :] = c_inside * coarse_rows[4, pl.ds(j, 1), :]
            for row in range(0, 4 * SUB, SUB):
                for plane in range(planes):
                    c_state[plane, j, pl.ds(row, SUB), :] = zero
                for part in range(2):
                    c_change[j, part, pl.ds(row, SUB), :] = zero

        @pl.when(has_up)
        def _():
            start_down.wait_recv()

        @pl.when(has_down)
        def _():
            start_up.wait_recv()

    @pl.when(has_before & even)
    def _():
        @pl.when(has_up)
        def _():
            for plane, j in each_slab():
                c_state[plane, j, above(deep), :] = start_above[plane, j]

        @pl.when(has_down)
        def _():
            for plane, j in each_slab():
                c_state[plane, j, below(deep), :] = start_below[plane, j]

        for plane, j in each_slab():
            c_state[plane, j, own, :] = start[plane, j]
        coarse_wave(c_core)
        for plane, j in each_slab():
            gain[plane, j] = c_state[plane, j, own, :]

        @pl.when(has_after)
        def _():
            for plane, j in each_slab():
                leave(plane, j, end[plane, j] - gain[plane, j])
            launch()

    @pl.when((has_before & even) | jnp.logical_not(has_after))
    def _():
        natural()

    def joined(place, extra_above=lambda: None, extra_below=lambda: None):
        @pl.when(has_up)
        def _():
            for copy in to_below:
                copy.wait_recv()
            for plane, j in each_slab():
                size = HALO[plane]
                place(
                    plane, j, above(size),
                    above_in[plane, j, pl.ds(0, size), :]
                    - start_above[plane, j, pl.ds(deep - size, size), :],
                )
            extra_above()

        @pl.when(has_down)
        def _():
            for copy in to_above:
                copy.wait_recv()
            for plane, j in each_slab():
                size = HALO[plane]
                place(
                    plane, j, below(size),
                    below_in[plane, j, pl.ds(0, size), :]
                    - start_below[plane, j, pl.ds(0, size), :],
                )
            extra_below()

        to_own.wait_recv()
        for plane, j in each_slab():
            place(plane, j, own, arrived[plane, j] - start[plane, j])

    @pl.when(cut == 1)
    def _():
        def place(plane, j, rows, value):
            c_state[plane, j, rows, :] = value

        def widen(rows, halo, skip):
            for plane, j in each_slab():
                count = HALO[plane]
                at = rows(count)
                c_state[plane, j, at, :] = (
                    c_state[plane, j, at, :] + halo[plane, j, pl.ds(skip(count), count), :]
                )

        for copy in first_halos:
            copy.wait_recv()
        joined(place, lambda: (
            widen(above, halo_above, lambda count: deep - count),
        ), lambda: (
            widen(below, halo_below, lambda count: 0),
        ))

    @pl.when(has_far_before)
    def _():
        def hold(plane, j, rows, value):
            offset[plane, j, rows, :] = value

        def add(plane, j, rows):
            c_state[plane, j, rows, :] = c_state[plane, j, rows, :] + offset[plane, j, rows, :]

        joined(hold)
        far_own.wait_recv()

        @pl.when(pair_up)
        def _():
            near_up.start()

        @pl.when(pair_down)
        def _():
            for plane, j in each_slab():
                near_low[plane, j] = pltpu.roll(far_in[plane, j], FAR, 0)
            near_down.start()

        for plane, j in each_slab():
            c_state[plane, j, own, :] = far_in[plane, j]

        @pl.when(cross_up)
        def _():
            far_down.wait_recv()

        @pl.when(cross_down)
        def _():
            far_up.wait_recv()

        @pl.when(pair_up)
        def _():
            near_down.wait_recv()

        @pl.when(pair_down)
        def _():
            near_up.wait_recv()

        @pl.when(has_up)
        def _():
            for plane, j in each_slab():
                c_state[plane, j, above(FAR), :] = far_above[plane, j]

        @pl.when(has_down)
        def _():
            for plane, j in each_slab():
                c_state[plane, j, below(FAR), :] = far_below[plane, j]

        coarse_wave((SUB // 2, 3 * SUB))

        @pl.when(has_up)
        def _():
            for plane, j in each_slab():
                add(plane, j, above(HALO[plane]))

        @pl.when(has_down)
        def _():
            for plane, j in each_slab():
                add(plane, j, below(HALO[plane]))

        for plane, j in each_slab():
            add(plane, j, own)

    @pl.when(odd)
    def _():
        coarse_wave(c_core)

        @pl.when(has_after)
        def _():
            for plane, j in each_slab():
                far_leaving[plane, j] = c_state[plane, j, own, :] + end[plane, j]
            pl.semaphore_wait(far_ready, count(far_after))

            @pl.when(has_far_after)
            def _():
                far_own.start()

            for plane, j in each_slab():
                value = far_leaving[plane, j]
                far_low[plane, j] = pltpu.roll(value, FAR, 0)
                low[plane, j] = pltpu.roll(value, deep, 0)
                gain[plane, j] = c_state[plane, j, own, :]
                c_state[plane, j, own, :] = value
            far_launch()

            for there, copy in (
                (cross_up, side_up), (cross_down, side_down),
                (pair_up, side_up), (pair_down, side_down),
            ):
                pl.when(there)(copy.start)

            @pl.when(has_up)
            def _():
                side_down.wait_recv()
                for plane, j in each_slab():
                    c_state[plane, j, above(deep), :] = side_above[plane, j]

            @pl.when(has_down)
            def _():
                side_up.wait_recv()
                for plane, j in each_slab():
                    c_state[plane, j, below(deep), :] = side_below[plane, j]

            coarse_wave(c_core)
            for plane, j in each_slab():
                leaving[plane, j] = c_state[plane, j, own, :]
            launch()

    @pl.when(has_after & ((cut == 0) | odd))
    def _():
        natural()

    @pl.when(has_before & even)
    def _():
        to_own.wait_recv()
        for plane, j in each_slab():
            gain[plane, j] = arrived[plane, j] - gain[plane, j]

    def deliver(load):
        for plane in range(planes):
            parts = relaid([load(plane, j // 2) for j in range(tiles)])
            for t in range(tiles):
                for r in range(2):
                    spread[plane, t, pl.ds(r, coarse_count, stride=2), :] = parts[t]
            for t in range(tiles):
                at = (plane, slice(None), pl.ds(t * LANES, LANES))
                out_ref[at] = out_ref[at] + spread[plane, t]

    straight = odd & jnp.logical_not(has_after)

    @pl.when(straight)
    def _():
        deliver(lambda plane, j: c_state[plane, j, own, :])

    @pl.when(has_before & jnp.logical_not(straight))
    def _():
        deliver(lambda plane, j: gain[plane, j])

    pl.when(has_before)(landed)
    for there, copies in (
        (has_up, rest_up), (has_down, rest_down),
        (has_after & has_up, [spill_up]), (has_after & has_down, [spill_down]),
        (has_before & has_up, [start_up]), (has_before & has_down, [start_down]),
    ):
        @pl.when(there)
        def _():
            for copy in copies:
                copy.wait_send()


def per_device(tile_count, slices, start_states):
    fields = start_states[0]
    planes, row_count, columns = fields.shape
    tiles = columns // LANES
    half = tiles // 2
    fine = line_tables(tiles, tiles, 1.0, columns, FINE_SPACING, FINE_STEP)
    coarse = line_tables(half, tiles, 2.0, columns, COARSE_SPACING, COARSE_STEP)
    fine_count = row_count + 4 * SUB
    coarse_count = row_count // 2
    c_count = coarse_count + 3 * SUB
    f32 = jnp.float32

    def vmem(*shape):
        return pltpu.VMEM(shape, f32)

    slab = vmem(planes, half, coarse_count, LANES)
    out = pl.pallas_call(
        functools.partial(kernel, tile_count, slices),
        out_shape=jax.ShapeDtypeStruct(fields.shape, f32),
        in_specs=[pl.BlockSpec(memory_space=pltpu.HBM)] * 5,
        out_specs=pl.BlockSpec(memory_space=pltpu.VMEM),
        scratch_shapes=[vmem(*fields.shape)]
        + [pltpu.VMEM(a.shape, a.dtype) for a in fine + coarse]
        + [vmem(tiles, LANES)] * 4
        + [
            vmem(planes, tiles, fine_count, LANES),
            vmem(tiles, 2 * (row_count + 2 * SUB), LANES),
            vmem(tiles, 2, fine_count, LANES),
        ]
        + [vmem(planes, tiles, SUB, LANES)] * 2
        + [slab] * 3
        + [
            vmem(planes, half, 2 * SUB, LANES),
            vmem(planes, half, c_count, LANES),
            vmem(half, 4 * SUB, LANES),
            vmem(half, 2, c_count, LANES),
            vmem(fine_count, LANES),
            vmem(tiles, fine_count, LANES),
            vmem(tiles, fine_count, LANES),
            vmem(c_count, LANES),
            vmem(half, c_count, LANES),
            vmem(half, c_count, LANES),
            vmem(planes, half, c_count, LANES),
            vmem(planes, tiles, row_count, LANES),
        ]
        + [slab] * 2
        + [vmem(planes, half, HALO[-1], LANES)] * 2
        + [slab] * 11
        + [vmem(planes, half, FAR, LANES)] * 2
        + [vmem(planes, half, HALO[-1], LANES)] * 6
        + [
            pltpu.SemaphoreType.DMA((len(fine + coarse) + planes,)),
            pltpu.SemaphoreType.DMA((22,)),
            pltpu.SemaphoreType.DMA((22,)),
            pltpu.SemaphoreType.REGULAR,
            pltpu.SemaphoreType.REGULAR,
        ],
        compiler_params=pltpu.CompilerParams(
            collective_id=0, has_side_effects=True, vmem_limit_bytes=24 * 1024 * 1024
        ),
    )(*[pltpu.with_memory_space_constraint(jnp.asarray(a), pltpu.HBM) for a in (fields,) + fine + coarse])
    return out[None]


def solution(mesh):
    spec = P("cuts", None, "tile", None)
    body = functools.partial(per_device, mesh.shape["tile"], mesh.shape["cuts"])
    return jax.shard_map(body, mesh=mesh, in_specs=(spec,), out_specs=spec, check_vma=False)
```
